32 devices in a mesh: seq: 4 (over y, core), ctx: 8 (over z, x).
Axes of the slice: x: 2, y: 2, z: 4, core: 2. Of those that a mesh axis runs over, the one named last changes fastest.
Arguments:
- layer_input: bfloat16 [4, 1024, 1024], P('seq', 'ctx')
- document_ids: int32 [4, 1024], P('seq', 'ctx'), may hold values from 0 to 3, never falling along the last dimension, each value on 1 to 512 neighbouring positions
- expert_routes: int32 [4, 1024, 8], P('seq', 'ctx'), may hold values from 0 to 15, all different within a row; in each aligned block of 128 rows (0 to 127, 128 to 255, ..., all dimensions but the last counted through in order) at most 96 rows name the same one
- rope_factor: float32 [1], replicated, may hold values from 1 to 4
- attention_gain: float32 [1024], P(('seq', 'ctx')), may hold values from 0.25 to 1.75
- feedforward_gain: float32 [1024], P(('seq', 'ctx')), may hold values from 0.25 to 1.75
- query_weight: float32 [1024, 1024], P(('seq', 'ctx')), may hold values from -0.1875 to 0.1875
- key_weight: float32 [1024, 512], P(('seq', 'ctx')), may hold values from -0.1875 to 0.1875
- value_weight: float32 [1024, 512], P(('seq', 'ctx')), may hold values from -0.1875 to 0.1875
- output_weight: float32 [1024, 1024], P(('seq', 'ctx')), may hold values from -1.5 to 1.5
- router_weight: float32 [1024, 16], P(('seq', 'ctx')), may hold values from -0.375 to 0.375
- gate_up: float32 [1024, 16, 1024], P(('seq', 'ctx')), may hold values from -0.1875 to 0.1875
- down_weight: float32 [512, 16, 1024], P(('seq', 'ctx')), may hold values from -0.25 to 0.25
- cotangent: bfloat16 [4, 1024, 1024], P('seq', 'ctx'), may hold values from -6 to 6
Outputs:
- layer_output: bfloat16 [4, 1024, 1024], P('seq', 'ctx')
- input_gradient: bfloat16 [4, 1024, 1024], P('seq', 'ctx')
- attention_gain_gradient: float32 [1024], P(('seq', 'ctx'))
- feedforward_gain_gradient: float32 [1024], P(('seq', 'ctx'))
- query_gradient: float32 [1024, 1024], P(('seq', 'ctx'))
- key_gradient: float32 [1024, 512], P(('seq', 'ctx'))
- value_gradient: float32 [1024, 512], P(('seq', 'ctx'))
- output_gradient: float32 [1024, 1024], P(('seq', 'ctx'))
- router_gradient: float32 [1024, 16], P(('seq', 'ctx'))
- gate_up_gradient: float32 [1024, 16, 1024], P(('seq', 'ctx'))
- down_gradient: float32 [512, 16, 1024], P(('seq', 'ctx'))
The draws below stay inside these ranges and needn't reach their ends.
Inputs may be any that keep to these rules, and one draw needn't show every extreme that they name: `document_ids`: document ids never fall along a sequence; each of the 4 documents holds 1 to 512 tokens, and one holds exactly 512. `expert_routes`: each token names 8 different experts. Among the 128 tokens of one device (aligned blocks of a sequence) no expert is named by more than 96 tokens, and in some block some expert is named by exactly 96.
All inputs are finite; a program needn't handle non-finite values.
Results may differ from the reference program's by a relative error of at most 0.025.
Values may be sent and summed in bfloat16 or wider, within the bound.
A program may use at most 320 MiB of HBM per device.

```python
import math
import jax
import jax.numpy as jnp
import numpy as np
from jax import lax

D = 1024
HEADS = 16
KV_HEADS = 8
HEAD_DIM = 64
FF = 512
EXPERTS = 16
TOPK = 8
DOCS = 4
TOK_DEV = 128
CAP = 96
SEQS = 4
LENGTH = 1024


def draw_layer_input(key, part):
    normal_key, row_key, column_key = jax.random.split(jax.random.fold_in(key, 11), 3)
    standard = jax.random.normal(normal_key, (SEQS, LENGTH, D), jnp.float32)
    row_scales = 10.0 ** (jax.random.uniform(row_key, (SEQS, LENGTH, 1), jnp.float32) - 0.5)
    column_scales = 10.0 ** (jax.random.uniform(column_key, (1, 1, D), jnp.float32) - 0.5)
    return (standard * row_scales * column_scales).astype(jnp.bfloat16)


def steps_of(key, extent, pieces, least, top_value):
    def one(position, parts):
        steps = jax.random.uniform(jax.random.fold_in(jax.random.fold_in(key, 6), position), (parts,), jnp.float32, least / len(pieces), top_value / len(pieces))
        return jnp.repeat(jnp.exp(steps), extent[position] // parts).reshape((-1,) + (1,) * (len(extent) - position - 1))

    level = one(*pieces[0])
    for cut in pieces[1:]:
        level = level * one(*cut)
    return level


def profile(amount, total, reach, slope):
    weights = [(1 << 20) // math.isqrt(rank ** slope) + 1 for rank in range(2, amount + 1)]
    rest, given = total - reach - (amount - 1), [1] * (amount - 1)
    while rest > 0:
        movable = [i for i in range(amount - 1) if given[i] < reach]
        pool, left = sum([weights[i] for i in movable]), rest
        for i in movable:
            extra = min(reach - given[i], max(1, left * weights[i] // pool), rest)
            given[i] = given[i] + extra
            rest = rest - extra
    return np.array([reach] + given)


def ragged(own_key, number_of, total, limit, lean):
    if number_of == 2:
        one = jax.random.randint(own_key, (), max(1, total - limit), min(limit, total - 1) + 1)
        return jnp.stack([one, total - one])
    lengths = jnp.asarray(profile(number_of, total, limit, lean), jnp.int32)
    twos = (number_of - 1) // 2
    source_of, taker = lengths[1:1 + 2 * twos:2], lengths[2:2 + 2 * twos:2]
    margin = jnp.minimum(source_of - 1, limit - taker)
    shifted = jax.random.randint(jax.random.fold_in(own_key, 1), (twos,), 0, 1 << 20) % (margin + 1)
    lengths = lengths.at[1:1 + 2 * twos:2].set(source_of - shifted).at[2:2 + 2 * twos:2].set(taker + shifted)
    return lengths[jax.random.permutation(jax.random.fold_in(own_key, 2), number_of)]


def deal_out(own_key, own, number, rows, number_of, top, bound, skew):
    order = jax.random.permutation(own_key, number_of)
    packed, ordinary = portions_of(number_of, rows * top, bound, skew, True), portions_of(number_of, rows * top, bound, skew, False)
    places = jnp.arange(number_of)

    def named(lengths, offset_by):
        used = int((lengths > 0).sum())
        fixed = max(1, used // 4)
        moved = fixed + (places - fixed + offset_by * (used - fixed)) % max(1, number_of - fixed)
        return jnp.zeros((number_of,), jnp.int32).at[order[jnp.where(places < fixed, places, moved)]].set(jnp.asarray(lengths, jnp.int32))

    lengths = jnp.where(number % 4 == 0, named(packed, number // 4), named(ordinary, number - number // 4 - 1))
    mixed = jax.random.permutation(jax.random.fold_in(own, 3), number_of)
    giver, taker = mixed[0:number_of // 2 * 2:2], mixed[1:number_of // 2 * 2:2]
    room = jnp.minimum(lengths[giver] - 1, bound - lengths[taker]) // 2
    room = jnp.where((giver == order[0]) | (taker == order[0]) | (lengths[taker] == 0), 0, jnp.maximum(room, 0))
    moved = jax.random.randint(jax.random.fold_in(own, 4), (number_of // 2,), 0, 1 << 20) % (room + 1)
    lengths = lengths.at[giver].add(-moved).at[taker].add(moved)
    members = jnp.searchsorted(jnp.cumsum(lengths), jnp.arange(rows * top), side="right").astype(jnp.int32)
    table = members.reshape(top, rows).T
    table = table[jax.random.permutation(jax.random.fold_in(own, 1), rows)]
    offset_by = jax.random.randint(jax.random.fold_in(own, 2), (rows, 1), 0, top)
    return jnp.take_along_axis(table, (jnp.arange(top)[None, :] + offset_by) % top, axis=1)


def portions_of(number_of, total, limit, lean, full):
    weights = [(1 << 20) // math.isqrt(grade ** lean) + 1 for grade in range(1, number_of + 1)]
    largest = limit if full else min(limit, max(-(-total // number_of), total * weights[0] // sum(weights)))
    least = 1 if total - largest >= number_of - 1 else 0
    counts, rest = [largest] + [least] * (number_of - 1), total - largest - least * (number_of - 1)
    while rest > 0:
        candidates = [i for i in range(1, number_of) if counts[i] < largest] or [i for i in range(1, number_of) if counts[i] < limit]
        whole, remaining = sum([weights[i] for i in candidates]), rest
        for i in candidates:
            extra = min(limit - counts[i], max(1, remaining * weights[i] // whole), rest)
            counts[i] = counts[i] + extra
            rest = rest - extra
    return np.array(counts)


def bell_draw(rng, extent, width, bound, cuts=(), kind=jnp.bfloat16):
    loudness = steps_of(rng, extent, cuts, -0.22, 0.18) if cuts else 1.0
    values = jax.random.normal(rng, extent, jnp.float32) * width * loudness
    return jnp.minimum(jnp.maximum(values, -bound), bound).astype(kind)


def setup_inputs(seed: int = 0) -> dict:
    key_list = jax.random.split(jax.random.key(seed), 15)
    layer_input = draw_layer_input(jax.random.fold_in(key_list[14], 71), 0)
    document_ids = jax.vmap(lambda own: jnp.searchsorted(jnp.cumsum(ragged(own, DOCS, LENGTH, LENGTH // 2, 0)), jnp.arange(LENGTH), side="right"))(jax.random.split(key_list[1], SEQS)).reshape((SEQS, LENGTH)).astype(jnp.int32)
    expert_routes_keys = jax.random.split(jax.random.fold_in(key_list[2], 1), SEQS * LENGTH // TOK_DEV)
    expert_routes_turns = jax.random.permutation(jax.random.fold_in(key_list[2], 3), SEQS * LENGTH // TOK_DEV)
    expert_routes = jax.vmap(lambda own, number: deal_out(jax.random.fold_in(key_list[2], 2), own, number, TOK_DEV, EXPERTS, TOPK, CAP, 1))(expert_routes_keys, expert_routes_turns).reshape((SEQS, LENGTH, TOPK))
    rope_factor = jnp.clip(jnp.exp(jax.random.uniform(key_list[3], (1,), jnp.float32, math.log(1.0), math.log(4.0))), 1.0, 4.0)
    attention_gain = jnp.clip(1.0 + 0.15 * jax.random.normal(key_list[4], (D,), jnp.float32), 0.25, 1.75)
    feedforward_gain = jnp.clip(1.0 + 0.15 * jax.random.normal(key_list[5], (D,), jnp.float32), 0.25, 1.75)
    query_weight = bell_draw(key_list[6], (D, HEADS * HEAD_DIM), D ** -0.5, 0.1875, ((0, 32),), jnp.float32)
    key_weight = bell_draw(key_list[7], (D, KV_HEADS * HEAD_DIM), D ** -0.5, 0.1875, ((0, 32),), jnp.float32)
    value_weight = bell_draw(key_list[8], (D, KV_HEADS * HEAD_DIM), D ** -0.5, 0.1875, ((0, 32),), jnp.float32)
    output_weight = bell_draw(key_list[9], (HEADS * HEAD_DIM, D), (HEADS * HEAD_DIM // 64) ** -0.5, 1.5, ((0, 32),), jnp.float32)
    router_weight = bell_draw(key_list[10], (D, EXPERTS), (D // 4) ** -0.5, 0.375, ((0, 32),), jnp.float32)
    gate_up = bell_draw(key_list[11], (D, EXPERTS, 2 * FF), D ** -0.5, 0.1875, ((0, 32),), jnp.float32)
    down_weight = bell_draw(key_list[12], (FF, EXPERTS, D), FF ** -0.5, 0.25, ((0, 32),), jnp.float32)
    cotangent = bell_draw(key_list[13], (SEQS, LENGTH, D), 1.0, 6.0, ((0, 4), (1, 8)))
    return dict(layer_input=layer_input, document_ids=document_ids, expert_routes=expert_routes, rope_factor=rope_factor, attention_gain=attention_gain, feedforward_gain=feedforward_gain, query_weight=query_weight, key_weight=key_weight, value_weight=value_weight, output_weight=output_weight, router_weight=router_weight, gate_up=gate_up, down_weight=down_weight, cotangent=cotangent)


@jax.custom_vjp
def low(v):
    return lax.optimization_barrier(v.astype(jnp.bfloat16)).astype(jnp.float32)

@jax.custom_vjp
def low_back(v):
    return v

def low_keep(v):
    return (low(v), None)

def low_pass(kept, grad):
    return (grad,)

def back_keep(v):
    return (v, None)

def back_low(kept, grad):
    return (low(grad),)
low.defvjp(low_keep, low_pass)
low_back.defvjp(back_keep, back_low)
NORM_EPS = 1e-06
ROPE_BASE = 10000.0
NEG_BIG = -1e+30
HIGH = lax.Precision.HIGHEST

def matmul(left, right):
    return jnp.dot(left, right, precision=HIGH, preferred_element_type=jnp.float32)

def rms_scale(values):
    return lax.rsqrt(lax.optimization_barrier(jnp.mean(values * values, axis=-1, keepdims=True)) + NORM_EPS)

def softmax_last(scores):
    row_peak = lax.optimization_barrier(jnp.max(scores, axis=-1, keepdims=True))
    expo = jnp.exp(scores - row_peak)
    return expo / lax.optimization_barrier(jnp.sum(expo, axis=-1, keepdims=True))

def rotate_pairs(values, cosine, sine):
    half_dim = values.shape[-1] // 2
    first_half = values[..., :half_dim]
    second_half = values[..., half_dim:]
    return jnp.concatenate([first_half * cosine - second_half * sine, second_half * cosine + first_half * sine], axis=-1)

def rope_tables(length, factor):
    places = jnp.arange(length).astype(jnp.float32)
    freqs = 1.0 / ROPE_BASE ** (jnp.arange(0, HEAD_DIM, 2).astype(jnp.float32) / HEAD_DIM)
    angles = (places / factor)[:, None] * freqs[None, :]
    return (jnp.cos(angles)[:, None, :], jnp.sin(angles)[:, None, :])

def layer(inputs, params, doc_row, route_rows, factor):
    gain_attention, gain_forward, query_matrix, key_matrix, value_matrix, out_matrix, router_matrix, gate_up_matrix, down_matrix = params
    length = inputs.shape[0]
    group_size = HEADS // KV_HEADS
    score_scale = HEAD_DIM ** (-0.5)
    normed_one = inputs * rms_scale(inputs)
    attend_input = low(normed_one * low(gain_attention))
    query_pre = low_back(matmul(attend_input, low(query_matrix))).reshape(length, HEADS, HEAD_DIM)
    key_pre = low_back(matmul(attend_input, low(key_matrix))).reshape(length, KV_HEADS, HEAD_DIM)
    values = low(low_back(matmul(attend_input, low(value_matrix)))).reshape(length, KV_HEADS, HEAD_DIM)
    cosine, sine = rope_tables(length, factor)
    queries = low(rotate_pairs(query_pre, cosine, sine)).reshape(length, KV_HEADS, group_size, HEAD_DIM)
    keys = low(rotate_pairs(key_pre, cosine, sine))
    block_rows = 512 if length % 512 == 0 else length
    key_places = jnp.arange(length).astype(jnp.int32)

    def attend(first_row):
        query_block = lax.dynamic_slice_in_dim(queries, first_row, block_rows, 0)
        doc_block = lax.dynamic_slice_in_dim(doc_row, first_row, block_rows, 0)
        raw_scores = jnp.einsum('qkgd,nkd->kgqn', query_block, keys, precision=HIGH) * score_scale
        scores = low_back(raw_scores)
        query_places = first_row + jnp.arange(block_rows).astype(jnp.int32)
        allowed = (key_places[None, :] <= query_places[:, None]) & (doc_row[None, :] == doc_block[:, None])
        weights = low(softmax_last(jnp.where(allowed, scores, NEG_BIG)))
        return jnp.einsum('kgqn,nkd->qkgd', weights, values, precision=HIGH)
    block_starts = (jnp.arange(length // block_rows) * block_rows).astype(jnp.int32)
    mixed = lax.map(jax.checkpoint(attend), block_starts).reshape(length, HEADS * HEAD_DIM)
    attend_out = low_back(matmul(low(low_back(mixed)), low(out_matrix)))
    middle = inputs + attend_out
    normed_two = middle * rms_scale(middle)
    expert_input = low(normed_two * low(gain_forward))
    logits = low_back(matmul(expert_input, low(router_matrix)))
    chosen = (route_rows[:, :, None] == jnp.arange(EXPERTS).astype(jnp.int32)[None, None, :]).astype(jnp.float32)
    gate_probs = softmax_last(lax.optimization_barrier(jnp.sum(chosen * logits[:, None, :], axis=-1)))
    combine = lax.optimization_barrier(jnp.sum(gate_probs[:, :, None] * chosen, axis=1))

    def expert_step(summed, stacked):
        pair_matrix, down_one, combine_column = stacked
        gate_and_up = low_back(matmul(expert_input, pair_matrix))
        gate_part = gate_and_up[:, :FF]
        up_part = gate_and_up[:, FF:]
        hidden = low(gate_part / (1.0 + jnp.exp(-gate_part)) * up_part)
        produced = low_back(matmul(hidden, down_one))
        return (summed + combine_column[:, None] * produced, None)
    stacks = (jnp.moveaxis(low(gate_up_matrix), 1, 0), jnp.moveaxis(low(down_matrix), 1, 0), combine.T)
    expert_mix, unused = lax.scan(jax.checkpoint(expert_step), jnp.zeros_like(inputs), stacks)
    return middle + expert_mix

def reference(layer_input, document_ids, expert_routes, rope_factor, attention_gain, feedforward_gain, query_weight, key_weight, value_weight, output_weight, router_weight, gate_up, down_weight, cotangent):
    params = (attention_gain, feedforward_gain, query_weight, key_weight, value_weight, output_weight, router_weight, gate_up, down_weight)
    factor = rope_factor[0]

    def one_sequence(summed, item):
        inputs, doc_row, route_rows, upstream = item

        def forward(input_values, param_values):
            return layer(input_values, param_values, doc_row, route_rows, factor)
        result, pullback = jax.vjp(forward, inputs.astype(jnp.float32), params)
        input_grad, param_grads = pullback(upstream.astype(jnp.float32))
        summed = jax.tree.map(lambda left, right: left + right, summed, param_grads)
        return (summed, (result.astype(jnp.bfloat16), input_grad.astype(jnp.bfloat16)))
    start_sums = jax.tree.map(jnp.zeros_like, params)
    grads, outputs = lax.scan(one_sequence, start_sums, (layer_input, document_ids, expert_routes, cotangent))
    return (outputs[0], outputs[1], grads[0], grads[1], grads[2], grads[3], grads[4], grads[5], grads[6], grads[7], grads[8])
```

```python
import functools
import math

import jax
import jax.numpy as jnp
from jax import lax
from jax.experimental import pallas as pl
from jax.experimental.pallas import tpu as pltpu
from jax.sharding import PartitionSpec as P

HEADS = 16
KV_HEADS = 8
HEAD_DIM = 64
GROUP = HEADS // KV_HEADS
HEAD_COLS = (GROUP + 2) * HEAD_DIM

NORM_EPS = 1e-06
ROPE_BASE = 10000.0
NEG_BIG = -1e30
LOW = jnp.bfloat16
WIDE = jnp.float32
MESH = pl.DeviceIdType.MESH


def ring_place(index, size):
    half = index // 2
    return half + (index % 2) * (size - 1 - 2 * half)


def ring_member(place, size):
    place = (place + 2 * size) % size
    far = place // (size // 2)
    return 2 * place + far * (2 * size - 1 - 4 * place)


def core_mate(index):
    return index + 1 - 2 * (index % 2)


def row_mate(index):
    return (index + 2) % 4


def push(src, dst, send, recv, **where):
    return pltpu.make_async_remote_copy(
        src_ref=src, dst_ref=dst, send_sem=send, recv_sem=recv, device_id=where, device_id_type=MESH
    )


def greet(peers):
    barrier = pltpu.get_barrier_semaphore()
    for where in peers:
        pl.semaphore_signal(barrier, inc=1, device_id=where, device_id_type=MESH)
    pl.semaphore_wait(barrier, len(peers))


def ring_peers(size):
    place = ring_place(lax.axis_index("ctx"), size)
    return ring_member(place + 1, size), ring_member(place - 1, size)


class RingGather:
    def __init__(self, size, source, target, send, recv):
        self.size, self.source, self.target, self.send, self.recv = size, source, target, send, recv
        self.me = lax.axis_index("ctx")
        self.place = ring_place(self.me, size)
        self.right, self.left = ring_peers(size)
        self.steps = size // 2

    def _copy(self, way, step, owner_place, use_source):
        owner = ring_member(owner_place, self.size)
        rows = self.source.shape[0]
        part = pl.ds(0, rows)
        if step == self.steps - 1:
            part = pl.ds(0, rows // 2) if way == 0 else pl.ds(rows // 2, rows // 2)
        dst = self.target.at[owner, part]
        src = self.source.at[part] if use_source else dst
        where = self.right if way == 0 else self.left
        return push(src, dst, self.send.at[way, step], self.recv.at[way, step], ctx=where)

    def outgoing(self, way, step):
        place = self.place - step if way == 0 else self.place + step
        return self._copy(way, step, place, step == 0)

    def incoming(self, way, step):
        place = self.place - 1 - step if way == 0 else self.place + 1 + step
        return self._copy(way, step, place, False)

    def start(self, step):
        for way in range(2):
            if step:
                self.incoming(way, step - 1).wait_recv()
            self.outgoing(way, step).start()

    def finish(self):
        for way in range(2):
            self.incoming(way, self.steps - 1).wait_recv()
            for step in range(self.steps):
                self.outgoing(way, step).wait_send()


def gather_kernel(size, count, *refs):
    sources, targets = refs[:count], refs[count : 2 * count]
    send, recv, own = refs[2 * count :]
    me = lax.axis_index("ctx")
    greet([{"ctx": where} for where in ring_peers(size)])
    rings, copies = [], []
    for i in range(count):
        copies.append(pltpu.make_async_copy(sources[i], targets[i].at[me], own.at[i]))
        copies[-1].start()
        rings.append(RingGather(size, sources[i], targets[i], send.at[i], recv.at[i]))
    for step in range(size // 2):
        for ring in rings:
            ring.start(step)
    for ring in rings:
        ring.finish()
    for copy in copies:
        copy.wait()


def gather_ctx(arrays, size, collective):
    count = len(arrays)
    return pl.pallas_call(
        functools.partial(gather_kernel, size, count),
        out_shape=[jax.ShapeDtypeStruct((size,) + a.shape, a.dtype) for a in arrays],
        in_specs=[pl.BlockSpec(memory_space=pl.ANY)] * count,
        out_specs=[pl.BlockSpec(memory_space=pl.ANY)] * count,
        scratch_shapes=[
            pltpu.SemaphoreType.DMA((count, 2, size // 2)),
            pltpu.SemaphoreType.DMA((count, 2, size // 2)),
            pltpu.SemaphoreType.DMA((count,)),
        ],
        compiler_params=pltpu.CompilerParams(collective_id=collective, has_side_effects=True),
        name="gather_ctx_%d" % collective,
    )(*arrays)


class RingReduce:
    def __init__(self, size, own, held, out_buf, send, recv):
        self.size, self.own, self.held, self.out_buf = size, own, held, out_buf
        self.send, self.recv = send, recv
        self.me = lax.axis_index("ctx")
        self.place = ring_place(self.me, size)
        self.right, self.left = ring_peers(size)
        self.steps = size // 2
        self.rows = own.shape[1]

    def _part(self, way, step):
        half = self.rows // 2
        if step:
            return pl.ds(0, self.rows)
        return pl.ds(0, half) if way == 0 else pl.ds(half, half)

    def _owner(self, way, step):
        ahead = self.steps - step
        return ring_member(self.place + ahead if way == 0 else self.place - ahead, self.size)

    def _copy(self, way, step):
        part = self._part(way, step)
        src = self.out_buf.at[way, step - 1] if step else self.own.at[self._owner(way, 0), part]
        where = self.right if way == 0 else self.left
        return push(src, self.held.at[way, step, part], self.send.at[way, step], self.recv.at[way, step], ctx=where)

    def start(self, step):
        for way in range(2):
            if step:
                self._copy(way, step - 1).wait_recv()
                owner = self._owner(way, step)
                if step == 1:
                    half = self.rows // 2
                    near = pl.ds(0, half) if way == 0 else pl.ds(half, half)
                    far = pl.ds(half, half) if way == 0 else pl.ds(0, half)
                    total = self.own[owner, near].astype(WIDE) + self.held[way, 0, near].astype(WIDE)
                    self.out_buf[way, 0, near] = total.astype(LOW)
                    self.out_buf[way, 0, far] = self.own[owner, far]
                else:
                    total = self.own[owner].astype(WIDE) + self.held[way, step - 1].astype(WIDE)
                    self.out_buf[way, step - 1] = total.astype(LOW)
            self._copy(way, step).start()

    def finish(self, target):
        last = self.steps - 1
        for way in range(2):
            self._copy(way, last).wait_recv()
        target[...] = (
            self.own[self.me].astype(WIDE) + self.held[0, last].astype(WIDE) + self.held[1, last].astype(WIDE)
        )
        for way in range(2):
            for step in range(self.steps):
                self._copy(way, step).wait_send()


def reduce_kernel(size, count, extra, *refs):
    n_in = count + extra
    own, target = refs[:count], refs[n_in : n_in + count]
    scratch = refs[2 * n_in :]
    held, out_buf, send, recv = scratch[:count], scratch[count : 2 * count], scratch[2 * count], scratch[2 * count + 1]
    me = lax.axis_index("ctx")
    right, left = ring_peers(size)
    if extra:
        greet([{"ctx": (me + k) % size} for k in range(1, size)])
    else:
        greet([{"ctx": right}, {"ctx": left}])
    direct = []
    if extra:
        source, spread = refs[count], refs[n_in + count]
        send_small, recv_small = scratch[2 * count + 2 :]
        spread[me] = source[me]
        for k in range(1, size):
            there = (me + k) % size
            direct.append(push(source.at[there], spread.at[me], send_small.at[k], recv_small.at[k], ctx=there))
            direct[-1].start()
    rings = [RingReduce(size, own[i], held[i], out_buf[i], send.at[i], recv.at[i]) for i in range(count)]
    for step in range(size // 2):
        for ring in rings:
            ring.start(step)
    for ring, where in zip(rings, target):
        ring.finish(where)
    if extra:
        for k in range(1, size):
            here = (me + size - k) % size
            push(source.at[here], spread.at[here], send_small.at[k], recv_small.at[k], ctx=here).wait_recv()
        for copy in direct:
            copy.wait_send()


def reduce_ctx(arrays, size, collective, small=None):
    count = len(arrays)
    extra = 0 if small is None else 1
    operands = list(arrays) + ([small] if extra else [])
    shapes = [jax.ShapeDtypeStruct(a.shape[1:], WIDE) for a in arrays]
    scratch = [pltpu.VMEM((2, size // 2) + a.shape[1:], LOW) for a in arrays]
    scratch += [pltpu.VMEM((2, size // 2 - 1) + a.shape[1:], LOW) for a in arrays]
    scratch += [pltpu.SemaphoreType.DMA((count, 2, size // 2))] * 2
    if extra:
        shapes.append(jax.ShapeDtypeStruct(small.shape, small.dtype))
        scratch += [pltpu.SemaphoreType.DMA((size,))] * 2
    return pl.pallas_call(
        functools.partial(reduce_kernel, size, count, extra),
        out_shape=shapes,
        in_specs=[pl.BlockSpec(memory_space=pltpu.VMEM)] * len(operands),
        out_specs=[pl.BlockSpec(memory_space=pltpu.VMEM)] * len(operands),
        scratch_shapes=scratch,
        compiler_params=pltpu.CompilerParams(
            collective_id=collective, has_side_effects=True, vmem_limit_bytes=60 << 20
        ),
        name="reduce_ctx_%d" % collective,
    )(*operands)


def exchange_kernel(size, split, source, target, send, recv, own):
    me = lax.axis_index("ctx")
    lane, row = me % split, me // split
    number = size // split
    greet([{"ctx": ((row + k) % number) * split + lane} for k in range(1, number)])
    mine = pltpu.make_async_copy(source.at[row], target.at[row], own)
    mine.start()
    copies = []
    for k in range(1, number):
        there = (row + k) % number
        copies.append(push(source.at[there], target.at[row], send.at[k], recv.at[k], ctx=there * split + lane))
        copies[-1].start()
    for k in range(1, number):
        here = (row + number - k) % number
        push(source.at[here], target.at[here], send.at[k], recv.at[k], ctx=here * split + lane).wait_recv()
    for copy in copies:
        copy.wait_send()
    mine.wait()


def exchange_ctx(array, size, split, collective):
    return pl.pallas_call(
        functools.partial(exchange_kernel, size, split),
        out_shape=jax.ShapeDtypeStruct(array.shape, array.dtype),
        in_specs=[pl.BlockSpec(memory_space=pl.ANY)],
        out_specs=pl.BlockSpec(memory_space=pl.ANY),
        scratch_shapes=[
            pltpu.SemaphoreType.DMA((size // split,)),
            pltpu.SemaphoreType.DMA((size // split,)),
            pltpu.SemaphoreType.DMA,
        ],
        compiler_params=pltpu.CompilerParams(collective_id=collective, has_side_effects=True),
        name="exchange_ctx_%d" % collective,
    )(array)


def spread_kernel(size, count, *refs):
    sources, pack = refs[:count], refs[count]
    targets, whole = refs[count + 1 : 2 * count + 1], refs[2 * count + 1]
    send, recv, own, send_a, recv_a, send_b, recv_b, own_pack = refs[2 * count + 2 :]
    me, seq = lax.axis_index("ctx"), lax.axis_index("seq")
    greet(
        [{"ctx": (me + k) % size} for k in range(1, size)]
        + [{"seq": core_mate(seq)}, {"seq": row_mate(seq)}]
    )
    rings, local = [], []
    for i in range(count):
        local.append(pltpu.make_async_copy(sources[i], targets[i].at[me], own.at[i]))
        rings.append(RingGather(size, sources[i], targets[i], send.at[i], recv.at[i]))
    local.append(pltpu.make_async_copy(pack.at[me], whole.at[seq, me], own_pack))
    for copy in local:
        copy.start()

    def outward(k):
        there = (me + k) % size
        return push(pack.at[there], whole.at[seq, me], send_a.at[k], recv_a.at[k], ctx=there)

    def inward(k):
        here = (me + size - k) % size
        return push(pack.at[here], whole.at[seq, here], send_a.at[k], recv_a.at[k], ctx=here)

    def sideways(which, k):
        here = (me + size - k) % size
        slab = whole.at[row_mate(seq) if which == 2 else seq, here]
        mate = row_mate(seq) if which == 1 else core_mate(seq)
        return push(slab, slab, send_b.at[which, k], recv_b.at[which, k], seq=mate)

    def landing(which, k):
        here = (me + size - k) % size
        owner = (core_mate(seq), row_mate(seq), core_mate(row_mate(seq)))[which]
        slab = whole.at[owner, here]
        return push(slab, slab, send_b.at[which, k], recv_b.at[which, k], seq=core_mate(seq))

    for ring in rings:
        ring.start(0)
    for k in range(1, size):
        outward(k).start()
    local[-1].wait()
    sideways(1, 0).start()
    sideways(0, 0).start()
    steps = size // 2
    for k in range(1, size):
        if k < steps:
            for ring in rings:
                ring.start(k)
        inward(k).wait_recv()
        sideways(1, k).start()
        sideways(0, k).start()
        landing(1, k - 1).wait_recv()
        sideways(2, k - 1).start()
    landing(1, size - 1).wait_recv()
    sideways(2, size - 1).start()
    for ring in rings:
        ring.finish()
    for copy in local[:-1]:
        copy.wait()
    for k in range(size):
        landing(0, k).wait_recv()
        landing(2, k).wait_recv()
        for which in range(3):
            sideways(which, k).wait_send()
        if k:
            outward(k).wait_send()


def spread_all(arrays, pack, size, rows, collective):
    count = len(arrays)
    shapes = [jax.ShapeDtypeStruct((size,) + a.shape, a.dtype) for a in arrays]
    shapes.append(jax.ShapeDtypeStruct((rows,) + pack.shape, pack.dtype))
    return pl.pallas_call(
        functools.partial(spread_kernel, size, count),
        out_shape=shapes,
        in_specs=[pl.BlockSpec(memory_space=pl.ANY)] * (count + 1),
        out_specs=[pl.BlockSpec(memory_space=pl.ANY)] * (count + 1),
        scratch_shapes=[
            pltpu.SemaphoreType.DMA((count, 2, size // 2)),
            pltpu.SemaphoreType.DMA((count, 2, size // 2)),
            pltpu.SemaphoreType.DMA((count,)),
            pltpu.SemaphoreType.DMA((size,)),
            pltpu.SemaphoreType.DMA((size,)),
            pltpu.SemaphoreType.DMA((3, size)),
            pltpu.SemaphoreType.DMA((3, size)),
            pltpu.SemaphoreType.DMA,
        ],
        compiler_params=pltpu.CompilerParams(collective_id=collective, has_side_effects=True),
        name="spread_all",
    )(*arrays, pack)


def home_kernel(
    size, grads, out, near, from_core, from_row, to_row, to_home,
    load, send_a, recv_a, send_b, recv_b, send_c, recv_c,
):
    me, seq = lax.axis_index("ctx"), lax.axis_index("seq")
    greet(
        [{"ctx": (me + k) % size} for k in range(1, size)]
        + [{"seq": core_mate(seq)}, {"seq": row_mate(seq)}]
    )

    def row_of(which):
        return row_mate(seq) if which == 0 else seq

    def fetch(which, k):
        there = (me + k) % size
        return pltpu.make_async_copy(grads.at[row_of(which), there], near.at[which, k], load.at[which, k])

    def to_core(which, k):
        there = (me + k) % size
        return push(
            grads.at[core_mate(row_of(which)), there], from_core.at[which, k],
            send_a.at[which, k], recv_a.at[which, k], seq=core_mate(seq),
        )

    def across(k):
        return push(to_row.at[k], from_row.at[k], send_b.at[k], recv_b.at[k], seq=row_mate(seq))

    def homeward(k):
        there = (me + k) % size
        return push(to_home.at[k], out.at[me], send_c.at[k], recv_c.at[k], ctx=there)

    def arriving(k):
        here = (me + size - k) % size
        return push(to_home.at[k], out.at[here], send_c.at[k], recv_c.at[k], ctx=here)

    for which in range(2):
        for k in range(size):
            to_core(which, k).start()
            fetch(which, k).start()

    def first(k, _):
        fetch(0, k).wait()
        to_core(0, k).wait_recv()
        to_row[k] = (near[0, k].astype(WIDE) + from_core[0, k].astype(WIDE)).astype(LOW)
        across(k).start()
        return 0

    lax.fori_loop(0, size, first, 0)

    def total(k):
        fetch(1, k).wait()
        to_core(1, k).wait_recv()
        across(k).wait_recv()
        return (near[1, k].astype(WIDE) + from_core[1, k].astype(WIDE) + from_row[k].astype(WIDE)).astype(LOW)

    def second(k, _):
        to_home[k] = total(k)
        homeward(k).start()
        return 0

    lax.fori_loop(1, size, second, 0)
    out[me] = total(0)

    def close(k, _):
        arriving(k).wait_recv()
        homeward(k).wait_send()
        return 0

    lax.fori_loop(1, size, close, 0)

    def drain(k, _):
        to_core(0, k).wait_send()
        to_core(1, k).wait_send()
        across(k).wait_send()
        return 0

    lax.fori_loop(0, size, drain, 0)


def bring_home(grads, size, collective):
    rows, _, height, width = grads.shape
    slab = (size, height, width)
    return pl.pallas_call(
        functools.partial(home_kernel, size),
        out_shape=jax.ShapeDtypeStruct(slab, LOW),
        in_specs=[pl.BlockSpec(memory_space=pl.ANY)],
        out_specs=pl.BlockSpec(memory_space=pltpu.VMEM),
        scratch_shapes=[
            pltpu.VMEM((2,) + slab, LOW),
            pltpu.VMEM((2,) + slab, LOW),
            pltpu.VMEM(slab, LOW),
            pltpu.VMEM(slab, LOW),
            pltpu.VMEM(slab, LOW),
            pltpu.SemaphoreType.DMA((2, size)),
            pltpu.SemaphoreType.DMA((2, size)),
            pltpu.SemaphoreType.DMA((2, size)),
            pltpu.SemaphoreType.DMA((size,)),
            pltpu.SemaphoreType.DMA((size,)),
            pltpu.SemaphoreType.DMA((size,)),
            pltpu.SemaphoreType.DMA((size,)),
        ],
        compiler_params=pltpu.CompilerParams(
            collective_id=collective, has_side_effects=True, vmem_limit_bytes=60 << 20
        ),
        name="bring_home",
    )(grads)


def as_rows(array, lead, width):
    flat = array.reshape(array.shape[:lead] + (-1,))
    short = -flat.shape[-1] % width
    if short:
        flat = jnp.pad(flat, [(0, 0)] * lead + [(0, short)])
    return flat.reshape(flat.shape[:lead] + (-1, width))


def pack_rows(arrays, lead, width):
    pieces = [as_rows(a, lead, width) for a in arrays]
    short = -sum(p.shape[lead] for p in pieces) % 16
    if short:
        pieces.append(jnp.zeros(pieces[0].shape[:lead] + (short, width), pieces[0].dtype))
    return jnp.concatenate(pieces, axis=lead)


def unpack_rows(packed, lead, shapes):
    width, start, parts = packed.shape[-1], 0, []
    for shape in shapes:
        amount = math.prod(shape)
        rows = -(-amount // width)
        piece = lax.slice_in_dim(packed, start, start + rows, axis=lead)
        if rows * width != amount:
            piece = piece.reshape(piece.shape[:lead] + (-1,))[..., :amount]
        parts.append(piece.reshape(packed.shape[:lead] + shape))
        start += rows
    return parts


def rms_scale(values):
    return lax.rsqrt(jnp.mean(values * values, axis=-1, keepdims=True) + NORM_EPS)


def rotate_pairs(values, cosine, sine):
    first, second = jnp.split(values, 2, axis=-1)
    return jnp.concatenate([first * cosine - second * sine, second * cosine + first * sine], axis=-1)


def unrotate_pairs(values, cosine, sine):
    first, second = jnp.split(values, 2, axis=-1)
    return jnp.concatenate([first * cosine + second * sine, second * cosine - first * sine], axis=-1)


def rope_tables(places, factor):
    freqs = 1.0 / ROPE_BASE ** (jnp.arange(0, HEAD_DIM, 2).astype(WIDE) / HEAD_DIM)
    angles = (places.astype(WIDE) / factor)[:, None] * freqs[None, :]
    return jnp.cos(angles), jnp.sin(angles)


def dot(equation, left, right):
    return jnp.einsum(equation, left, right, preferred_element_type=WIDE)


def on_device(
    layer_input, document_ids, expert_routes, rope_factor, attention_gain, feedforward_gain,
    query_weight, key_weight, value_weight, output_weight, router_weight, gate_up, down_weight, cotangent,
):
    nseq, nctx = lax.axis_size("seq"), lax.axis_size("ctx")
    tokens, width = layer_input.shape[1:]
    length = tokens * nctx
    rows, experts, ff2 = gate_up.shape
    ff = ff2 // 2
    down_rows = down_weight.shape[0]
    per_unit = max(1, experts // nctx)
    ff_split = max(1, nctx // experts)
    ff_part = ff // ff_split
    head_split = nctx // KV_HEADS
    unit = lax.axis_index("ctx")
    scale = HEAD_DIM**-0.5

    gu_pack = (
        gate_up.astype(LOW).reshape(rows, experts, 2, ff_split, ff_part).transpose(1, 3, 0, 2, 4)
        .reshape(nctx, per_unit, rows, 2 * ff_part)
    )
    down_pack = jnp.repeat(
        down_weight.astype(LOW).transpose(1, 0, 2), ff_split, axis=0
    ).reshape(nctx, per_unit, down_rows, width)
    out_pack = jnp.broadcast_to(output_weight.astype(LOW)[None], (nctx, rows, width))
    head_pack = jnp.concatenate(
        [
            query_weight.reshape(rows, KV_HEADS, GROUP * HEAD_DIM),
            key_weight.reshape(rows, KV_HEADS, HEAD_DIM),
            value_weight.reshape(rows, KV_HEADS, HEAD_DIM),
        ],
        axis=-1,
    ).astype(LOW).transpose(1, 0, 2)
    head_pack = jnp.repeat(head_pack, head_split, axis=0)
    small_pack = jnp.concatenate(
        [router_weight, attention_gain[:, None], feedforward_gain[:, None]], axis=1
    ).astype(LOW).T.reshape(-1)
    small_pack = jnp.broadcast_to(small_pack[None], (nctx, small_pack.shape[0]))
    shapes = [
        (per_unit, rows, 2 * ff_part), (per_unit, down_rows, width), (rows, width),
        (rows, HEAD_COLS), (experts + 2, rows),
    ]
    pack = pack_rows([gu_pack, down_pack, out_pack, head_pack, small_pack], 1, width)
    documents = jnp.broadcast_to(document_ids.reshape(1, tokens), (16, tokens))

    inputs_all, upstream_all, documents_all, whole = spread_all(
        [layer_input[0], cotangent[0], documents], pack, nctx, nseq, 1
    )
    gu_full, down_full, out_full, head_full, small_full = unpack_rows(whole, 2, shapes)
    gu_full = gu_full.reshape(nseq * nctx, per_unit, rows, 2 * ff_part).transpose(1, 0, 2, 3)
    gu_full = gu_full.reshape(per_unit, width, 2 * ff_part)
    down_full = down_full.reshape(nseq * nctx, per_unit, down_rows, width).transpose(1, 0, 2, 3)
    down_full = down_full.reshape(per_unit, ff, width)
    if ff_split > 1:
        down_full = lax.dynamic_slice_in_dim(down_full, (unit % ff_split) * ff_part, ff_part, 1)
    out_full = out_full.reshape(HEADS * HEAD_DIM, width)
    head_full = head_full.reshape(width, HEAD_COLS)
    small_full = small_full.reshape(nseq * nctx, experts + 2, rows).transpose(1, 0, 2).reshape(experts + 2, width)
    router_full = small_full[:experts]
    gain_one = small_full[experts].astype(WIDE)
    gain_two = small_full[experts + 1].astype(WIDE)

    hidden_all = inputs_all.reshape(length, width).astype(WIDE)
    scale_all = rms_scale(hidden_all)
    normed_all = hidden_all * scale_all
    attend_input = (normed_all * gain_one).astype(LOW)
    heads_pre = dot("td,dj->tj", attend_input, head_full)
    places = jnp.arange(length, dtype=jnp.int32)
    cosine, sine = rope_tables(places, rope_factor[0])
    query_pre = heads_pre[:, : GROUP * HEAD_DIM].reshape(length, GROUP, HEAD_DIM)
    keys = rotate_pairs(heads_pre[:, GROUP * HEAD_DIM : -HEAD_DIM], cosine, sine).astype(LOW)
    values = heads_pre[:, -HEAD_DIM:].astype(LOW)
    queries = rotate_pairs(query_pre, cosine[:, None], sine[:, None]).astype(LOW)
    docs = documents_all[:, 0].reshape(length)

    def my_rows(array):
        if head_split == 1:
            return array
        blocks = array.reshape((nctx // head_split, head_split, tokens) + array.shape[1:])
        picked = lax.dynamic_index_in_dim(blocks, unit % head_split, 1, keepdims=False)
        return picked.reshape((length // head_split,) + array.shape[1:])

    def all_rows(array):
        if head_split == 1:
            return array
        blocks = array.reshape((nctx // head_split, 1, tokens) + array.shape[1:])
        empty = jnp.zeros((nctx // head_split, head_split, tokens) + array.shape[1:], array.dtype)
        start = (0, unit % head_split) + (0,) * (blocks.ndim - 2)
        return lax.dynamic_update_slice(empty, blocks, start).reshape((length,) + array.shape[1:])

    my_queries = my_rows(queries).transpose(1, 0, 2)
    my_docs, my_places = my_rows(docs), my_rows(places)
    allowed = (places[None, :] <= my_places[:, None]) & (docs[None, :] == my_docs[:, None])
    scores = jnp.where(allowed[None], dot("gqd,nd->gqn", my_queries, keys) * scale, NEG_BIG)
    peak = jnp.max(scores, axis=-1, keepdims=True)
    expo = jnp.exp(scores - peak)
    probs = expo / jnp.sum(expo, axis=-1, keepdims=True)
    probs_low = probs.astype(LOW)
    attended = dot("gqn,nd->gqd", probs_low, values)
    head_out = attended.transpose(1, 0, 2).reshape(KV_HEADS, tokens, GROUP * HEAD_DIM).astype(LOW)
    mixed = exchange_ctx(head_out, nctx, head_split, 2)
    mixed_low = mixed.transpose(1, 0, 2).reshape(tokens, HEADS * HEAD_DIM)

    inputs = layer_input[0].astype(WIDE)
    middle = inputs + dot("tj,jd->td", mixed_low, out_full)
    scale_two = rms_scale(middle)
    normed_two = middle * scale_two
    expert_input = (normed_two * gain_two).astype(LOW)
    logits = dot("td,ed->te", expert_input, router_full)
    chosen = jnp.any(
        expert_routes[0][:, :, None] == jnp.arange(experts, dtype=jnp.int32)[None, None, :], axis=1
    )
    picked = jnp.where(chosen, logits, NEG_BIG)
    expo_gate = jnp.where(chosen, jnp.exp(picked - jnp.max(picked, axis=-1, keepdims=True)), 0.0)
    combine = expo_gate / jnp.sum(expo_gate, axis=-1, keepdims=True)

    expert_all, combine_all = gather_ctx([expert_input, combine.T], nctx, 3)
    expert_all = expert_all.reshape(length, width)
    upstream_low = upstream_all.reshape(length, width)
    upstream_wide = upstream_low.astype(WIDE)
    first_expert = unit // ff_split * per_unit
    out_part = jnp.zeros((length, width), WIDE)
    back_part = jnp.zeros((length, width), WIDE)
    gate_grads, gu_grads, down_grads = [], [], []
    for i in range(per_unit):
        weight = lax.dynamic_index_in_dim(combine_all, first_expert + i, 1, keepdims=False).reshape(length, 1)
        gate_and_up = dot("td,df->tf", expert_all, gu_full[i])
        gate, up = gate_and_up[:, :ff_part], gate_and_up[:, ff_part:]
        sigmoid = 1.0 / (1.0 + jnp.exp(-gate))
        activated = gate / (1.0 + jnp.exp(-gate))
        hidden = (activated * up).astype(LOW)
        produced = dot("tf,fd->td", hidden, down_full[i])
        out_part = out_part + weight * produced
        gate_grads.append(jnp.sum(upstream_wide * produced, axis=-1))
        grad_low = (weight * upstream_wide).astype(LOW)
        hidden_grad = dot("td,fd->tf", grad_low, down_full[i])
        down_grads.append(dot("tf,td->fd", hidden, grad_low))
        both = jnp.concatenate(
            [hidden_grad * up * sigmoid * (1.0 + gate * (1.0 - sigmoid)), hidden_grad * activated], axis=-1
        ).astype(LOW)
        gu_grads.append(dot("td,tf->df", expert_all, both))
        back_part = back_part + dot("tf,df->td", both, gu_full[i])
    gate_grad_rows = jnp.stack(gate_grads, axis=0).reshape(per_unit, nctx, tokens).transpose(1, 0, 2)
    gate_grad_rows = jnp.pad(gate_grad_rows, ((0, 0), (0, -per_unit % 8), (0, 0)))
    mix, back_sum, gate_grad_all = reduce_ctx(
        [out_part.astype(LOW).reshape(nctx, tokens, width), back_part.astype(LOW).reshape(nctx, tokens, width)],
        nctx, 4, small=gate_grad_rows,
    )

    layer_output = (middle + mix).astype(LOW)[None]
    upstream = cotangent[0].astype(WIDE)
    gate_grad = gate_grad_all[:, :per_unit].reshape(experts, ff_split, tokens).sum(axis=1).T
    gate_grad = jnp.where(chosen, gate_grad, 0.0)
    select_grad = combine * (gate_grad - jnp.sum(combine * gate_grad, axis=-1, keepdims=True))
    logit_grad = select_grad.astype(LOW)
    back_two = back_sum + dot("te,ed->td", logit_grad, router_full)
    router_part = dot("te,td->ed", logit_grad, expert_input)
    gain_two_part = jnp.sum(back_two * normed_two, axis=0)
    normed_two_grad = back_two * gain_two
    middle_grad = upstream + scale_two * (
        normed_two_grad - normed_two * jnp.mean(normed_two_grad * normed_two, axis=-1, keepdims=True)
    )
    project_grad = middle_grad.astype(LOW)
    out_grad_part = dot("tj,td->jd", mixed_low, project_grad)
    mixed_grad = dot("td,jd->tj", project_grad, out_full).astype(LOW)
    mixed_grad = mixed_grad.reshape(tokens, KV_HEADS, GROUP * HEAD_DIM).transpose(1, 0, 2)

    head_grad = exchange_ctx(mixed_grad, nctx, head_split, 5)
    head_grad = head_grad.reshape(length // head_split, GROUP, HEAD_DIM).transpose(1, 0, 2)
    delta = jnp.sum(head_grad.astype(WIDE) * attended, axis=-1, keepdims=True)
    value_grad = dot("gqn,gqd->nd", probs_low, head_grad)
    prob_grad = dot("gqd,nd->gqn", head_grad, values)
    score_grad = (probs * (prob_grad - delta)).astype(LOW)
    query_grad = dot("gqn,nd->gqd", score_grad, keys) * scale
    key_grad = dot("gqn,gqd->nd", score_grad, my_queries) * scale
    cos_q, sin_q = my_rows(cosine)[:, None], my_rows(sine)[:, None]
    query_pre_grad = unrotate_pairs(query_grad.transpose(1, 0, 2), cos_q, sin_q)
    query_pre_grad = all_rows(query_pre_grad.reshape(length // head_split, GROUP * HEAD_DIM))
    key_pre_grad = unrotate_pairs(key_grad, cosine, sine)
    heads_grad = jnp.concatenate([query_pre_grad, key_pre_grad, value_grad], axis=-1).astype(LOW)
    head_grads = dot("td,tj->dj", attend_input, heads_grad)
    attend_grad = dot("tj,dj->td", heads_grad, head_full)
    gain_one_part = jnp.sum(attend_grad * normed_all, axis=0)

    small_grads = jnp.concatenate([router_part, gain_one_part[None], gain_two_part[None]], axis=0)
    down_stack = jnp.stack(down_grads)
    if ff_split > 1:
        down_stack = lax.dynamic_update_slice_in_dim(
            jnp.zeros((per_unit, ff, width), WIDE), down_stack, (unit % ff_split) * ff_part, 1
        )
    grads = pack_rows(
        [
            jnp.stack(gu_grads).astype(LOW).reshape(per_unit, nseq, nctx, rows, 2 * ff_part).transpose(1, 2, 0, 3, 4),
            down_stack.astype(LOW).reshape(per_unit, nseq, nctx, down_rows, width).transpose(1, 2, 0, 3, 4),
            out_grad_part.astype(LOW).reshape(nseq, nctx, rows, width),
            head_grads.astype(LOW).reshape(nseq, nctx, rows, HEAD_COLS),
            small_grads.astype(LOW).reshape(experts + 2, nseq, nctx, rows).transpose(1, 2, 0, 3),
        ],
        2,
        width,
    )
    (attend_sum,) = reduce_ctx([attend_grad.astype(LOW).reshape(nctx, tokens, width)], nctx, 6)
    landed = bring_home(grads, nctx, 7)
    gu_home, down_home, out_home, head_home, small_home = [p.astype(WIDE) for p in unpack_rows(landed, 1, shapes)]
    gate_up_gradient = (
        gu_home.reshape(experts, ff_split, rows, 2, ff_part).transpose(2, 0, 3, 1, 4).reshape(rows, experts, ff2)
    )
    down_gradient = down_home.reshape(experts, ff_split, down_rows, width).sum(axis=1).transpose(1, 0, 2)
    output_gradient = out_home.sum(axis=0)
    head_home = head_home.reshape(KV_HEADS, head_split, rows, HEAD_COLS).sum(axis=1).transpose(1, 0, 2)
    query_gradient = head_home[..., : GROUP * HEAD_DIM].reshape(rows, HEADS * HEAD_DIM)
    key_gradient = head_home[..., GROUP * HEAD_DIM : -HEAD_DIM].reshape(rows, KV_HEADS * HEAD_DIM)
    value_gradient = head_home[..., -HEAD_DIM:].reshape(rows, KV_HEADS * HEAD_DIM)
    small_home = small_home.sum(axis=0)
    router_gradient = small_home[:experts].T

    scale_one = rms_scale(inputs)
    normed_one = inputs * scale_one
    normed_one_grad = attend_sum * gain_one
    input_gradient = (
        middle_grad
        + scale_one
        * (normed_one_grad - normed_one * jnp.mean(normed_one_grad * normed_one, axis=-1, keepdims=True))
    ).astype(LOW)[None]
    return (
        layer_output, input_gradient, small_home[experts], small_home[experts + 1],
        query_gradient, key_gradient, value_gradient, output_gradient, router_gradient,
        gate_up_gradient, down_gradient,
    )


def solution(mesh):
    both = ("seq", "ctx")
    return jax.shard_map(
        on_device,
        mesh=mesh,
        in_specs=(
            P("seq", "ctx", None), P("seq", "ctx"), P("seq", "ctx", None), P(), P(both), P(both),
            P(both, None), P(both, None), P(both, None), P(both, None), P(both, None),
            P(both, None, None), P(both, None, None), P("seq", "ctx", None),
        ),
        out_specs=(
            P("seq", "ctx", None), P("seq", "ctx", None), P(both), P(both),
            P(both, None), P(both, None), P(both, None), P(both, None), P(both, None),
            P(both, None, None), P(both, None, None),
        ),
        check_vma=False,
    )
```

```python
import functools
import math

import jax
import jax.numpy as jnp
from jax import lax
from jax.experimental import pallas as pl
from jax.experimental.pallas import tpu as pltpu
from jax.sharding import PartitionSpec as P

HEADS = 16
KV_HEADS = 8
HEAD_DIM = 64
GROUP = HEADS // KV_HEADS
HEAD_COLS = (GROUP + 2) * HEAD_DIM

NORM_EPS = 1e-06
ROPE_BASE = 10000.0
NEG_BIG = -1e30
LOW = jnp.bfloat16
WIDE = jnp.float32
MESH = pl.DeviceIdType.MESH


def ring_place(index, size):
    half = index // 2
    return half + (index % 2) * (size - 1 - 2 * half)


def ring_member(place, size):
    place = (place + 2 * size) % size
    far = place // (size // 2)
    return 2 * place + far * (2 * size - 1 - 4 * place)


def slot_of(distance, size):
    if distance == 0:
        return 0
    if abs(distance) == size // 2:
        return 1
    return 2 * abs(distance) + (distance > 0)


def core_mate(index):
    return index + 1 - 2 * (index % 2)


def row_mate(index):
    return (index + 2) % 4


def push(src, dst, send, recv, **where):
    return pltpu.make_async_remote_copy(
        src_ref=src, dst_ref=dst, send_sem=send, recv_sem=recv, device_id=where, device_id_type=MESH
    )


def greet(peers):
    barrier = pltpu.get_barrier_semaphore()
    for where in peers:
        pl.semaphore_signal(barrier, inc=1, device_id=where, device_id_type=MESH)
    pl.semaphore_wait(barrier, len(peers))


def ring_peers(size):
    place = ring_place(lax.axis_index("ctx"), size)
    return ring_member(place + 1, size), ring_member(place - 1, size)


class RingGather:
    def __init__(self, size, source, target, send, recv, relative=False):
        self.size, self.source, self.target, self.send, self.recv = size, source, target, send, recv
        self.relative = relative
        self.place = ring_place(lax.axis_index("ctx"), size)
        self.right, self.left = ring_peers(size)
        self.steps = size // 2

    def _copy(self, way, step, arriving):
        sign = 2 * way - 1
        rows = self.source.shape[0]
        part = pl.ds(way * (rows // 2), rows // 2) if step == self.steps - 1 else pl.ds(0, rows)
        if self.relative:
            here, there = slot_of(sign * step, self.size), slot_of(sign * (step + 1), self.size)
        else:
            here = there = ring_member(self.place + sign * (step + arriving), self.size)
        dst = self.target.at[there, part]
        src = self.target.at[here, part] if step else self.source.at[part]
        where = self.left if way else self.right
        return push(dst if arriving else src, dst, self.send.at[way, step], self.recv.at[way, step], ctx=where)

    def start(self, step):
        for way in range(2):
            if step:
                self._copy(way, step - 1, 1).wait_recv()
            self._copy(way, step, 0).start()

    def land(self):
        for way in range(2):
            self._copy(way, self.steps - 1, 1).wait_recv()

    def drain(self):
        for way in range(2):
            for step in range(self.steps):
                self._copy(way, step, 0).wait_send()

    def finish(self):
        self.land()
        self.drain()


def row_step(rows):
    return rows if rows < 16 else 16


def sum_into(target, parts):
    rows = target.shape[-2]
    step = row_step(rows)

    def add_at(lead):
        def body(r, _):
            at = lead + (pl.ds(pl.multiple_of(r * step, step), step),)
            total = parts[0][at].astype(WIDE)
            for part in parts[1:]:
                total = total + part[at].astype(WIDE)
            target[at] = total.astype(target.dtype)
            return 0

        lax.fori_loop(0, rows // step, body, 0)

    for lead in [()] if target.ndim == 2 else [(u,) for u in range(target.shape[0])]:
        add_at(lead)


def dot_nn(a, b):
    return lax.dot_general(a, b, (((1,), (0,)), ((), ())), preferred_element_type=WIDE)


def dot_nt(a, b):
    return lax.dot_general(a, b, (((1,), (1,)), ((), ())), preferred_element_type=WIDE)


def dot_tn(a, b):
    return lax.dot_general(a, b, (((0,), (0,)), ((), ())), preferred_element_type=WIDE)


class RingReduce:
    def __init__(self, size, held, send, recv):
        self.size, self.held, self.send, self.recv = size, held, send, recv
        self.place = ring_place(lax.axis_index("ctx"), size)
        self.right, self.left = ring_peers(size)
        self.steps = size // 2
        self.rows = held.shape[2]

    def owner(self, way, step):
        ahead = self.steps - step
        return ring_member(self.place + ahead if way == 0 else self.place - ahead, self.size)

    def _copy(self, way, step, source):
        half = self.rows // 2
        part = pl.ds(0, self.rows) if step else pl.ds(half * way, half)
        where = self.right if way == 0 else self.left
        return push(
            source, self.held.at[way, step, part], self.send.at[way, step], self.recv.at[way, step], ctx=where
        )

    def start(self, step, own):
        for way in range(2):
            half = self.rows // 2
            near = pl.ds(0, half) if way == 0 else pl.ds(half, half)
            far = pl.ds(half, half) if way == 0 else pl.ds(0, half)
            source = own[way].at[near]
            if step:
                self._copy(way, step - 1, source).wait_recv()
                source = self.held.at[way, step - 1]
                if step == 1:
                    sum_into(source.at[near], [own[way].at[near], source.at[near]])
                    sum_into(source.at[far], [own[way].at[far]])
                else:
                    sum_into(source, [own[way], source])
            self._copy(way, step, source).start()

    def finish(self, target, own, first):
        last, half = self.steps - 1, self.rows // 2
        for way in range(2):
            self._copy(way, last, self.held.at[way, last]).wait_recv()
        sum_into(target, [own, self.held.at[0, last], self.held.at[1, last]])
        for way in range(2):
            for step in range(self.steps):
                source = self.held.at[way, step - 1] if step else first.at[pl.ds(half * way, half)]
                self._copy(way, step, source).wait_send()


def expert_kernel(
    size, split,
    expert_input, combine_rows, upstream, gu_hbm, down_hbm,
    mix, back_sum, gate_home, gu_grads, down_grads,
    tokens_all, combine_all, gu_weight, down_weight, combine_cols, gate_up, hidden, both_grad, out_acc, out_own,
    back_own, gate_send, held_out, held_back,
    send_b, recv_b, send_c, recv_c, send_y, recv_y, send_d, recv_d, send_g, recv_g, own_sem,
):
    me = lax.axis_index("ctx")
    place = ring_place(me, size)
    per_unit, width, ff2 = gu_weight.shape
    ff = ff2 // 2
    tokens = expert_input.shape[0]
    group = 2 * tokens
    groups = size // 2
    first_expert = me // split * per_unit
    greet([{"ctx": (me + k) % size} for k in range(1, size)])

    loads = [
        pltpu.make_async_copy(expert_input, tokens_all.at[0], own_sem.at[0]),
        pltpu.make_async_copy(combine_rows, combine_all.at[0], own_sem.at[1]),
        pltpu.make_async_copy(gu_hbm, gu_weight, own_sem.at[2]),
        pltpu.make_async_copy(down_hbm, down_weight, own_sem.at[3]),
    ]
    rings = [
        RingGather(size, combine_rows, combine_all, send_c, recv_c, True),
        RingGather(size, expert_input, tokens_all, send_b, recv_b, True),
    ]
    for ring in rings:
        ring.start(0)
    for load in loads:
        load.start()
    for load in loads:
        load.wait()
    lanes = lax.broadcasted_iota(jnp.int32, (group, 128), 1)

    def forward(turn, _):
        for step in range(1, groups):
            @pl.when(turn == step - 1)
            def _():
                for ring in rings:
                    ring.start(step)

        @pl.when(turn == groups - 1)
        def _():
            for ring in rings:
                ring.land()

        g = (turn + 1) % groups
        pair = pl.ds(2 * g, 2)
        rows = pl.ds(pl.multiple_of(g * group, group), group)
        token = tokens_all[pair].reshape(group, width)
        up_wide = upstream[pair].reshape(group, width).astype(WIDE)
        weights = jnp.concatenate([combine_all[2 * g].T, combine_all[2 * g + 1].T], axis=0)
        names = lax.broadcasted_iota(jnp.int32, weights.shape, 1)
        out_acc[...] = jnp.zeros_like(out_acc)

        def one(e, gates):
            weight = jnp.sum(jnp.where(names == first_expert + e, weights, 0.0), axis=1, keepdims=True)
            combine_cols[e, rows] = jnp.broadcast_to(weight, (group, 128))
            both = dot_nn(token, gu_weight[e])
            gate_up[e, rows] = both.astype(gate_up.dtype)
            gate, up = both[:, :ff], both[:, ff:]
            hid = (gate / (1.0 + jnp.exp(-gate)) * up).astype(LOW)
            hidden[e, rows] = hid
            produced = dot_nn(hid, down_weight[e])
            out_acc[...] += weight * produced
            dg = jnp.sum(up_wide * produced, axis=1, keepdims=True)
            return jnp.where(lanes == e, dg, gates)

        gates = lax.fori_loop(0, per_unit, one, jnp.zeros((group, 128), WIDE)).T
        gate_send[2 * g] = gates[:8, :tokens]
        gate_send[2 * g + 1] = gates[:8, tokens:]
        out_own[pair] = out_acc[...].astype(LOW).reshape(2, tokens, width)
        return 0

    lax.fori_loop(0, groups, forward, 0)

    def gate_copy(distance):
        there = ring_member(place + distance, size)
        k = distance % size
        return push(gate_send.at[slot_of(distance, size)], gate_home.at[me], send_g.at[k], recv_g.at[k], ctx=there)

    distances = [d for d in range(1 - groups, groups + 1) if d]
    for distance in distances:
        gate_copy(distance).start()
    gate_home[me] = gate_send[0]

    ring_out = RingReduce(size, held_out, send_y, recv_y)
    ring_back = RingReduce(size, held_back, send_d, recv_d)

    def backward(turn, _):
        for step in range(groups):
            @pl.when(turn == step)
            def _():
                ring_out.start(
                    step, [out_own.at[slot_of(groups - step, size)], out_own.at[slot_of(step - groups, size)]]
                )

        g = (groups - turn) % groups
        pair = pl.ds(2 * g, 2)
        rows = pl.ds(pl.multiple_of(g * group, group), group)
        up_wide = upstream[pair].reshape(group, width).astype(WIDE)
        out_acc[...] = jnp.zeros_like(out_acc)

        def one(e, _):
            weight = combine_cols[e, rows][:, 0:1]
            grad = (weight * up_wide).astype(LOW)
            hid_grad = dot_nt(grad, down_weight[e])
            gate = gate_up[e, rows, pl.ds(0, ff)].astype(WIDE)
            up = gate_up[e, rows, pl.ds(ff, ff)].astype(WIDE)
            sigmoid = 1.0 / (1.0 + jnp.exp(-gate))
            gate_part = (hid_grad * up * sigmoid * (1.0 + gate * (1.0 - sigmoid))).astype(LOW)
            up_part = (hid_grad * (gate * sigmoid)).astype(LOW)
            both_grad[e, rows, pl.ds(0, ff)] = gate_part
            both_grad[e, rows, pl.ds(ff, ff)] = up_part
            out_acc[...] += dot_nt(both_grad[e, rows], gu_weight[e])
            return 0

        lax.fori_loop(0, per_unit, one, 0)
        near = 2 * ((g + groups - 1) // groups)
        back_own[pl.ds(near, 2)] = out_acc[...].astype(LOW).reshape(2, tokens, width)
        for step in range(groups):
            @pl.when(turn == step)
            def _():
                ring_back.start(step, [back_own.at[1]] * 2 if step == 0 else [back_own.at[3], back_own.at[2]])
        return 0

    lax.fori_loop(0, groups, backward, 0)

    tile = 256
    length = size * tokens

    def gu_tile(j, _):
        turned = tokens_all[:, :, pl.ds(pl.multiple_of(j * tile, tile), tile)].reshape(length, tile)
        turned = turned.astype(WIDE).T.astype(LOW)
        depth = gu_grads.shape[2]
        count = tile // depth

        def one(e, _):
            part = dot_nn(turned, both_grad[e]).reshape(count, depth, ff2)
            gu_grads[e, pl.ds(j * count, count)] = part.astype(LOW)
            return 0

        return lax.fori_loop(0, per_unit, one, 0)

    lax.fori_loop(0, width // tile, gu_tile, 0)

    def down_tile(index, _):
        e, j = index // (ff // tile), index % (ff // tile)
        turned = hidden[e, :, pl.ds(pl.multiple_of(j * tile, tile), tile)].astype(WIDE).T.astype(LOW)
        depth = down_grads.shape[2]
        count = tile // depth
        for half in range(2):
            cols = pl.ds(half * (width // 2), width // 2)
            grad = upstream[:, :, cols].reshape(length, width // 2).astype(WIDE) * combine_cols[e][:, 0:1]
            part = dot_nn(turned, grad.astype(LOW)).reshape(count, depth, width // 2)
            down_grads[e, pl.ds(j * count, count), :, cols] = part.astype(LOW)
        return 0

    lax.fori_loop(0, per_unit * (ff // tile), down_tile, 0)

    ring_back.finish(back_sum, back_own.at[0], back_own.at[1])
    ring_out.finish(mix, out_own.at[0], out_own.at[1])
    for ring in rings:
        ring.drain()
    for distance in distances:
        here = ring_member(place - distance, size)
        k = distance % size
        push(gate_send.at[0], gate_home.at[here], send_g.at[k], recv_g.at[k], ctx=here).wait_recv()
        gate_copy(distance).wait_send()


def run_experts(expert_input, combine_rows, upstream, gu_full, down_full, size, split, owners, down_rows, collective):
    tokens, width = expert_input.shape
    per_unit, _, ff2 = gu_full.shape
    ff = ff2 // 2
    length = size * tokens
    dma = pltpu.SemaphoreType.DMA
    vmem = pl.BlockSpec(memory_space=pltpu.VMEM)
    anywhere = pl.BlockSpec(memory_space=pl.ANY)
    steps = (2, size // 2)
    return pl.pallas_call(
        functools.partial(expert_kernel, size, split),
        out_shape=[
            jax.ShapeDtypeStruct((tokens, width), WIDE),
            jax.ShapeDtypeStruct((tokens, width), WIDE),
            jax.ShapeDtypeStruct((size, 8, tokens), WIDE),
            jax.ShapeDtypeStruct((per_unit, owners, width // owners, ff2), LOW),
            jax.ShapeDtypeStruct((per_unit, ff // down_rows, down_rows, width), LOW),
        ],
        in_specs=[vmem, vmem, vmem, anywhere, anywhere],
        out_specs=[vmem] * 5,
        scratch_shapes=[
            pltpu.VMEM((size, tokens, width), LOW),
            pltpu.VMEM((size,) + combine_rows.shape, WIDE),
            pltpu.VMEM(gu_full.shape, LOW),
            pltpu.VMEM(down_full.shape, LOW),
            pltpu.VMEM((per_unit, length, 128), WIDE),
            pltpu.VMEM((per_unit, length, ff2), WIDE if length <= 2048 else LOW),
            pltpu.VMEM((per_unit, length, ff), LOW),
            pltpu.VMEM((per_unit, length, ff2), LOW),
            pltpu.VMEM((2 * tokens, width), WIDE),
            pltpu.VMEM((size, tokens, width), LOW),
            pltpu.VMEM((4, tokens, width), LOW),
            pltpu.VMEM((size, 8, tokens), WIDE),
            pltpu.VMEM((2, size // 2, tokens, width), LOW),
            pltpu.VMEM((2, size // 2, tokens, width), LOW),
            dma(steps), dma(steps), dma(steps), dma(steps), dma(steps), dma(steps), dma(steps), dma(steps),
            dma((size,)), dma((size,)), dma((4,)),
        ],
        compiler_params=pltpu.CompilerParams(
            collective_id=collective, has_side_effects=True, vmem_limit_bytes=63 << 20
        ),
        name="run_experts",
    )(expert_input, combine_rows, upstream, gu_full, down_full)


def exchange_kernel(size, split, source, target, send, recv, own):
    me = lax.axis_index("ctx")
    lane, row = me % split, me // split
    number = size // split
    greet([{"ctx": ((row + k) % number) * split + lane} for k in range(1, number)])
    mine = pltpu.make_async_copy(source.at[row], target.at[row], own)
    mine.start()
    copies = []
    for k in range(1, number):
        there = (row + k) % number
        copies.append(push(source.at[there], target.at[row], send.at[k], recv.at[k], ctx=there * split + lane))
        copies[-1].start()
    for k in range(1, number):
        here = (row + number - k) % number
        push(source.at[here], target.at[here], send.at[k], recv.at[k], ctx=here * split + lane).wait_recv()
    for copy in copies:
        copy.wait_send()
    mine.wait()


def exchange_ctx(array, size, split, collective):
    return pl.pallas_call(
        functools.partial(exchange_kernel, size, split),
        out_shape=jax.ShapeDtypeStruct(array.shape, array.dtype),
        in_specs=[pl.BlockSpec(memory_space=pl.ANY)],
        out_specs=pl.BlockSpec(memory_space=pl.ANY),
        scratch_shapes=[
            pltpu.SemaphoreType.DMA((size // split,)),
            pltpu.SemaphoreType.DMA((size // split,)),
            pltpu.SemaphoreType.DMA,
        ],
        compiler_params=pltpu.CompilerParams(collective_id=collective, has_side_effects=True),
        name="exchange_ctx_%d" % collective,
    )(array)


def spread_kernel(size, count, *refs):
    sources, pack = refs[:count], refs[count]
    targets, whole = refs[count + 1 : 2 * count + 1], refs[2 * count + 1]
    send, recv, own, send_a, recv_a, send_b, recv_b, own_pack = refs[2 * count + 2 :]
    me, seq = lax.axis_index("ctx"), lax.axis_index("seq")
    greet(
        [{"ctx": (me + k) % size} for k in range(1, size)]
        + [{"seq": core_mate(seq)}, {"seq": row_mate(seq)}]
    )
    rings, local = [], []
    for i in range(count):
        local.append(pltpu.make_async_copy(sources[i], targets[i].at[0 if i == 1 else me], own.at[i]))
        rings.append(RingGather(size, sources[i], targets[i], send.at[i], recv.at[i], i == 1))
    local.append(pltpu.make_async_copy(pack.at[me], whole.at[seq, me], own_pack))
    for copy in local:
        copy.start()

    def outward(k):
        there = (me + k) % size
        return push(pack.at[there], whole.at[seq, me], send_a.at[k], recv_a.at[k], ctx=there)

    def inward(k):
        here = (me + size - k) % size
        return push(pack.at[here], whole.at[seq, here], send_a.at[k], recv_a.at[k], ctx=here)

    def sideways(which, k):
        here = (me + size - k) % size
        slab = whole.at[row_mate(seq) if which == 2 else seq, here]
        mate = row_mate(seq) if which == 1 else core_mate(seq)
        return push(slab, slab, send_b.at[which, k], recv_b.at[which, k], seq=mate)

    def landing(which, k):
        here = (me + size - k) % size
        owner = (core_mate(seq), row_mate(seq), core_mate(row_mate(seq)))[which]
        slab = whole.at[owner, here]
        return push(slab, slab, send_b.at[which, k], recv_b.at[which, k], seq=core_mate(seq))

    for ring in rings:
        ring.start(0)
    for k in range(1, size):
        outward(k).start()
    local[-1].wait()
    sideways(1, 0).start()
    sideways(0, 0).start()
    steps = size // 2
    for k in range(1, size):
        if k < steps:
            for ring in rings:
                ring.start(k)
        inward(k).wait_recv()
        sideways(1, k).start()
        sideways(0, k).start()
        landing(1, k - 1).wait_recv()
        sideways(2, k - 1).start()
    landing(1, size - 1).wait_recv()
    sideways(2, size - 1).start()
    for ring in rings:
        ring.finish()
    for copy in local[:-1]:
        copy.wait()
    for k in range(size):
        landing(0, k).wait_recv()
        landing(2, k).wait_recv()
        for which in range(3):
            sideways(which, k).wait_send()
        if k:
            outward(k).wait_send()


def spread_all(arrays, pack, size, rows, collective):
    count = len(arrays)
    shapes = [jax.ShapeDtypeStruct((size,) + a.shape, a.dtype) for a in arrays]
    shapes.append(jax.ShapeDtypeStruct((rows,) + pack.shape, pack.dtype))
    return pl.pallas_call(
        functools.partial(spread_kernel, size, count),
        out_shape=shapes,
        in_specs=[pl.BlockSpec(memory_space=pl.ANY)] * (count + 1),
        out_specs=[pl.BlockSpec(memory_space=pl.ANY)] * (count + 1),
        scratch_shapes=[
            pltpu.SemaphoreType.DMA((count, 2, size // 2)),
            pltpu.SemaphoreType.DMA((count, 2, size // 2)),
            pltpu.SemaphoreType.DMA((count,)),
            pltpu.SemaphoreType.DMA((size,)),
            pltpu.SemaphoreType.DMA((size,)),
            pltpu.SemaphoreType.DMA((3, size)),
            pltpu.SemaphoreType.DMA((3, size)),
            pltpu.SemaphoreType.DMA,
        ],
        compiler_params=pltpu.CompilerParams(collective_id=collective, has_side_effects=True),
        name="spread_all",
    )(*arrays, pack)


class Homing:
    def __init__(self, size, grads, out, bufs, sems):
        self.size, self.grads, self.out = size, grads, out
        self.near, self.from_core, self.from_row, self.to_row, self.to_home = bufs
        self.load, self.send_a, self.recv_a, self.send_b, self.recv_b, self.send_c, self.recv_c = sems
        self.me, self.seq = lax.axis_index("ctx"), lax.axis_index("seq")

    def _block(self, s0, k):
        index = s0 * self.size + (self.me + k) % self.size
        return self.grads.at[:, index] if self.grads.ndim == 4 else self.grads.at[index]

    def _row(self, which):
        return row_mate(self.seq) if which == 0 else self.seq

    def fetch(self, which, k):
        return pltpu.make_async_copy(self._block(self._row(which), k), self.near.at[which, k], self.load.at[which, k])

    def to_core(self, which, k):
        return push(
            self._block(core_mate(self._row(which)), k), self.from_core.at[which, k],
            self.send_a.at[which, k], self.recv_a.at[which, k], seq=core_mate(self.seq),
        )

    def across(self, k):
        return push(
            self.to_row.at[k], self.from_row.at[k], self.send_b.at[k], self.recv_b.at[k], seq=row_mate(self.seq)
        )

    def homeward(self, k):
        there = (self.me + k) % self.size
        return push(self.to_home.at[k], self.out.at[self.me], self.send_c.at[k], self.recv_c.at[k], ctx=there)

    def arriving(self, k):
        here = (self.me + self.size - k) % self.size
        return push(self.to_home.at[k], self.out.at[here], self.send_c.at[k], self.recv_c.at[k], ctx=here)

    def start(self):
        def body(k, _):
            for which in range(2):
                self.to_core(which, k).start()
                self.fetch(which, k).start()
            return 0

        lax.fori_loop(0, self.size, body, 0)

    def first(self, k):
        self.fetch(0, k).wait()
        self.to_core(0, k).wait_recv()
        sum_into(self.to_row.at[k], [self.near.at[0, k], self.from_core.at[0, k]])
        self.across(k).start()

    def second(self, k, home=False):
        self.fetch(1, k).wait()
        self.to_core(1, k).wait_recv()
        self.across(k).wait_recv()
        target = self.out.at[self.me] if home else self.to_home.at[k]
        sum_into(target, [self.near.at[1, k], self.from_core.at[1, k], self.from_row.at[k]])
        if not home:
            self.homeward(k).start()

    def close(self):
        def body(k, _):
            self.arriving(k).wait_recv()
            self.homeward(k).wait_send()
            return 0

        lax.fori_loop(1, self.size, body, 0)

        def drain(k, _):
            self.to_core(0, k).wait_send()
            self.to_core(1, k).wait_send()
            self.across(k).wait_send()
            return 0

        lax.fori_loop(0, self.size, drain, 0)

    @staticmethod
    def scratch(size, block):
        slab = (size,) + block
        dma = pltpu.SemaphoreType.DMA
        return [
            pltpu.VMEM((2,) + slab, LOW), pltpu.VMEM((2,) + slab, LOW), pltpu.VMEM(slab, LOW),
            pltpu.VMEM(slab, LOW), pltpu.VMEM(slab, LOW),
            dma((2, size)), dma((2, size)), dma((2, size)), dma((size,)), dma((size,)), dma((size,)), dma((size,)),
        ]


class SmallSum:
    def __init__(self, size, small, out, from_seq, total, from_ctx, sems):
        self.size, self.small, self.out = size, small, out
        self.from_seq, self.total, self.from_ctx = from_seq, total, from_ctx
        self.send_a, self.recv_a, self.send_b, self.recv_b = sems
        self.me, self.seq = lax.axis_index("ctx"), lax.axis_index("seq")

    def _swap(self, k):
        there = (self.seq + k) % 4
        return push(self.small.at[there], self.from_seq.at[k], self.send_a.at[k], self.recv_a.at[k], seq=there)

    def _tell(self, k):
        there = (self.me + k) % self.size
        return push(self.total, self.from_ctx.at[self.me], self.send_b.at[k], self.recv_b.at[k], ctx=there)

    def _hear(self, k):
        here = (self.me + self.size - k) % self.size
        return push(self.total, self.from_ctx.at[here], self.send_b.at[k], self.recv_b.at[k], ctx=here)

    def start(self):
        for k in range(1, 4):
            self._swap(k).start()

    def middle(self):
        for k in range(1, 4):
            self._swap(k).wait_recv()
        self.total[...] = self.small[self.seq] + self.from_seq[1] + self.from_seq[2] + self.from_seq[3]
        for k in range(1, self.size):
            self._tell(k).start()

    def finish(self):
        total = self.total[...]
        for k in range(1, self.size):
            self._hear(k).wait_recv()
            total = total + self.from_ctx[(self.me + self.size - k) % self.size]
        self.out[...] = total
        for k in range(1, 4):
            self._swap(k).wait_send()
        for k in range(1, self.size):
            self._tell(k).wait_send()

    @staticmethod
    def scratch(size, rows, lanes):
        dma = pltpu.SemaphoreType.DMA
        part = (rows, lanes // 4)
        return [
            pltpu.VMEM((4,) + part, WIDE), pltpu.VMEM(part, WIDE), pltpu.VMEM((size,) + part, WIDE),
            dma((4,)), dma((4,)), dma((size,)), dma((size,)),
        ]


def back_kernel(
    size, split, tile,
    mixed_grad, gu_grads, down_grads, out_grads, small, query_pair, key_value, out_pair, log_total,
    docs_row, docs_col, places_row, cosine, sine, gain, inputs_all, row_scale, head_weight,
    attend_sum, gu_home, down_home, out_home, head_home, small_home,
    head_grad, key_pad, value_pad, key_acc, value_acc, query_acc, heads_grad, heads_turned, head_part, small_full,
    attend_own, held, send_r, recv_r, send_x, recv_x, own_x, *scratch,
):
    me, seq = lax.axis_index("ctx"), lax.axis_index("seq")
    lane, row, number = me % split, me // split, size // split
    tokens = mixed_grad.shape[1]
    length, width = inputs_all.shape
    greet(
        [{"ctx": (me + k) % size} for k in range(1, size)]
        + [{"seq": (seq + k) % 4} for k in range(1, 4)]
    )

    def homing(i, grads, out):
        part = scratch[12 * i : 12 * i + 12]
        return Homing(size, grads, out, part[:5], part[5:])

    early = [homing(0, gu_grads, gu_home), homing(1, down_grads, down_home), homing(2, out_grads, out_home)]
    late = homing(3, head_part, head_home)
    tail = scratch[48:]
    total_small = SmallSum(size, small_full, small_home, tail[0], tail[1], tail[2], tail[3:])

    mine = pltpu.make_async_copy(mixed_grad.at[row], head_grad.at[row], own_x)
    mine.start()
    swaps = []
    for k in range(1, number):
        there = (row + k) % number
        swaps.append(
            push(mixed_grad.at[there], head_grad.at[row], send_x.at[k], recv_x.at[k], ctx=there * split + lane)
        )
        swaps[-1].start()
    for home in early:
        home.start()

    steps = []
    for k in range(size):
        steps += [functools.partial(home.first, k) for home in early]
    for k in range(1, size):
        steps += [functools.partial(home.second, k) for home in early]
    steps += [functools.partial(home.second, 0, True) for home in early]

    def pump(count):
        for _ in range(min(count, len(steps))):
            steps.pop(0)()

    half = lax.broadcasted_iota(jnp.int32, (tile, 2 * HEAD_DIM), 1) < HEAD_DIM
    zero = jnp.zeros((tile, 2 * HEAD_DIM), WIDE)

    def prepare(i, _):
        rows = pl.ds(pl.multiple_of(i * tile, tile), tile)
        pair = key_value[rows].astype(WIDE)
        turned = pltpu.roll(pair, HEAD_DIM, 1)
        key_pad[0, rows] = jnp.where(half, pair, zero).astype(LOW)
        key_pad[1, rows] = jnp.where(half, zero, turned).astype(LOW)
        value_pad[0, rows] = jnp.where(half, turned, zero).astype(LOW)
        value_pad[1, rows] = jnp.where(half, zero, pair).astype(LOW)
        key_acc[rows] = zero
        value_acc[rows] = zero
        heads_grad[rows, pl.ds(0, 2 * HEAD_DIM)] = zero.astype(LOW)
        return 0

    lax.fori_loop(0, length // tile, prepare, 0)
    for k in range(1, number):
        here = (row + number - k) % number
        push(mixed_grad.at[here], head_grad.at[here], send_x.at[k], recv_x.at[k], ctx=here * split + lane).wait_recv()
    mine.wait()

    scale = HEAD_DIM**-0.5
    blocks = tile // tokens
    for i in range(number * tokens // tile):
        rows = pl.ds(i * tile, tile)
        query = query_pair[rows]
        grad = head_grad[pl.ds(i * blocks, blocks)].reshape(tile, 2 * HEAD_DIM)
        product = (grad.astype(WIDE) * out_pair[rows].astype(WIDE)).T
        deltas = [
            jnp.sum(product[h * HEAD_DIM : (h + 1) * HEAD_DIM], axis=0, keepdims=True) for h in range(GROUP)
        ]
        query_doc, query_place = docs_row[0:1, rows], places_row[0:1, rows]
        totals = [log_total[h : h + 1, rows] for h in range(GROUP)]
        query_acc[...] = zero

        def pairs(j, _):
            keys = pl.ds(pl.multiple_of(j * tile, tile), tile)
            place = lax.broadcasted_iota(jnp.int32, (tile, tile), 0) + j * tile
            allowed = (place <= query_place) & (docs_col[keys] == query_doc)
            key_part, value_part, query_part = zero, zero, zero
            for h in range(GROUP):
                mine_half = half if h == 0 else jnp.logical_not(half)
                score = dot_nt(key_pad[h, keys], query)
                prob = jnp.where(allowed, jnp.exp(score * scale - totals[h]), 0.0)
                slope = dot_nt(value_pad[h, keys], grad)
                ds = (prob * (slope - deltas[h])).astype(LOW)
                value_part = jnp.where(mine_half, dot_nn(prob.astype(LOW), grad), value_part)
                key_part = jnp.where(mine_half, dot_nn(ds, query), key_part)
                query_part = query_part + dot_tn(ds, key_pad[h, keys])
            key_acc[keys] += key_part
            value_acc[keys] += value_part
            query_acc[...] += query_part
            return 0

        lax.fori_loop(0, min(length // tile, (i + 1) * split), pairs, 0)
        turn = query_acc[...] * scale
        for b in range(blocks):
            at = pl.ds(pl.multiple_of(((i * blocks + b) * split + lane) * tokens, tokens), tokens)
            piece = turn[b * tokens : (b + 1) * tokens]
            heads_grad[at, pl.ds(0, 2 * HEAD_DIM)] = unturn(piece, cosine, sine, at, 0).astype(LOW)
        pump(9)

    def fold(i, _):
        rows = pl.ds(pl.multiple_of(i * tile, tile), tile)
        key_part, value_part = key_acc[rows], value_acc[rows]
        key_part = (key_part + pltpu.roll(key_part, HEAD_DIM, 1)) * scale
        value_part = value_part + pltpu.roll(value_part, HEAD_DIM, 1)
        both = jnp.where(half, key_part, value_part)
        heads_grad[rows, pl.ds(2 * HEAD_DIM, 2 * HEAD_DIM)] = unturn(both, cosine, sine, rows, 1).astype(LOW)
        return 0

    lax.fori_loop(0, length // tile, fold, 0)

    def transpose(i, _):
        rows = pl.ds(pl.multiple_of(i * tile, tile), tile)
        heads_turned[:, rows] = heads_grad[rows].astype(WIDE).T.astype(LOW)
        return 0

    lax.fori_loop(0, length // tile, transpose, 0)

    reduce = RingReduce(size, held, send_r, recv_r)
    small_full[...] = small[...]
    gain_row = small.shape[1] - 8

    def attend(place, slot):
        owner = ring_member(place, size)
        rows = pl.ds(pl.multiple_of(owner * tokens, tokens), tokens)
        part = dot_nt(heads_grad[rows], head_weight[...])
        attend_own[slot] = part.astype(LOW)
        normed = inputs_all[rows].astype(WIDE) * row_scale[rows]
        share = jnp.sum(part * normed, axis=0, keepdims=True)
        lanes = width // 4
        for s0 in range(4):
            small_full[s0, gain_row : gain_row + 1] += share[:, s0 * lanes : (s0 + 1) * lanes]

    place = ring_place(me, size)
    half_ring = size // 2
    attend(place + half_ring, 0)
    reduce.start(0, [attend_own.at[0]] * 2)
    for step in range(1, half_ring):
        attend(place + half_ring - step, 1)
        attend(place - half_ring + step, 2)
        if step == 1:
            def columns(j, _):
                cols = pl.ds(pl.multiple_of(j * tile, tile), tile)
                normed = inputs_all[:, cols].astype(WIDE) * row_scale[...]
                part = dot_nn(heads_turned[...], (normed * gain[0:1, cols]).astype(LOW)).T.astype(LOW)
                depth = head_part.shape[1]
                head_part[pl.ds(j * (tile // depth), tile // depth)] = part.reshape(tile // depth, depth, HEAD_COLS)
                return 0

            lax.fori_loop(0, width // tile, columns, 0)
            late.start()
        reduce.start(step, [attend_own.at[1], attend_own.at[2]])
        pump(6)
    attend(place, 1)
    total_small.start()
    pump(len(steps))
    for k in range(size):
        late.first(k)
    total_small.middle()
    for k in range(1, size):
        late.second(k)
    late.second(0, True)
    reduce.finish(attend_sum, attend_own.at[1], attend_own.at[0])
    for home in early:
        home.close()
    late.close()
    total_small.finish()
    for copy in swaps:
        copy.wait_send()


def swap_halves(values):
    lane = lax.broadcasted_iota(jnp.int32, values.shape, 1) % HEAD_DIM
    return jnp.where(
        lane < HEAD_DIM // 2,
        pltpu.roll(values, values.shape[1] - HEAD_DIM // 2, 1),
        pltpu.roll(values, HEAD_DIM // 2, 1),
    )


def unturn(values, cosine, sine, rows, which):
    cos, sin = cosine[rows], sine[rows]
    if which:
        half = lax.broadcasted_iota(jnp.int32, values.shape, 1) < HEAD_DIM
        cos, sin = jnp.where(half, cos, 1.0), jnp.where(half, sin, 0.0)
    return values * cos - swap_halves(values) * sin


def attention_back(arrays, size, split, collective):
    (mixed_grad, gu_grads, down_grads, out_grads, small, query_pair, key_value, out_pair, log_total,
     docs_row, docs_col, places_row, cosine, sine, gain, inputs_all, row_scale, head_weight) = arrays
    tokens = mixed_grad.shape[1]
    length, width = inputs_all.shape
    tile = 2 * tokens
    blocks = [
        (gu_grads.shape[0],) + gu_grads.shape[2:], (down_grads.shape[0],) + down_grads.shape[2:],
        out_grads.shape[1:], (out_grads.shape[1], HEAD_COLS),
    ]
    small_rows = small.shape[1]
    dma = pltpu.SemaphoreType.DMA
    vmem = pl.BlockSpec(memory_space=pltpu.VMEM)
    anywhere = pl.BlockSpec(memory_space=pl.ANY)
    pair = (length, 2 * HEAD_DIM)
    scratch = [
        pltpu.VMEM(mixed_grad.shape, LOW),
        pltpu.VMEM((GROUP,) + pair, LOW), pltpu.VMEM((GROUP,) + pair, LOW),
        pltpu.VMEM(pair, WIDE), pltpu.VMEM(pair, WIDE), pltpu.VMEM((tile, 2 * HEAD_DIM), WIDE),
        pltpu.VMEM((length, HEAD_COLS), LOW), pltpu.VMEM((HEAD_COLS, length), LOW),
        pltpu.VMEM((4 * size, out_grads.shape[1], HEAD_COLS), LOW),
        pltpu.VMEM(small.shape, WIDE),
        pltpu.VMEM((3, tokens, width), LOW), pltpu.VMEM((2, size // 2, tokens, width), LOW),
        dma((2, size // 2)), dma((2, size // 2)), dma((size // split,)), dma((size // split,)), dma,
    ]
    for block in blocks:
        scratch += Homing.scratch(size, block)
    scratch += SmallSum.scratch(size, small_rows, width)
    return pl.pallas_call(
        functools.partial(back_kernel, size, split, tile),
        out_shape=[jax.ShapeDtypeStruct((tokens, width), WIDE)]
        + [jax.ShapeDtypeStruct((size,) + block, LOW) for block in blocks]
        + [jax.ShapeDtypeStruct((small_rows, width // 4), WIDE)],
        in_specs=[vmem, anywhere, anywhere, anywhere] + [vmem] * 14,
        out_specs=[vmem] * 6,
        scratch_shapes=scratch,
        compiler_params=pltpu.CompilerParams(
            collective_id=collective, has_side_effects=True, vmem_limit_bytes=62 << 20
        ),
        name="attention_back",
    )(*arrays)


def as_rows(array, lead, width):
    flat = array.reshape(array.shape[:lead] + (-1,))
    short = -flat.shape[-1] % width
    if short:
        flat = jnp.pad(flat, [(0, 0)] * lead + [(0, short)])
    return flat.reshape(flat.shape[:lead] + (-1, width))


def pack_rows(arrays, lead, width):
    pieces = [as_rows(a, lead, width) for a in arrays]
    short = -sum(p.shape[lead] for p in pieces) % 16
    if short:
        pieces.append(jnp.zeros(pieces[0].shape[:lead] + (short, width), pieces[0].dtype))
    return jnp.concatenate(pieces, axis=lead)


def unpack_rows(packed, lead, shapes):
    width, start, parts = packed.shape[-1], 0, []
    for shape in shapes:
        amount = math.prod(shape)
        rows = -(-amount // width)
        piece = lax.slice_in_dim(packed, start, start + rows, axis=lead)
        if rows * width != amount:
            piece = piece.reshape(piece.shape[:lead] + (-1,))[..., :amount]
        parts.append(piece.reshape(packed.shape[:lead] + shape))
        start += rows
    return parts


def rms_scale(values):
    return lax.rsqrt(jnp.mean(values * values, axis=-1, keepdims=True) + NORM_EPS)


def rotate_pairs(values, cosine, sine):
    first, second = jnp.split(values, 2, axis=-1)
    return jnp.concatenate([first * cosine - second * sine, second * cosine + first * sine], axis=-1)


def unrotate_pairs(values, cosine, sine):
    first, second = jnp.split(values, 2, axis=-1)
    return jnp.concatenate([first * cosine + second * sine, second * cosine - first * sine], axis=-1)


def rope_tables(places, factor):
    freqs = 1.0 / ROPE_BASE ** (jnp.arange(0, HEAD_DIM, 2).astype(WIDE) / HEAD_DIM)
    angles = (places.astype(WIDE) / factor)[:, None] * freqs[None, :]
    return jnp.cos(angles), jnp.sin(angles)


def dot(equation, left, right):
    return jnp.einsum(equation, left, right, preferred_element_type=WIDE)


def on_device(
    layer_input, document_ids, expert_routes, rope_factor, attention_gain, feedforward_gain,
    query_weight, key_weight, value_weight, output_weight, router_weight, gate_up, down_weight, cotangent,
):
    nseq, nctx = lax.axis_size("seq"), lax.axis_size("ctx")
    tokens, width = layer_input.shape[1:]
    length = tokens * nctx
    rows, experts, ff2 = gate_up.shape
    ff = ff2 // 2
    down_rows = down_weight.shape[0]
    per_unit = max(1, experts // nctx)
    ff_split = max(1, nctx // experts)
    ff_part = ff // ff_split
    head_split = nctx // KV_HEADS
    unit = lax.axis_index("ctx")
    scale = HEAD_DIM**-0.5

    gu_pack = (
        gate_up.astype(LOW).reshape(rows, experts, 2, ff_split, ff_part).transpose(1, 3, 0, 2, 4)
        .reshape(nctx, per_unit, rows, 2 * ff_part)
    )
    down_pack = jnp.repeat(
        down_weight.astype(LOW).transpose(1, 0, 2), ff_split, axis=0
    ).reshape(nctx, per_unit, down_rows, width)
    out_pack = jnp.broadcast_to(output_weight.astype(LOW)[None], (nctx, rows, width))
    head_pack = jnp.concatenate(
        [
            query_weight.reshape(rows, KV_HEADS, GROUP * HEAD_DIM),
            key_weight.reshape(rows, KV_HEADS, HEAD_DIM),
            value_weight.reshape(rows, KV_HEADS, HEAD_DIM),
        ],
        axis=-1,
    ).astype(LOW).transpose(1, 0, 2)
    head_pack = jnp.repeat(head_pack, head_split, axis=0)
    small_pack = jnp.concatenate(
        [router_weight, attention_gain[:, None], feedforward_gain[:, None]], axis=1
    ).astype(LOW).T.reshape(-1)
    small_pack = jnp.broadcast_to(small_pack[None], (nctx, small_pack.shape[0]))
    shapes = [
        (per_unit, rows, 2 * ff_part), (per_unit, down_rows, width), (rows, width),
        (rows, HEAD_COLS), (experts + 2, rows),
    ]
    pack = pack_rows([gu_pack, down_pack, out_pack, head_pack, small_pack], 1, width)
    documents = jnp.broadcast_to(document_ids.reshape(1, tokens), (16, tokens))

    inputs_all, upstream_all, documents_all, whole = spread_all(
        [layer_input[0], cotangent[0], documents], pack, nctx, nseq, 1
    )
    gu_full, down_full, out_full, head_full, small_full = unpack_rows(whole, 2, shapes)
    gu_full = gu_full.reshape(nseq * nctx, per_unit, rows, 2 * ff_part).transpose(1, 0, 2, 3)
    gu_full = gu_full.reshape(per_unit, width, 2 * ff_part)
    down_full = down_full.reshape(nseq * nctx, per_unit, down_rows, width).transpose(1, 0, 2, 3)
    down_full = down_full.reshape(per_unit, ff, width)
    if ff_split > 1:
        down_full = lax.dynamic_slice_in_dim(down_full, (unit % ff_split) * ff_part, ff_part, 1)
    out_full = out_full.reshape(HEADS * HEAD_DIM, width)
    head_full = head_full.reshape(width, HEAD_COLS)
    small_full = small_full.reshape(nseq * nctx, experts + 2, rows).transpose(1, 0, 2).reshape(experts + 2, width)
    router_full = small_full[:experts]
    gain_one = small_full[experts].astype(WIDE)
    gain_two = small_full[experts + 1].astype(WIDE)

    hidden_all = inputs_all.reshape(length, width).astype(WIDE)
    scale_all = rms_scale(hidden_all)
    normed_all = hidden_all * scale_all
    attend_input = (normed_all * gain_one).astype(LOW)
    heads_pre = dot("td,dj->tj", attend_input, head_full)
    places = jnp.arange(length, dtype=jnp.int32)
    cosine, sine = rope_tables(places, rope_factor[0])
    query_pre = heads_pre[:, : GROUP * HEAD_DIM].reshape(length, GROUP, HEAD_DIM)
    keys = rotate_pairs(heads_pre[:, GROUP * HEAD_DIM : -HEAD_DIM], cosine, sine).astype(LOW)
    values = heads_pre[:, -HEAD_DIM:].astype(LOW)
    queries = rotate_pairs(query_pre, cosine[:, None], sine[:, None]).astype(LOW)
    docs = documents_all[:, 0].reshape(length)

    def my_rows(array):
        if head_split == 1:
            return array
        blocks = array.reshape((nctx // head_split, head_split, tokens) + array.shape[1:])
        picked = lax.dynamic_index_in_dim(blocks, unit % head_split, 1, keepdims=False)
        return picked.reshape((length // head_split,) + array.shape[1:])

    def all_rows(array):
        if head_split == 1:
            return array
        blocks = array.reshape((nctx // head_split, 1, tokens) + array.shape[1:])
        empty = jnp.zeros((nctx // head_split, head_split, tokens) + array.shape[1:], array.dtype)
        start = (0, unit % head_split) + (0,) * (blocks.ndim - 2)
        return lax.dynamic_update_slice(empty, blocks, start).reshape((length,) + array.shape[1:])

    my_queries = my_rows(queries).transpose(1, 0, 2)
    my_docs, my_places = my_rows(docs), my_rows(places)
    allowed = (places[None, :] <= my_places[:, None]) & (docs[None, :] == my_docs[:, None])
    scores = jnp.where(allowed[None], dot("gqd,nd->gqn", my_queries, keys) * scale, NEG_BIG)
    peak = jnp.max(scores, axis=-1, keepdims=True)
    expo = jnp.exp(scores - peak)
    probs = expo / jnp.sum(expo, axis=-1, keepdims=True)
    probs_low = probs.astype(LOW)
    attended = dot("gqn,nd->gqd", probs_low, values)
    out_pair = attended.transpose(1, 0, 2).reshape(length // head_split, GROUP * HEAD_DIM)
    log_total = jnp.pad((peak + jnp.log(jnp.sum(expo, axis=-1, keepdims=True)))[..., 0], ((0, 8 - GROUP), (0, 0)))
    head_out = out_pair.reshape(KV_HEADS, tokens, GROUP * HEAD_DIM).astype(LOW)
    mixed = exchange_ctx(head_out, nctx, head_split, 2)
    mixed_low = mixed.transpose(1, 0, 2).reshape(tokens, HEADS * HEAD_DIM)

    inputs = layer_input[0].astype(WIDE)
    middle = inputs + dot("tj,jd->td", mixed_low, out_full)
    scale_two = rms_scale(middle)
    normed_two = middle * scale_two
    expert_input = (normed_two * gain_two).astype(LOW)
    logits = dot("td,ed->te", expert_input, router_full)
    chosen = jnp.any(
        expert_routes[0][:, :, None] == jnp.arange(experts, dtype=jnp.int32)[None, None, :], axis=1
    )
    picked = jnp.where(chosen, logits, NEG_BIG)
    expo_gate = jnp.where(chosen, jnp.exp(picked - jnp.max(picked, axis=-1, keepdims=True)), 0.0)
    combine = expo_gate / jnp.sum(expo_gate, axis=-1, keepdims=True)

    owners = nseq * nctx
    mix, back_sum, gate_grad_all, gu_grads, down_grads = run_experts(
        expert_input, combine.T, upstream_all, gu_full, down_full, nctx, ff_split, owners, down_rows, 3
    )

    layer_output = (middle + mix).astype(LOW)[None]
    upstream = cotangent[0].astype(WIDE)
    gate_grad = gate_grad_all[:, :per_unit].reshape(experts, ff_split, tokens).sum(axis=1).T
    gate_grad = jnp.where(chosen, gate_grad, 0.0)
    select_grad = combine * (gate_grad - jnp.sum(combine * gate_grad, axis=-1, keepdims=True))
    logit_grad = select_grad.astype(LOW)
    back_two = back_sum + dot("te,ed->td", logit_grad, router_full)
    router_part = dot("te,td->ed", logit_grad, expert_input)
    gain_two_part = jnp.sum(back_two * normed_two, axis=0)
    normed_two_grad = back_two * gain_two
    middle_grad = upstream + scale_two * (
        normed_two_grad - normed_two * jnp.mean(normed_two_grad * normed_two, axis=-1, keepdims=True)
    )
    project_grad = middle_grad.astype(LOW)
    out_grad_part = dot("tj,td->jd", mixed_low, project_grad)
    mixed_grad = dot("td,jd->tj", project_grad, out_full).astype(LOW)
    mixed_grad = mixed_grad.reshape(tokens, KV_HEADS, GROUP * HEAD_DIM).transpose(1, 0, 2)

    small_grads = jnp.concatenate(
        [router_part, gain_two_part[None], jnp.zeros((31 - experts, width), WIDE)], axis=0
    ).reshape(32, nseq, width // nseq).transpose(1, 0, 2)
    if ff_split > 1:
        down_grads = lax.dynamic_update_slice_in_dim(
            jnp.zeros((per_unit, owners, down_rows, width), LOW), down_grads,
            (unit % ff_split) * (ff_part // down_rows), 1,
        )
    cos_table = jnp.concatenate([cosine] * 4, axis=1)
    sin_table = jnp.concatenate([-sine, sine] * 2, axis=1)
    attend_sum, gu_home, down_home, out_home, head_home, small_home = attention_back(
        [
            mixed_grad,
            gu_grads,
            down_grads,
            out_grad_part.astype(LOW).reshape(owners, rows, width),
            small_grads,
            my_queries.transpose(1, 0, 2).reshape(length // head_split, GROUP * HEAD_DIM),
            jnp.concatenate([keys, values], axis=1),
            out_pair,
            log_total,
            jnp.broadcast_to(my_docs[None], (8, length // head_split)),
            docs[:, None],
            jnp.broadcast_to(my_places[None], (8, length // head_split)),
            cos_table, sin_table, jnp.broadcast_to(gain_one[None], (8, width)),
            inputs_all.reshape(length, width),
            scale_all, head_full,
        ],
        nctx, head_split, 7,
    )
    gu_home, down_home = gu_home.astype(WIDE), down_home.astype(WIDE)
    out_home, head_home = out_home.astype(WIDE), head_home.astype(WIDE)
    gate_up_gradient = (
        gu_home.reshape(experts, ff_split, rows, 2, ff_part).transpose(2, 0, 3, 1, 4).reshape(rows, experts, ff2)
    )
    down_gradient = down_home.reshape(experts, ff_split, down_rows, width).sum(axis=1).transpose(1, 0, 2)
    output_gradient = out_home.sum(axis=0)
    head_home = head_home.reshape(KV_HEADS, head_split, rows, HEAD_COLS).sum(axis=1).transpose(1, 0, 2)
    query_gradient = head_home[..., : GROUP * HEAD_DIM].reshape(rows, HEADS * HEAD_DIM)
    key_gradient = head_home[..., GROUP * HEAD_DIM : -HEAD_DIM].reshape(rows, KV_HEADS * HEAD_DIM)
    value_gradient = head_home[..., -HEAD_DIM:].reshape(rows, KV_HEADS * HEAD_DIM)
    small_home = lax.dynamic_slice_in_dim(small_home, unit * rows, rows, axis=1)
    router_gradient = small_home[:experts].T

    scale_one = rms_scale(inputs)
    normed_one = inputs * scale_one
    normed_one_grad = attend_sum * gain_one
    input_gradient = (
        middle_grad
        + scale_one
        * (normed_one_grad - normed_one * jnp.mean(normed_one_grad * normed_one, axis=-1, keepdims=True))
    ).astype(LOW)[None]
    return (
        layer_output, input_gradient, small_home[24], small_home[experts],
        query_gradient, key_gradient, value_gradient, output_gradient, router_gradient,
        gate_up_gradient, down_gradient,
    )


def solution(mesh):
    both = ("seq", "ctx")
    return jax.shard_map(
        on_device,
        mesh=mesh,
        in_specs=(
            P("seq", "ctx", None), P("seq", "ctx"), P("seq", "ctx", None), P(), P(both), P(both),
            P(both, None), P(both, None), P(both, None), P(both, None), P(both, None),
            P(both, None, None), P(both, None, None), P("seq", "ctx", None),
        ),
        out_specs=(
            P("seq", "ctx", None), P("seq", "ctx", None), P(both), P(both),
            P(both, None), P(both, None), P(both, None), P(both, None), P(both, None),
            P(both, None, None), P(both, None, None),
        ),
        check_vma=False,
    )
```

```python
import functools
import math

import jax
import jax.numpy as jnp
from jax import lax
from jax.experimental import pallas as pl
from jax.experimental.pallas import tpu as pltpu
from jax.sharding import PartitionSpec as P

HEADS = 16
KV_HEADS = 8
HEAD_DIM = 64
GROUP = HEADS // KV_HEADS
HEAD_COLS = (GROUP + 2) * HEAD_DIM

NORM_EPS = 1e-06
ROPE_BASE = 10000.0
NEG_BIG = -1e30
LOW = jnp.bfloat16
WIDE = jnp.float32
MESH = pl.DeviceIdType.MESH


def ring_place(index, size):
    half = index // 2
    return half + (index % 2) * (size - 1 - 2 * half)


def ring_member(place, size):
    place = (place + 2 * size) % size
    far = place // (size // 2)
    return 2 * place + far * (2 * size - 1 - 4 * place)


def slot_of(distance, size):
    if distance == 0:
        return 0
    if abs(distance) == size // 2:
        return 1
    return 2 * abs(distance) + (distance > 0)


def core_mate(index):
    return index + 1 - 2 * (index % 2)


def row_mate(index):
    return (index + 2) % 4


def push(src, dst, send, recv, **where):
    return pltpu.make_async_remote_copy(
        src_ref=src, dst_ref=dst, send_sem=send, recv_sem=recv, device_id=where, device_id_type=MESH
    )


def greet(peers):
    barrier = pltpu.get_barrier_semaphore()
    for where in peers:
        pl.semaphore_signal(barrier, inc=1, device_id=where, device_id_type=MESH)
    pl.semaphore_wait(barrier, len(peers))


def ring_peers(size):
    place = ring_place(lax.axis_index("ctx"), size)
    return ring_member(place + 1, size), ring_member(place - 1, size)


class RingGather:
    def __init__(self, size, source, target, send, recv, relative=False):
        self.size, self.source, self.target, self.send, self.recv = size, source, target, send, recv
        self.relative = relative
        self.place = ring_place(lax.axis_index("ctx"), size)
        self.right, self.left = ring_peers(size)
        self.steps = size // 2

    def _copy(self, way, step, arriving):
        sign = 2 * way - 1
        rows = self.source.shape[0]
        part = pl.ds(way * (rows // 2), rows // 2) if step == self.steps - 1 else pl.ds(0, rows)
        if self.relative:
            here, there = slot_of(sign * step, self.size), slot_of(sign * (step + 1), self.size)
        else:
            here = there = ring_member(self.place + sign * (step + arriving), self.size)
        dst = self.target.at[there, part]
        src = self.target.at[here, part] if step else self.source.at[part]
        where = self.left if way else self.right
        return push(dst if arriving else src, dst, self.send.at[way, step], self.recv.at[way, step], ctx=where)

    def start(self, step):
        for way in range(2):
            if step:
                self._copy(way, step - 1, 1).wait_recv()
            self._copy(way, step, 0).start()

    def land(self):
        for way in range(2):
            self._copy(way, self.steps - 1, 1).wait_recv()

    def drain(self):
        for way in range(2):
            for step in range(self.steps):
                self._copy(way, step, 0).wait_send()

    def finish(self):
        self.land()
        self.drain()


def row_step(rows):
    return rows if rows < 16 else 16


def sum_into(target, parts):
    rows = target.shape[-2]
    step = row_step(rows)

    def add_at(lead):
        def body(r, _):
            at = lead + (pl.ds(pl.multiple_of(r * step, step), step),)
            total = parts[0][at].astype(WIDE)
            for part in parts[1:]:
                total = total + part[at].astype(WIDE)
            target[at] = total.astype(target.dtype)
            return 0

        lax.fori_loop(0, rows // step, body, 0)

    for lead in [()] if target.ndim == 2 else [(u,) for u in range(target.shape[0])]:
        add_at(lead)


def dot_nn(a, b):
    return lax.dot_general(a, b, (((1,), (0,)), ((), ())), preferred_element_type=WIDE)


def dot_nt(a, b):
    return lax.dot_general(a, b, (((1,), (1,)), ((), ())), preferred_element_type=WIDE)


def dot_tn(a, b):
    return lax.dot_general(a, b, (((0,), (0,)), ((), ())), preferred_element_type=WIDE)


class RingReduce:
    def __init__(self, size, held, send, recv):
        self.size, self.held, self.send, self.recv = size, held, send, recv
        self.place = ring_place(lax.axis_index("ctx"), size)
        self.right, self.left = ring_peers(size)
        self.steps = size // 2
        self.rows = held.shape[2]

    def owner(self, way, step):
        ahead = self.steps - step
        return ring_member(self.place + ahead if way == 0 else self.place - ahead, self.size)

    def _copy(self, way, step, source):
        half = self.rows // 2
        part = pl.ds(0, self.rows) if step else pl.ds(half * way, half)
        where = self.right if way == 0 else self.left
        return push(
            source, self.held.at[way, step, part], self.send.at[way, step], self.recv.at[way, step], ctx=where
        )

    def start(self, step, own):
        for way in range(2):
            half = self.rows // 2
            near = pl.ds(0, half) if way == 0 else pl.ds(half, half)
            far = pl.ds(half, half) if way == 0 else pl.ds(0, half)
            source = own[way].at[near]
            if step:
                self._copy(way, step - 1, source).wait_recv()
                source = self.held.at[way, step - 1]
                if step == 1:
                    sum_into(source.at[near], [own[way].at[near], source.at[near]])
                    sum_into(source.at[far], [own[way].at[far]])
                else:
                    sum_into(source, [own[way], source])
            self._copy(way, step, source).start()

    def finish(self, target, own, first):
        last, half = self.steps - 1, self.rows // 2
        for way in range(2):
            self._copy(way, last, self.held.at[way, last]).wait_recv()
        sum_into(target, [own, self.held.at[0, last], self.held.at[1, last]])
        for way in range(2):
            for step in range(self.steps):
                source = self.held.at[way, step - 1] if step else first.at[pl.ds(half * way, half)]
                self._copy(way, step, source).wait_send()


def expert_kernel(
    size, split,
    expert_input, combine_rows, upstream, gu_hbm, down_hbm,
    mix, back_sum, gate_home, gu_grads, down_grads,
    tokens_all, combine_all, gu_weight, down_weight, combine_cols, gate_up, hidden, both_grad, out_acc, out_own,
    back_own, gate_send, held_out, held_back,
    send_b, recv_b, send_c, recv_c, send_y, recv_y, send_d, recv_d, send_g, recv_g, own_sem,
):
    me = lax.axis_index("ctx")
    place = ring_place(me, size)
    per_unit, width, ff2 = gu_weight.shape
    ff = ff2 // 2
    tokens = expert_input.shape[0]
    group = 2 * tokens
    groups = size // 2
    first_expert = me // split * per_unit
    greet([{"ctx": (me + k) % size} for k in range(1, size)])

    loads = [
        pltpu.make_async_copy(expert_input, tokens_all.at[0], own_sem.at[0]),
        pltpu.make_async_copy(combine_rows, combine_all.at[0], own_sem.at[1]),
        pltpu.make_async_copy(gu_hbm, gu_weight, own_sem.at[2]),
        pltpu.make_async_copy(down_hbm, down_weight, own_sem.at[3]),
    ]
    rings = [
        RingGather(size, combine_rows, combine_all, send_c, recv_c, True),
        RingGather(size, expert_input, tokens_all, send_b, recv_b, True),
    ]
    for ring in rings:
        ring.start(0)
    for load in loads:
        load.start()
    for load in loads:
        load.wait()
    lanes = lax.broadcasted_iota(jnp.int32, (group, 128), 1)

    def forward(turn, _):
        for step in range(1, groups):
            @pl.when(turn == step - 1)
            def _():
                for ring in rings:
                    ring.start(step)

        @pl.when(turn == groups - 1)
        def _():
            for ring in rings:
                ring.land()

        g = (turn + 1) % groups
        pair = pl.ds(2 * g, 2)
        rows = pl.ds(pl.multiple_of(g * group, group), group)
        token = tokens_all[pair].reshape(group, width)
        up_wide = upstream[pair].reshape(group, width).astype(WIDE)
        weights = jnp.concatenate([combine_all[2 * g].T, combine_all[2 * g + 1].T], axis=0)
        names = lax.broadcasted_iota(jnp.int32, weights.shape, 1)
        out_acc[...] = jnp.zeros_like(out_acc)

        def one(e, gates):
            weight = jnp.sum(jnp.where(names == first_expert + e, weights, 0.0), axis=1, keepdims=True)
            combine_cols[e, rows] = jnp.broadcast_to(weight, (group, 128))
            both = dot_nn(token, gu_weight[e])
            gate_up[e, rows] = both.astype(gate_up.dtype)
            gate, up = both[:, :ff], both[:, ff:]
            hid = (gate / (1.0 + jnp.exp(-gate)) * up).astype(LOW)
            hidden[e, rows] = hid
            produced = dot_nn(hid, down_weight[e])
            out_acc[...] += weight * produced
            dg = jnp.sum(up_wide * produced, axis=1, keepdims=True)
            return jnp.where(lanes == e, dg, gates)

        gates = lax.fori_loop(0, per_unit, one, jnp.zeros((group, 128), WIDE)).T
        gate_send[2 * g] = gates[:8, :tokens]
        gate_send[2 * g + 1] = gates[:8, tokens:]
        out_own[pair] = out_acc[...].astype(LOW).reshape(2, tokens, width)
        return 0

    lax.fori_loop(0, groups, forward, 0)

    def gate_copy(distance):
        there = ring_member(place + distance, size)
        k = distance % size
        return push(gate_send.at[slot_of(distance, size)], gate_home.at[me], send_g.at[k], recv_g.at[k], ctx=there)

    distances = [d for d in range(1 - groups, groups + 1) if d]
    for distance in distances:
        gate_copy(distance).start()
    gate_home[me] = gate_send[0]

    ring_out = RingReduce(size, held_out, send_y, recv_y)
    ring_back = RingReduce(size, held_back, send_d, recv_d)

    def backward(turn, _):
        for step in range(groups):
            @pl.when(turn == step)
            def _():
                ring_out.start(
                    step, [out_own.at[slot_of(groups - step, size)], out_own.at[slot_of(step - groups, size)]]
                )

        g = (groups - turn) % groups
        pair = pl.ds(2 * g, 2)
        rows = pl.ds(pl.multiple_of(g * group, group), group)
        up_wide = upstream[pair].reshape(group, width).astype(WIDE)
        out_acc[...] = jnp.zeros_like(out_acc)

        def one(e, _):
            weight = combine_cols[e, rows][:, 0:1]
            grad = (weight * up_wide).astype(LOW)
            hid_grad = dot_nt(grad, down_weight[e])
            gate = gate_up[e, rows, pl.ds(0, ff)].astype(WIDE)
            up = gate_up[e, rows, pl.ds(ff, ff)].astype(WIDE)
            sigmoid = 1.0 / (1.0 + jnp.exp(-gate))
            gate_part = (hid_grad * up * sigmoid * (1.0 + gate * (1.0 - sigmoid))).astype(LOW)
            up_part = (hid_grad * (gate * sigmoid)).astype(LOW)
            both_grad[e, rows, pl.ds(0, ff)] = gate_part
            both_grad[e, rows, pl.ds(ff, ff)] = up_part
            out_acc[...] += dot_nt(both_grad[e, rows], gu_weight[e])
            return 0

        lax.fori_loop(0, per_unit, one, 0)
        near = 2 * ((g + groups - 1) // groups)
        back_own[pl.ds(near, 2)] = out_acc[...].astype(LOW).reshape(2, tokens, width)
        for step in range(groups):
            @pl.when(turn == step)
            def _():
                ring_back.start(step, [back_own.at[1]] * 2 if step == 0 else [back_own.at[3], back_own.at[2]])
        return 0

    lax.fori_loop(0, groups, backward, 0)

    tile = 256
    length = size * tokens

    def gu_tile(j, _):
        turned = tokens_all[:, :, pl.ds(pl.multiple_of(j * tile, tile), tile)].reshape(length, tile)
        turned = turned.astype(WIDE).T.astype(LOW)
        depth = gu_grads.shape[2]
        count = tile // depth

        def one(e, _):
            part = dot_nn(turned, both_grad[e]).reshape(count, depth, ff2)
            gu_grads[e, pl.ds(j * count, count)] = part.astype(LOW)
            return 0

        return lax.fori_loop(0, per_unit, one, 0)

    lax.fori_loop(0, width // tile, gu_tile, 0)

    def down_tile(index, _):
        e, j = index // (ff // tile), index % (ff // tile)
        turned = hidden[e, :, pl.ds(pl.multiple_of(j * tile, tile), tile)].astype(WIDE).T.astype(LOW)
        depth = down_grads.shape[2]
        count = tile // depth
        for half in range(2):
            cols = pl.ds(half * (width // 2), width // 2)
            grad = upstream[:, :, cols].reshape(length, width // 2).astype(WIDE) * combine_cols[e][:, 0:1]
            part = dot_nn(turned, grad.astype(LOW)).reshape(count, depth, width // 2)
            down_grads[e, pl.ds(j * count, count), :, cols] = part.astype(LOW)
        return 0

    lax.fori_loop(0, per_unit * (ff // tile), down_tile, 0)

    ring_back.finish(back_sum, back_own.at[0], back_own.at[1])
    ring_out.finish(mix, out_own.at[0], out_own.at[1])
    for ring in rings:
        ring.drain()
    for distance in distances:
        here = ring_member(place - distance, size)
        k = distance % size
        push(gate_send.at[0], gate_home.at[here], send_g.at[k], recv_g.at[k], ctx=here).wait_recv()
        gate_copy(distance).wait_send()


def run_experts(expert_input, combine_rows, upstream, gu_full, down_full, size, split, owners, down_rows, collective):
    tokens, width = expert_input.shape
    per_unit, _, ff2 = gu_full.shape
    ff = ff2 // 2
    length = size * tokens
    dma = pltpu.SemaphoreType.DMA
    vmem = pl.BlockSpec(memory_space=pltpu.VMEM)
    anywhere = pl.BlockSpec(memory_space=pl.ANY)
    steps = (2, size // 2)
    return pl.pallas_call(
        functools.partial(expert_kernel, size, split),
        out_shape=[
            jax.ShapeDtypeStruct((tokens, width), WIDE),
            jax.ShapeDtypeStruct((tokens, width), WIDE),
            jax.ShapeDtypeStruct((size, 8, tokens), WIDE),
            jax.ShapeDtypeStruct((per_unit, owners, width // owners, ff2), LOW),
            jax.ShapeDtypeStruct((per_unit, ff // down_rows, down_rows, width), LOW),
        ],
        in_specs=[vmem, vmem, vmem, anywhere, anywhere],
        out_specs=[vmem] * 5,
        scratch_shapes=[
            pltpu.VMEM((size, tokens, width), LOW),
            pltpu.VMEM((size,) + combine_rows.shape, WIDE),
            pltpu.VMEM(gu_full.shape, LOW),
            pltpu.VMEM(down_full.shape, LOW),
            pltpu.VMEM((per_unit, length, 128), WIDE),
            pltpu.VMEM((per_unit, length, ff2), WIDE if length <= 2048 else LOW),
            pltpu.VMEM((per_unit, length, ff), LOW),
            pltpu.VMEM((per_unit, length, ff2), LOW),
            pltpu.VMEM((2 * tokens, width), WIDE),
            pltpu.VMEM((size, tokens, width), LOW),
            pltpu.VMEM((4, tokens, width), LOW),
            pltpu.VMEM((size, 8, tokens), WIDE),
            pltpu.VMEM((2, size // 2, tokens, width), LOW),
            pltpu.VMEM((2, size // 2, tokens, width), LOW),
            dma(steps), dma(steps), dma(steps), dma(steps), dma(steps), dma(steps), dma(steps), dma(steps),
            dma((size,)), dma((size,)), dma((4,)),
        ],
        compiler_params=pltpu.CompilerParams(
            collective_id=collective, has_side_effects=True, vmem_limit_bytes=63 << 20
        ),
        name="run_experts",
    )(expert_input, combine_rows, upstream, gu_full, down_full)


class Spread:
    def __init__(self, size, source, slab, sems):
        self.size, self.source, self.slab = size, source, slab
        self.send_a, self.recv_a, self.send_b, self.recv_b, self.own = sems
        self.me, self.seq = lax.axis_index("ctx"), lax.axis_index("seq")

    def _from(self, k):
        return (self.me + self.size - k) % self.size

    def local(self):
        return pltpu.make_async_copy(self.source(self.me), self.slab(self.seq * self.size + self.me), self.own)

    def outward(self, k):
        there = (self.me + k) % self.size
        slab = self.slab(self.seq * self.size + self.me)
        return push(self.source(there), slab, self.send_a.at[k], self.recv_a.at[k], ctx=there)

    def inward(self, k):
        here = self._from(k)
        slab = self.slab(self.seq * self.size + here)
        return push(self.source(here), slab, self.send_a.at[k], self.recv_a.at[k], ctx=here)

    def sideways(self, which, k):
        owner = row_mate(self.seq) if which == 2 else self.seq
        slab = self.slab(owner * self.size + self._from(k))
        mate = row_mate(self.seq) if which == 1 else core_mate(self.seq)
        return push(slab, slab, self.send_b.at[which, k], self.recv_b.at[which, k], seq=mate)

    def landing(self, which, k):
        owner = (core_mate(self.seq), row_mate(self.seq), core_mate(row_mate(self.seq)))[which]
        slab = self.slab(owner * self.size + self._from(k))
        return push(slab, slab, self.send_b.at[which, k], self.recv_b.at[which, k], seq=core_mate(self.seq))

    def start(self):
        for k in range(1, self.size):
            self.outward(k).start()

    def step(self, k):
        if k == 0:
            self.local().wait()
        else:
            self.inward(k).wait_recv()
        self.sideways(1, k).start()
        self.sideways(0, k).start()
        if k:
            self.pass_on(k - 1)

    def pass_on(self, k):
        self.landing(1, k).wait_recv()
        self.sideways(2, k).start()

    def land(self):
        for k in range(self.size):
            self.landing(0, k).wait_recv()
            self.landing(2, k).wait_recv()

    def drain(self):
        for k in range(self.size):
            for which in range(3):
                self.sideways(which, k).wait_send()
            if k:
                self.outward(k).wait_send()

    @staticmethod
    def scratch(size):
        dma = pltpu.SemaphoreType.DMA
        return [dma((size,)), dma((size,)), dma((3, size)), dma((3, size)), dma]


def front_kernel(
    size, split, tile,
    tokens_in, upstream, docs_in, cos_turned, sin_turned, pack, gu_pack, down_pack, out_rows,
    inputs_all, upstream_all, mixed, query_pair, key_value, out_pair, log_total, docs_row, docs_col, places_row,
    cosine, sine, row_scale, head_weight, small, gu_full, down_full, out_full,
    docs_all, pack_all, key_pad, value_turned, head_out,
    send_t, recv_t, send_u, recv_u, send_n, recv_n, send_x, recv_x, own, *scratch,
):
    me, seq = lax.axis_index("ctx"), lax.axis_index("seq")
    lane, row, number = me % split, me // split, size // split
    tokens, width = tokens_in.shape
    steps = size // 2
    place = ring_place(me, size)
    greet(
        [{"ctx": (me + k) % size} for k in range(1, size)]
        + [{"seq": core_mate(seq)}, {"seq": row_mate(seq)}]
    )
    heads = Spread(size, lambda c: pack.at[c], lambda owner: pack_all.at[owner], scratch[0:5])
    bulk = [
        Spread(size, lambda c: gu_pack.at[c], lambda owner: gu_full.at[:, owner], scratch[5:10]),
        Spread(size, lambda c: down_pack.at[c], lambda owner: down_full.at[:, owner], scratch[10:15]),
        Spread(size, lambda c: out_rows, lambda owner: out_full.at[owner], scratch[15:20]),
    ]
    ring = RingGather(size, tokens_in, inputs_all, send_t, recv_t)
    ring_up = RingGather(size, upstream, upstream_all, send_u, recv_u, True)

    def note(k):
        return push(docs_in, docs_all.at[me], send_n.at[k], recv_n.at[k], ctx=(me + k) % size)

    def noted(k):
        here = (me + size - k) % size
        return push(docs_in, docs_all.at[here], send_n.at[k], recv_n.at[k], ctx=here)

    heads.start()
    for k in range(1, size):
        note(k).start()
    ring.start(0)
    heads.local().start()
    local = [
        pltpu.make_async_copy(tokens_in, inputs_all.at[me], own.at[0]),
        pltpu.make_async_copy(upstream, upstream_all.at[0], own.at[1]),
    ]
    for copy in local:
        copy.start()
    for part in bulk:
        part.local().start()
    docs_all[me] = docs_in[...]

    def tables(i, _):
        rows = pl.ds(pl.multiple_of(i * tile, tile), tile)
        cos, sin = cos_turned[:, rows], sin_turned[:, rows]
        cosine[rows] = jnp.concatenate([cos] * 4, axis=0).T
        sine[rows] = jnp.concatenate([-sin, sin] * 2, axis=0).T
        return 0

    lax.fori_loop(0, size * tokens // tile, tables, 0)
    for k in range(size):
        heads.step(k)
    heads.pass_on(size - 1)
    for part in bulk:
        part.step(0)
    ring.start(1)
    for k in range(1, size):
        noted(k).wait_recv()
    log_total[...] = jnp.zeros_like(log_total)

    def documents(c, _):
        rows = pl.ds(pl.multiple_of(c * tokens, tokens), tokens)
        docs_col[rows] = docs_all[c].astype(WIDE).T[:, 0:1].astype(jnp.int32)
        return 0

    lax.fori_loop(0, size, documents, 0)

    def my_documents(b, _):
        rows = pl.ds(pl.multiple_of(b * tokens, tokens), tokens)
        docs_row[:, rows] = docs_all[b * split + lane]
        first = (b * split + lane) * tokens
        places_row[:, rows] = lax.broadcasted_iota(jnp.int32, (8, tokens), 1) + first
        return 0

    lax.fori_loop(0, number, my_documents, 0)
    heads.land()
    whole = pack_all[...].astype(WIDE).reshape(width, pack_all.shape[2])
    head_weight[...] = whole[:, :HEAD_COLS].astype(LOW)
    small[...] = whole[:, HEAD_COLS:].T[: small.shape[0]]
    gain_row = small.shape[0] - 8
    for copy in local:
        copy.wait()

    half = lax.broadcasted_iota(jnp.int32, (tokens, 2 * HEAD_DIM), 1) < HEAD_DIM

    def project(spot):
        owner = ring_member(spot, size)
        rows = pl.ds(pl.multiple_of(owner * tokens, tokens), tokens)
        values = inputs_all[owner].astype(WIDE)
        scale_one = lax.rsqrt(jnp.mean(values * values, axis=-1, keepdims=True) + NORM_EPS)
        row_scale[rows] = scale_one
        attend = (values * scale_one * small[gain_row : gain_row + 1]).astype(LOW)
        pre = dot_nn(attend, head_weight[...])
        cos, sin = cosine[rows], sine[rows]
        query, pair = pre[:, : 2 * HEAD_DIM], pre[:, 2 * HEAD_DIM :]
        query = query * cos + swap_halves(query) * sin
        pair = pair * jnp.where(half, cos, 1.0) + swap_halves(pair) * jnp.where(half, sin, 0.0)
        key_value[rows] = pair.astype(LOW)
        key_pad[0, rows] = jnp.where(half, pair, 0.0).astype(LOW)
        key_pad[1, rows] = jnp.where(half, 0.0, pltpu.roll(pair, HEAD_DIM, 1)).astype(LOW)
        value_turned[:, rows] = pair.T[HEAD_DIM:].astype(LOW)

        @pl.when(owner % split == lane)
        def _():
            query_pair[pl.ds(pl.multiple_of(owner // split * tokens, tokens), tokens)] = query.astype(LOW)

    project(place)

    def visit(turn, _):
        for step in range(1, steps):
            @pl.when(turn == step)
            def _():
                if step > 1:
                    ring.start(step)
                if step == steps - 1:
                    ring_up.start(0)
                    for part in bulk:
                        part.start()

        def side(way, _):
            project(place + (2 * way - 1) * turn)
            return 0

        return lax.fori_loop(0, 2, side, 0)

    lax.fori_loop(1, steps, visit, 0)
    ring.land()
    project(place + steps)

    todo = []
    for k in range(1, size):
        todo += [functools.partial(part.step, k) for part in bulk]
        if k % 2 == 0 and k // 2 < steps:
            todo.append(functools.partial(ring_up.start, k // 2))

    def pump(count):
        for _ in range(min(count, len(todo))):
            todo.pop(0)()

    scale = HEAD_DIM**-0.5
    for i in range(number * tokens // tile):
        rows = pl.ds(i * tile, tile)
        query = query_pair[rows]
        query_doc, query_place = docs_row[0:1, rows], places_row[0:1, rows]

        def pairs(j, carry):
            keys = pl.ds(pl.multiple_of(j * tile, tile), tile)
            spot = lax.broadcasted_iota(jnp.int32, (tile, tile), 0) + j * tile
            allowed = (spot <= query_place) & (docs_col[keys] == query_doc)
            found = []
            for h in range(GROUP):
                peak, total, gathered = carry[3 * h : 3 * h + 3]
                score = jnp.where(allowed, dot_nt(key_pad[h, keys], query) * scale, NEG_BIG)
                higher = jnp.maximum(peak, jnp.max(score, axis=0, keepdims=True))
                keep = jnp.exp(peak - higher)
                prob = jnp.exp(score - higher)
                total = total * keep + jnp.sum(prob, axis=0, keepdims=True)
                gathered = gathered * keep + dot_nn(value_turned[:, keys], prob.astype(LOW))
                found += [higher, total, gathered]
            return tuple(found)

        empty = (
            jnp.full((1, tile), NEG_BIG, WIDE), jnp.zeros((1, tile), WIDE), jnp.zeros((HEAD_DIM, tile), WIDE)
        )
        found = lax.fori_loop(0, min(size * tokens // tile, (i + 1) * split), pairs, empty * GROUP)
        for h in range(GROUP):
            log_total[h : h + 1, rows] = found[3 * h] + jnp.log(found[3 * h + 1])
        result = jnp.concatenate([found[3 * h + 2] / found[3 * h + 1] for h in range(GROUP)], axis=0).T
        out_pair[rows] = result
        blocks = tile // tokens
        head_out[pl.ds(i * blocks, blocks)] = result.astype(LOW).reshape(blocks, tokens, 2 * HEAD_DIM)
        pump(3)

    def seat(index):
        return mixed.at[:, pl.ds(pl.multiple_of(index * 2 * HEAD_DIM, 2 * HEAD_DIM), 2 * HEAD_DIM)]

    swaps = []
    for k in range(1, number):
        there = (row + k) % number
        swaps.append(push(head_out.at[there], seat(row), send_x.at[k], recv_x.at[k], ctx=there * split + lane))
        swaps[-1].start()
    mine = pltpu.make_async_copy(head_out.at[row], seat(row), own.at[2])
    mine.start()
    pump(len(todo))
    for part in bulk:
        part.pass_on(size - 1)
    ring_up.land()
    for k in range(1, number):
        here = (row + number - k) % number
        push(head_out.at[here], seat(here), send_x.at[k], recv_x.at[k], ctx=here * split + lane).wait_recv()
    mine.wait()
    for part in bulk:
        part.land()
    for copy in swaps:
        copy.wait_send()
    for k in range(1, size):
        note(k).wait_send()
    ring.drain()
    ring_up.drain()
    for part in [heads] + bulk:
        part.drain()


def run_front(tokens_in, upstream, docs, cos_turned, sin_turned, pack, gu_pack, down_pack, out_rows, split, owners, small_rows,
              collective):
    size = pack.shape[0]
    tokens, width = tokens_in.shape
    length, mine = size * tokens, size * tokens // split
    tile = 2 * tokens
    dma = pltpu.SemaphoreType.DMA
    vmem = pl.BlockSpec(memory_space=pltpu.VMEM)
    anywhere = pl.BlockSpec(memory_space=pl.ANY)
    pair = 2 * HEAD_DIM
    per_unit = gu_pack.shape[1]
    shape = jax.ShapeDtypeStruct
    return pl.pallas_call(
        functools.partial(front_kernel, size, split, tile),
        out_shape=[
            shape((size, tokens, width), LOW), shape((size, tokens, width), LOW),
            shape((tokens, HEADS * HEAD_DIM), LOW), shape((mine, pair), LOW), shape((length, pair), LOW),
            shape((mine, pair), WIDE), shape((8, mine), WIDE), shape((8, mine), jnp.int32),
            shape((length, 1), jnp.int32), shape((8, mine), jnp.int32),
            shape((length, pair), WIDE), shape((length, pair), WIDE), shape((length, 1), WIDE),
            shape((width, HEAD_COLS), LOW), shape((small_rows, width), WIDE),
            shape((per_unit, owners) + gu_pack.shape[2:], LOW),
            shape((per_unit, owners) + down_pack.shape[2:], LOW),
            shape((owners,) + out_rows.shape, LOW),
        ],
        in_specs=[vmem] * 9,
        out_specs=[vmem, anywhere] + [vmem] * 13 + [anywhere] * 3,
        scratch_shapes=[
            pltpu.VMEM((size, 8, tokens), jnp.int32),
            pltpu.VMEM((owners,) + pack.shape[1:], LOW),
            pltpu.VMEM((GROUP, length, pair), LOW),
            pltpu.VMEM((HEAD_DIM, length), LOW),
            pltpu.VMEM((size // split, tokens, pair), LOW),
            dma((2, size // 2)), dma((2, size // 2)), dma((2, size // 2)), dma((2, size // 2)),
            dma((size,)), dma((size,)), dma((size // split,)), dma((size // split,)), dma((3,)),
        ] + Spread.scratch(size) * 4,
        compiler_params=pltpu.CompilerParams(
            collective_id=collective, has_side_effects=True, vmem_limit_bytes=60 << 20
        ),
        name="run_front",
    )(tokens_in, upstream, docs, cos_turned, sin_turned, pack, gu_pack, down_pack, out_rows)


class Homing:
    def __init__(self, size, grads, out, bufs, sems):
        self.size, self.grads, self.out = size, grads, out
        self.near, self.from_core, self.from_row, self.to_row, self.to_home = bufs
        self.load, self.send_a, self.recv_a, self.send_b, self.recv_b, self.send_c, self.recv_c = sems
        self.me, self.seq = lax.axis_index("ctx"), lax.axis_index("seq")

    def _block(self, s0, k):
        index = s0 * self.size + (self.me + k) % self.size
        return self.grads.at[:, index] if self.grads.ndim == 4 else self.grads.at[index]

    def _row(self, which):
        return row_mate(self.seq) if which == 0 else self.seq

    def fetch(self, which, k):
        return pltpu.make_async_copy(self._block(self._row(which), k), self.near.at[which, k], self.load.at[which, k])

    def to_core(self, which, k):
        return push(
            self._block(core_mate(self._row(which)), k), self.from_core.at[which, k],
            self.send_a.at[which, k], self.recv_a.at[which, k], seq=core_mate(self.seq),
        )

    def across(self, k):
        return push(
            self.to_row.at[k], self.from_row.at[k], self.send_b.at[k], self.recv_b.at[k], seq=row_mate(self.seq)
        )

    def homeward(self, k):
        there = (self.me + k) % self.size
        return push(self.to_home.at[k], self.out.at[self.me], self.send_c.at[k], self.recv_c.at[k], ctx=there)

    def arriving(self, k):
        here = (self.me + self.size - k) % self.size
        return push(self.to_home.at[k], self.out.at[here], self.send_c.at[k], self.recv_c.at[k], ctx=here)

    def start(self):
        def body(k, _):
            for which in range(2):
                self.to_core(which, k).start()
                self.fetch(which, k).start()
            return 0

        lax.fori_loop(0, self.size, body, 0)

    def first(self, k):
        self.fetch(0, k).wait()
        self.to_core(0, k).wait_recv()
        sum_into(self.to_row.at[k], [self.near.at[0, k], self.from_core.at[0, k]])
        self.across(k).start()

    def second(self, k, home=False):
        self.fetch(1, k).wait()
        self.to_core(1, k).wait_recv()
        self.across(k).wait_recv()
        target = self.out.at[self.me] if home else self.to_home.at[k]
        sum_into(target, [self.near.at[1, k], self.from_core.at[1, k], self.from_row.at[k]])
        if not home:
            self.homeward(k).start()

    def close(self):
        def body(k, _):
            self.arriving(k).wait_recv()
            self.homeward(k).wait_send()
            return 0

        lax.fori_loop(1, self.size, body, 0)

        def drain(k, _):
            self.to_core(0, k).wait_send()
            self.to_core(1, k).wait_send()
            self.across(k).wait_send()
            return 0

        lax.fori_loop(0, self.size, drain, 0)

    @staticmethod
    def scratch(size, block):
        slab = (size,) + block
        dma = pltpu.SemaphoreType.DMA
        return [
            pltpu.VMEM((2,) + slab, LOW), pltpu.VMEM((2,) + slab, LOW), pltpu.VMEM(slab, LOW),
            pltpu.VMEM(slab, LOW), pltpu.VMEM(slab, LOW),
            dma((2, size)), dma((2, size)), dma((2, size)), dma((size,)), dma((size,)), dma((size,)), dma((size,)),
        ]


class SmallSum:
    def __init__(self, size, small, out, from_seq, total, from_ctx, sems):
        self.size, self.small, self.out = size, small, out
        self.from_seq, self.total, self.from_ctx = from_seq, total, from_ctx
        self.send_a, self.recv_a, self.send_b, self.recv_b = sems
        self.me, self.seq = lax.axis_index("ctx"), lax.axis_index("seq")

    def _swap(self, k):
        there = (self.seq + k) % 4
        return push(self.small.at[there], self.from_seq.at[k], self.send_a.at[k], self.recv_a.at[k], seq=there)

    def _tell(self, k):
        there = (self.me + k) % self.size
        return push(self.total, self.from_ctx.at[self.me], self.send_b.at[k], self.recv_b.at[k], ctx=there)

    def _hear(self, k):
        here = (self.me + self.size - k) % self.size
        return push(self.total, self.from_ctx.at[here], self.send_b.at[k], self.recv_b.at[k], ctx=here)

    def start(self):
        for k in range(1, 4):
            self._swap(k).start()

    def middle(self):
        for k in range(1, 4):
            self._swap(k).wait_recv()
        self.total[...] = self.small[self.seq] + self.from_seq[1] + self.from_seq[2] + self.from_seq[3]
        for k in range(1, self.size):
            self._tell(k).start()

    def finish(self):
        total = self.total[...]
        for k in range(1, self.size):
            self._hear(k).wait_recv()
            total = total + self.from_ctx[(self.me + self.size - k) % self.size]
        self.out[...] = total
        for k in range(1, 4):
            self._swap(k).wait_send()
        for k in range(1, self.size):
            self._tell(k).wait_send()

    @staticmethod
    def scratch(size, rows, lanes):
        dma = pltpu.SemaphoreType.DMA
        part = (rows, lanes // 4)
        return [
            pltpu.VMEM((4,) + part, WIDE), pltpu.VMEM(part, WIDE), pltpu.VMEM((size,) + part, WIDE),
            dma((4,)), dma((4,)), dma((size,)), dma((size,)),
        ]


def back_kernel(
    size, split, tile,
    mixed_grad, gu_grads, down_grads, out_grads, small, query_pair, key_value, out_pair, log_total,
    docs_row, docs_col, places_row, cosine, sine, gain, inputs_all, row_scale, head_weight,
    attend_sum, gu_home, down_home, out_home, head_home, small_home,
    head_grad, key_pad, value_pad, key_acc, value_acc, query_acc, heads_grad, heads_turned, head_part, small_full,
    attend_own, held, send_r, recv_r, send_x, recv_x, own_x, *scratch,
):
    me, seq = lax.axis_index("ctx"), lax.axis_index("seq")
    lane, row, number = me % split, me // split, size // split
    tokens = mixed_grad.shape[1]
    length, width = inputs_all.shape
    greet(
        [{"ctx": (me + k) % size} for k in range(1, size)]
        + [{"seq": (seq + k) % 4} for k in range(1, 4)]
    )

    def homing(i, grads, out):
        part = scratch[12 * i : 12 * i + 12]
        return Homing(size, grads, out, part[:5], part[5:])

    early = [homing(0, gu_grads, gu_home), homing(1, down_grads, down_home), homing(2, out_grads, out_home)]
    late = homing(3, head_part, head_home)
    tail = scratch[48:]
    total_small = SmallSum(size, small_full, small_home, tail[0], tail[1], tail[2], tail[3:])

    mine = pltpu.make_async_copy(mixed_grad.at[row], head_grad.at[row], own_x)
    mine.start()
    swaps = []
    for k in range(1, number):
        there = (row + k) % number
        swaps.append(
            push(mixed_grad.at[there], head_grad.at[row], send_x.at[k], recv_x.at[k], ctx=there * split + lane)
        )
        swaps[-1].start()
    for home in early:
        home.start()

    steps = []
    for k in range(size):
        steps += [functools.partial(home.first, k) for home in early]
    for k in range(1, size):
        steps += [functools.partial(home.second, k) for home in early]
    steps += [functools.partial(home.second, 0, True) for home in early]

    def pump(count):
        for _ in range(min(count, len(steps))):
            steps.pop(0)()

    half = lax.broadcasted_iota(jnp.int32, (tile, 2 * HEAD_DIM), 1) < HEAD_DIM
    zero = jnp.zeros((tile, 2 * HEAD_DIM), WIDE)

    def prepare(i, _):
        rows = pl.ds(pl.multiple_of(i * tile, tile), tile)
        pair = key_value[rows].astype(WIDE)
        turned = pltpu.roll(pair, HEAD_DIM, 1)
        key_pad[0, rows] = jnp.where(half, pair, zero).astype(LOW)
        key_pad[1, rows] = jnp.where(half, zero, turned).astype(LOW)
        value_pad[0, rows] = jnp.where(half, turned, zero).astype(LOW)
        value_pad[1, rows] = jnp.where(half, zero, pair).astype(LOW)
        key_acc[rows] = zero
        value_acc[rows] = zero
        heads_grad[rows, pl.ds(0, 2 * HEAD_DIM)] = zero.astype(LOW)
        return 0

    lax.fori_loop(0, length // tile, prepare, 0)
    for k in range(1, number):
        here = (row + number - k) % number
        push(mixed_grad.at[here], head_grad.at[here], send_x.at[k], recv_x.at[k], ctx=here * split + lane).wait_recv()
    mine.wait()

    scale = HEAD_DIM**-0.5
    blocks = tile // tokens
    for i in range(number * tokens // tile):
        rows = pl.ds(i * tile, tile)
        query = query_pair[rows]
        grad = head_grad[pl.ds(i * blocks, blocks)].reshape(tile, 2 * HEAD_DIM)
        product = (grad.astype(WIDE) * out_pair[rows].astype(WIDE)).T
        deltas = [
            jnp.sum(product[h * HEAD_DIM : (h + 1) * HEAD_DIM], axis=0, keepdims=True) for h in range(GROUP)
        ]
        query_doc, query_place = docs_row[0:1, rows], places_row[0:1, rows]
        totals = [log_total[h : h + 1, rows] for h in range(GROUP)]
        query_acc[...] = zero

        def pairs(j, _):
            keys = pl.ds(pl.multiple_of(j * tile, tile), tile)
            place = lax.broadcasted_iota(jnp.int32, (tile, tile), 0) + j * tile
            allowed = (place <= query_place) & (docs_col[keys] == query_doc)
            key_part, value_part, query_part = zero, zero, zero
            for h in range(GROUP):
                mine_half = half if h == 0 else jnp.logical_not(half)
                score = dot_nt(key_pad[h, keys], query)
                prob = jnp.where(allowed, jnp.exp(score * scale - totals[h]), 0.0)
                slope = dot_nt(value_pad[h, keys], grad)
                ds = (prob * (slope - deltas[h])).astype(LOW)
                value_part = jnp.where(mine_half, dot_nn(prob.astype(LOW), grad), value_part)
                key_part = jnp.where(mine_half, dot_nn(ds, query), key_part)
                query_part = query_part + dot_tn(ds, key_pad[h, keys])
            key_acc[keys] += key_part
            value_acc[keys] += value_part
            query_acc[...] += query_part
            return 0

        lax.fori_loop(0, min(length // tile, (i + 1) * split), pairs, 0)
        turn = query_acc[...] * scale
        for b in range(blocks):
            at = pl.ds(pl.multiple_of(((i * blocks + b) * split + lane) * tokens, tokens), tokens)
            piece = turn[b * tokens : (b + 1) * tokens]
            heads_grad[at, pl.ds(0, 2 * HEAD_DIM)] = unturn(piece, cosine, sine, at, 0).astype(LOW)
        pump(9)

    def fold(i, _):
        rows = pl.ds(pl.multiple_of(i * tile, tile), tile)
        key_part, value_part = key_acc[rows], value_acc[rows]
        key_part = (key_part + pltpu.roll(key_part, HEAD_DIM, 1)) * scale
        value_part = value_part + pltpu.roll(value_part, HEAD_DIM, 1)
        both = jnp.where(half, key_part, value_part)
        heads_grad[rows, pl.ds(2 * HEAD_DIM, 2 * HEAD_DIM)] = unturn(both, cosine, sine, rows, 1).astype(LOW)
        return 0

    lax.fori_loop(0, length // tile, fold, 0)

    def transpose(i, _):
        rows = pl.ds(pl.multiple_of(i * tile, tile), tile)
        heads_turned[:, rows] = heads_grad[rows].astype(WIDE).T.astype(LOW)
        return 0

    lax.fori_loop(0, length // tile, transpose, 0)

    reduce = RingReduce(size, held, send_r, recv_r)
    small_full[...] = small[...]
    gain_row = small.shape[1] - 8

    def attend(place, slot):
        owner = ring_member(place, size)
        rows = pl.ds(pl.multiple_of(owner * tokens, tokens), tokens)
        part = dot_nt(heads_grad[rows], head_weight[...])
        attend_own[slot] = part.astype(LOW)
        normed = inputs_all[rows].astype(WIDE) * row_scale[rows]
        share = jnp.sum(part * normed, axis=0, keepdims=True)
        lanes = width // 4
        for s0 in range(4):
            small_full[s0, gain_row : gain_row + 1] += share[:, s0 * lanes : (s0 + 1) * lanes]

    place = ring_place(me, size)
    half_ring = size // 2
    attend(place + half_ring, 0)
    reduce.start(0, [attend_own.at[0]] * 2)
    for step in range(1, half_ring):
        attend(place + half_ring - step, 1)
        attend(place - half_ring + step, 2)
        if step == 1:
            def columns(j, _):
                cols = pl.ds(pl.multiple_of(j * tile, tile), tile)
                normed = inputs_all[:, cols].astype(WIDE) * row_scale[...]
                part = dot_nn(heads_turned[...], (normed * gain[gain.shape[0] - 8 : gain.shape[0] - 7, cols]).astype(LOW)).T.astype(LOW)
                depth = head_part.shape[1]
                head_part[pl.ds(j * (tile // depth), tile // depth)] = part.reshape(tile // depth, depth, HEAD_COLS)
                return 0

            lax.fori_loop(0, width // tile, columns, 0)
            late.start()
        reduce.start(step, [attend_own.at[1], attend_own.at[2]])
        pump(6)
    attend(place, 1)
    total_small.start()
    pump(len(steps))
    for k in range(size):
        late.first(k)
    total_small.middle()
    for k in range(1, size):
        late.second(k)
    late.second(0, True)
    reduce.finish(attend_sum, attend_own.at[1], attend_own.at[0])
    for home in early:
        home.close()
    late.close()
    total_small.finish()
    for copy in swaps:
        copy.wait_send()


def swap_halves(values):
    lane = lax.broadcasted_iota(jnp.int32, values.shape, 1) % HEAD_DIM
    return jnp.where(
        lane < HEAD_DIM // 2,
        pltpu.roll(values, values.shape[1] - HEAD_DIM // 2, 1),
        pltpu.roll(values, HEAD_DIM // 2, 1),
    )


def unturn(values, cosine, sine, rows, which):
    cos, sin = cosine[rows], sine[rows]
    if which:
        half = lax.broadcasted_iota(jnp.int32, values.shape, 1) < HEAD_DIM
        cos, sin = jnp.where(half, cos, 1.0), jnp.where(half, sin, 0.0)
    return values * cos - swap_halves(values) * sin


def attention_back(arrays, size, split, collective):
    (mixed_grad, gu_grads, down_grads, out_grads, small, query_pair, key_value, out_pair, log_total,
     docs_row, docs_col, places_row, cosine, sine, gain, inputs_all, row_scale, head_weight) = arrays
    tokens = mixed_grad.shape[1]
    length, width = inputs_all.shape
    tile = 2 * tokens
    blocks = [
        (gu_grads.shape[0],) + gu_grads.shape[2:], (down_grads.shape[0],) + down_grads.shape[2:],
        out_grads.shape[1:], (out_grads.shape[1], HEAD_COLS),
    ]
    small_rows = small.shape[1]
    dma = pltpu.SemaphoreType.DMA
    vmem = pl.BlockSpec(memory_space=pltpu.VMEM)
    anywhere = pl.BlockSpec(memory_space=pl.ANY)
    pair = (length, 2 * HEAD_DIM)
    scratch = [
        pltpu.VMEM(mixed_grad.shape, LOW),
        pltpu.VMEM((GROUP,) + pair, LOW), pltpu.VMEM((GROUP,) + pair, LOW),
        pltpu.VMEM(pair, WIDE), pltpu.VMEM(pair, WIDE), pltpu.VMEM((tile, 2 * HEAD_DIM), WIDE),
        pltpu.VMEM((length, HEAD_COLS), LOW), pltpu.VMEM((HEAD_COLS, length), LOW),
        pltpu.VMEM((4 * size, out_grads.shape[1], HEAD_COLS), LOW),
        pltpu.VMEM(small.shape, WIDE),
        pltpu.VMEM((3, tokens, width), LOW), pltpu.VMEM((2, size // 2, tokens, width), LOW),
        dma((2, size // 2)), dma((2, size // 2)), dma((size // split,)), dma((size // split,)), dma,
    ]
    for block in blocks:
        scratch += Homing.scratch(size, block)
    scratch += SmallSum.scratch(size, small_rows, width)
    return pl.pallas_call(
        functools.partial(back_kernel, size, split, tile),
        out_shape=[jax.ShapeDtypeStruct((tokens, width), WIDE)]
        + [jax.ShapeDtypeStruct((size,) + block, LOW) for block in blocks]
        + [jax.ShapeDtypeStruct((small_rows, width // 4), WIDE)],
        in_specs=[vmem, anywhere, anywhere, anywhere] + [vmem] * 14,
        out_specs=[vmem] * 6,
        scratch_shapes=scratch,
        compiler_params=pltpu.CompilerParams(
            collective_id=collective, has_side_effects=True, vmem_limit_bytes=62 << 20
        ),
        name="attention_back",
    )(*arrays)


def rms_scale(values):
    return lax.rsqrt(jnp.mean(values * values, axis=-1, keepdims=True) + NORM_EPS)


def rope_tables(places, factor):
    freqs = 1.0 / ROPE_BASE ** (jnp.arange(0, HEAD_DIM, 2).astype(WIDE) / HEAD_DIM)
    angles = (places.astype(WIDE) / factor)[None, :] * freqs[:, None]
    return jnp.cos(angles), jnp.sin(angles)


def dot(equation, left, right):
    return jnp.einsum(equation, left, right, preferred_element_type=WIDE)


def on_device(
    layer_input, document_ids, expert_routes, rope_factor, attention_gain, feedforward_gain,
    query_weight, key_weight, value_weight, output_weight, router_weight, gate_up, down_weight, cotangent,
):
    nseq, nctx = lax.axis_size("seq"), lax.axis_size("ctx")
    tokens, width = layer_input.shape[1:]
    length = tokens * nctx
    rows, experts, ff2 = gate_up.shape
    ff = ff2 // 2
    down_rows = down_weight.shape[0]
    per_unit = max(1, experts // nctx)
    ff_split = max(1, nctx // experts)
    ff_part = ff // ff_split
    head_split = nctx // KV_HEADS
    unit = lax.axis_index("ctx")
    owners = nseq * nctx

    if ff_split == 1:
        gu_pack = gate_up.astype(LOW).transpose(1, 0, 2).reshape(nctx, per_unit, rows, ff2)
    else:
        gu_pack = (
            gate_up.astype(LOW).reshape(rows, experts, 2, ff_split, ff_part).transpose(1, 3, 0, 2, 4)
            .reshape(nctx, per_unit, rows, 2 * ff_part)
        )
    down_pack = jnp.repeat(
        down_weight.astype(LOW).transpose(1, 0, 2), ff_split, axis=0
    ).reshape(nctx, per_unit, down_rows, width)
    head_pack = jnp.concatenate(
        [
            query_weight.reshape(rows, KV_HEADS, GROUP * HEAD_DIM),
            key_weight.reshape(rows, KV_HEADS, HEAD_DIM),
            value_weight.reshape(rows, KV_HEADS, HEAD_DIM),
        ],
        axis=-1,
    ).astype(LOW).transpose(1, 0, 2)
    head_pack = jnp.repeat(head_pack, head_split, axis=0)
    small_rows = experts + 8
    small_pack = jnp.concatenate(
        [router_weight, attention_gain[:, None], feedforward_gain[:, None], jnp.zeros((rows, 110 + 16 - experts), WIDE)],
        axis=1,
    ).astype(LOW)
    small_pack = jnp.broadcast_to(small_pack[None], (nctx,) + small_pack.shape)
    pack = jnp.concatenate([head_pack, small_pack], axis=2)
    documents = jnp.broadcast_to(document_ids.reshape(1, tokens), (8, tokens))
    cos_turned, sin_turned = rope_tables(jnp.arange(length, dtype=jnp.int32), rope_factor[0])

    (inputs_all, upstream_all, mixed_low, query_pair, key_value, out_pair, log_total, docs_row, docs_col, places_row,
     cosine, sine, row_scale, head_full, small_full, gu_full, down_full, out_full) = run_front(
        layer_input[0], cotangent[0], documents, cos_turned, sin_turned, pack, gu_pack, down_pack,
        output_weight.astype(LOW), head_split, owners, small_rows, 1,
    )
    gu_full = gu_full.reshape(per_unit, width, 2 * ff_part)
    down_full = down_full.reshape(per_unit, ff, width)
    if ff_split > 1:
        down_full = lax.dynamic_slice_in_dim(down_full, (unit % ff_split) * ff_part, ff_part, 1)
    out_full = out_full.reshape(HEADS * HEAD_DIM, width)
    router_full = small_full[:experts].astype(LOW)
    gain_one, gain_two = small_full[experts], small_full[experts + 1]

    inputs = layer_input[0].astype(WIDE)
    middle = inputs + dot("tj,jd->td", mixed_low, out_full)
    scale_two = rms_scale(middle)
    normed_two = middle * scale_two
    expert_input = (normed_two * gain_two).astype(LOW)
    logits = dot("td,ed->te", expert_input, router_full)
    chosen = jnp.any(
        expert_routes[0][:, :, None] == jnp.arange(experts, dtype=jnp.int32)[None, None, :], axis=1
    )
    picked = jnp.where(chosen, logits, NEG_BIG)
    expo_gate = jnp.where(chosen, jnp.exp(picked - jnp.max(picked, axis=-1, keepdims=True)), 0.0)
    combine = expo_gate / jnp.sum(expo_gate, axis=-1, keepdims=True)

    mix, back_sum, gate_grad_all, gu_grads, down_grads = run_experts(
        expert_input, combine.T, upstream_all, gu_full, down_full, nctx, ff_split, owners, down_rows, 3
    )

    layer_output = (middle + mix).astype(LOW)[None]
    upstream = cotangent[0].astype(WIDE)
    gate_grad = gate_grad_all[:, :per_unit].reshape(experts, ff_split, tokens).sum(axis=1).T
    gate_grad = jnp.where(chosen, gate_grad, 0.0)
    select_grad = combine * (gate_grad - jnp.sum(combine * gate_grad, axis=-1, keepdims=True))
    logit_grad = select_grad.astype(LOW)
    back_two = back_sum + dot("te,ed->td", logit_grad, router_full)
    router_part = dot("te,td->ed", logit_grad, expert_input)
    gain_two_part = jnp.sum(back_two * normed_two, axis=0)
    normed_two_grad = back_two * gain_two
    middle_grad = upstream + scale_two * (
        normed_two_grad - normed_two * jnp.mean(normed_two_grad * normed_two, axis=-1, keepdims=True)
    )
    project_grad = middle_grad.astype(LOW)
    out_grad_part = dot("tj,td->jd", mixed_low, project_grad)
    mixed_grad = dot("td,jd->tj", project_grad, out_full).astype(LOW)
    mixed_grad = mixed_grad.reshape(tokens, KV_HEADS, GROUP * HEAD_DIM).transpose(1, 0, 2)

    small_grads = jnp.concatenate(
        [router_part, gain_two_part[None], jnp.zeros((31 - experts, width), WIDE)], axis=0
    ).reshape(32, nseq, width // nseq).transpose(1, 0, 2)
    if ff_split > 1:
        down_grads = lax.dynamic_update_slice_in_dim(
            jnp.zeros((per_unit, owners, down_rows, width), LOW), down_grads,
            (unit % ff_split) * (ff_part // down_rows), 1,
        )
    attend_sum, gu_home, down_home, out_home, head_home, small_home = attention_back(
        [
            mixed_grad,
            gu_grads,
            down_grads,
            out_grad_part.astype(LOW).reshape(owners, rows, width),
            small_grads,
            query_pair, key_value, out_pair, log_total, docs_row, docs_col, places_row,
            cosine, sine, small_full, inputs_all.reshape(length, width), row_scale, head_full,
        ],
        nctx, head_split, 7,
    )
    gu_home, down_home = gu_home.astype(WIDE), down_home.astype(WIDE)
    out_home, head_home = out_home.astype(WIDE), head_home.astype(WIDE)
    gate_up_gradient = (
        gu_home.reshape(experts, ff_split, rows, 2, ff_part).transpose(2, 0, 3, 1, 4).reshape(rows, experts, ff2)
    )
    down_gradient = down_home.reshape(experts, ff_split, down_rows, width).sum(axis=1).transpose(1, 0, 2)
    output_gradient = out_home.sum(axis=0)
    head_home = head_home.reshape(KV_HEADS, head_split, rows, HEAD_COLS).sum(axis=1).transpose(1, 0, 2)
    query_gradient = head_home[..., : GROUP * HEAD_DIM].reshape(rows, HEADS * HEAD_DIM)
    key_gradient = head_home[..., GROUP * HEAD_DIM : -HEAD_DIM].reshape(rows, KV_HEADS * HEAD_DIM)
    value_gradient = head_home[..., -HEAD_DIM:].reshape(rows, KV_HEADS * HEAD_DIM)
    small_home = lax.dynamic_slice_in_dim(small_home, unit * rows, rows, axis=1)
    router_gradient = small_home[:experts].T

    scale_one = rms_scale(inputs)
    normed_one = inputs * scale_one
    normed_one_grad = attend_sum * gain_one
    input_gradient = (
        middle_grad
        + scale_one
        * (normed_one_grad - normed_one * jnp.mean(normed_one_grad * normed_one, axis=-1, keepdims=True))
    ).astype(LOW)[None]
    return (
        layer_output, input_gradient, small_home[24], small_home[experts],
        query_gradient, key_gradient, value_gradient, output_gradient, router_gradient,
        gate_up_gradient, down_gradient,
    )


def solution(mesh):
    both = ("seq", "ctx")
    return jax.shard_map(
        on_device,
        mesh=mesh,
        in_specs=(
            P("seq", "ctx", None), P("seq", "ctx"), P("seq", "ctx", None), P(), P(both), P(both),
            P(both, None), P(both, None), P(both, None), P(both, None), P(both, None),
            P(both, None, None), P(both, None, None), P("seq", "ctx", None),
        ),
        out_specs=(
            P("seq", "ctx", None), P("seq", "ctx", None), P(both), P(both),
            P(both, None), P(both, None), P(both, None), P(both, None), P(both, None),
            P(both, None, None), P(both, None, None),
        ),
        check_vma=False,
    )
```

```python
import functools
import math

import jax
import jax.numpy as jnp
from jax import lax
from jax.experimental import pallas as pl
from jax.experimental.pallas import tpu as pltpu
from jax.sharding import PartitionSpec as P

HEADS = 16
KV_HEADS = 8
HEAD_DIM = 64
GROUP = HEADS // KV_HEADS
HEAD_COLS = (GROUP + 2) * HEAD_DIM

NORM_EPS = 1e-06
ROPE_BASE = 10000.0
NEG_BIG = -1e30
LOW = jnp.bfloat16
WIDE = jnp.float32
MESH = pl.DeviceIdType.MESH


def ring_place(index, size):
    half = index // 2
    return half + (index % 2) * (size - 1 - 2 * half)


def ring_member(place, size):
    place = (place + 2 * size) % size
    far = place // (size // 2)
    return 2 * place + far * (2 * size - 1 - 4 * place)


def slot_of(distance, size):
    if distance == 0:
        return 0
    if abs(distance) == size // 2:
        return 1
    return 2 * abs(distance) + (distance > 0)


def slot_seen(owner, viewer, size):
    half = size // 2
    ahead = (ring_place(owner, size) - ring_place(viewer, size) + 2 * size) % size
    far = ahead // half
    plain = (2 * ahead + 1) * (1 - far) + 2 * (size - ahead) * far
    same = (size - ahead) // size
    opposite = (size - (ahead + half) % size) // size
    return plain - same - (size - 1) * opposite


def core_mate(index):
    return index + 1 - 2 * (index % 2)


def row_mate(index):
    return (index + 2) % 4


def push(src, dst, send, recv, **where):
    return pltpu.make_async_remote_copy(
        src_ref=src, dst_ref=dst, send_sem=send, recv_sem=recv, device_id=where, device_id_type=MESH
    )


def greet(peers):
    barrier = pltpu.get_barrier_semaphore()
    for where in peers:
        pl.semaphore_signal(barrier, inc=1, device_id=where, device_id_type=MESH)
    pl.semaphore_wait(barrier, len(peers))


def ring_peers(size):
    place = ring_place(lax.axis_index("ctx"), size)
    return ring_member(place + 1, size), ring_member(place - 1, size)


class RingGather:
    def __init__(self, size, source, target, send, recv, relative=False):
        self.size, self.source, self.target, self.send, self.recv = size, source, target, send, recv
        self.relative = relative
        self.place = ring_place(lax.axis_index("ctx"), size)
        self.right, self.left = ring_peers(size)
        self.steps = size // 2

    def _copy(self, way, step, arriving):
        sign = 2 * way - 1
        rows = self.source.shape[0]
        part = pl.ds(way * (rows // 2), rows // 2) if step == self.steps - 1 else pl.ds(0, rows)
        if self.relative:
            here, there = slot_of(sign * step, self.size), slot_of(sign * (step + 1), self.size)
        else:
            here = there = ring_member(self.place + sign * (step + arriving), self.size)
        dst = self.target.at[there, part]
        src = self.target.at[here, part] if step else self.source.at[part]
        where = self.left if way else self.right
        return push(dst if arriving else src, dst, self.send.at[way, step], self.recv.at[way, step], ctx=where)

    def start(self, step):
        for way in range(2):
            if step:
                self._copy(way, step - 1, 1).wait_recv()
            self._copy(way, step, 0).start()

    def land(self):
        for way in range(2):
            self._copy(way, self.steps - 1, 1).wait_recv()

    def drain(self):
        for way in range(2):
            for step in range(self.steps):
                self._copy(way, step, 0).wait_send()

    def finish(self):
        self.land()
        self.drain()


class LineGather:
    def __init__(self, size, source, slab, sems):
        self.source, self.slab, self.count = source, slab, size // 2
        self.send, self.recv, self.send_m, self.recv_m = sems
        self.me = lax.axis_index("ctx")
        self.spot, self.side = self.me // 2, self.me % 2
        self.mate = core_mate(self.me)

    def _line(self, way, step):
        owner = self.me - 2 * step if way == 0 else self.me + 2 * step
        there = self.me + 2 if way == 0 else self.me - 2
        source = self.slab(owner, self.me) if step else self.source
        return push(source, self.slab(owner, there), self.send.at[way, step], self.recv.at[way, step], ctx=there)

    def _arriving(self, way, step):
        owner = self.me - 2 * step - 2 if way == 0 else self.me + 2 * step + 2
        here = self.slab(owner, self.me)
        return push(here, here, self.send.at[way, step], self.recv.at[way, step], ctx=self.mate)

    def _across(self, spot, own=False):
        owner = 2 * spot + self.side
        source = self.source if own else self.slab(owner, self.me)
        return push(
            source, self.slab(owner, self.mate), self.send_m.at[spot], self.recv_m.at[spot], ctx=self.mate
        )

    def _sends(self, way, step):
        if way == 0:
            return (self.spot + 1 < self.count) & (self.spot >= step)
        return (self.spot >= 1) & (self.spot + step < self.count)

    def start(self):
        for way in range(2):
            pl.when(self._sends(way, 0))(self._line(way, 0).start)
        self._across(self.spot, True).start()

    def turn(self, step):
        for way in range(2):
            there = self.spot >= step if way == 0 else self.spot + step < self.count

            @pl.when(there)
            def _():
                self._arriving(way, step - 1).wait_recv()
                self._across(self.spot - step if way == 0 else self.spot + step).start()

            pl.when(self._sends(way, step))(self._line(way, step).start)

    def finish(self):
        for spot in range(self.count):
            owner = 2 * spot + 1 - self.side
            here = self.slab(owner, self.me)
            push(here, here, self.send_m.at[spot], self.recv_m.at[spot], ctx=self.mate).wait_recv()

    def drain(self):
        for spot in range(self.count):
            self._across(spot).wait_send()
        for way in range(2):
            for step in range(self.count - 1):
                pl.when(self._sends(way, step))(self._line(way, step).wait_send)

    @staticmethod
    def scratch(size):
        dma, count = pltpu.SemaphoreType.DMA, size // 2
        return [dma((2, count)), dma((2, count)), dma((count,)), dma((count,))]


def row_step(rows):
    return rows if rows < 16 else 16


def sum_into(target, parts):
    rows = target.shape[-2]
    step = row_step(rows)

    def add_at(lead):
        def body(r, _):
            at = lead + (pl.ds(pl.multiple_of(r * step, step), step),)
            total = parts[0][at].astype(WIDE)
            for part in parts[1:]:
                total = total + part[at].astype(WIDE)
            target[at] = total.astype(target.dtype)
            return 0

        lax.fori_loop(0, rows // step, body, 0)

    for lead in [()] if target.ndim == 2 else [(u,) for u in range(target.shape[0])]:
        add_at(lead)


def dot_nn(a, b):
    return lax.dot_general(a, b, (((1,), (0,)), ((), ())), preferred_element_type=WIDE)


def dot_nt(a, b):
    return lax.dot_general(a, b, (((1,), (1,)), ((), ())), preferred_element_type=WIDE)


def dot_tn(a, b):
    return lax.dot_general(a, b, (((0,), (0,)), ((), ())), preferred_element_type=WIDE)


class RingReduce:
    def __init__(self, size, held, send, recv):
        self.size, self.held, self.send, self.recv = size, held, send, recv
        self.place = ring_place(lax.axis_index("ctx"), size)
        self.right, self.left = ring_peers(size)
        self.steps = size // 2
        self.rows = held.shape[2]

    def owner(self, way, step):
        ahead = self.steps - step
        return ring_member(self.place + ahead if way == 0 else self.place - ahead, self.size)

    def _copy(self, way, step, source):
        half = self.rows // 2
        part = pl.ds(0, self.rows) if step else pl.ds(half * way, half)
        where = self.right if way == 0 else self.left
        return push(
            source, self.held.at[way, step, part], self.send.at[way, step], self.recv.at[way, step], ctx=where
        )

    def start(self, step, own):
        for way in range(2):
            half = self.rows // 2
            near = pl.ds(0, half) if way == 0 else pl.ds(half, half)
            far = pl.ds(half, half) if way == 0 else pl.ds(0, half)
            source = own[way].at[near]
            if step:
                self._copy(way, step - 1, source).wait_recv()
                source = self.held.at[way, step - 1]
                if step == 1:
                    sum_into(source.at[near], [own[way].at[near], source.at[near]])
                    sum_into(source.at[far], [own[way].at[far]])
                else:
                    sum_into(source, [own[way], source])
            self._copy(way, step, source).start()

    def finish(self, target, own, first):
        last, half = self.steps - 1, self.rows // 2
        for way in range(2):
            self._copy(way, last, self.held.at[way, last]).wait_recv()
        sum_into(target, [own, self.held.at[0, last], self.held.at[1, last]])
        for way in range(2):
            for step in range(self.steps):
                source = self.held.at[way, step - 1] if step else first.at[pl.ds(half * way, half)]
                self._copy(way, step, source).wait_send()


def expert_kernel(
    size, split,
    expert_input, combine_rows, upstream, gu_hbm, down_hbm,
    mix, back_sum, gate_home, gu_grads, down_grads,
    tokens_all, combine_all, gu_weight, down_weight, combine_cols, gate_up, hidden, both_grad, out_acc, out_own,
    back_own, gate_send, held_out, held_back,
    send_b, recv_b, send_c, recv_c, send_y, recv_y, send_d, recv_d, send_g, recv_g, own_sem,
):
    me = lax.axis_index("ctx")
    place = ring_place(me, size)
    per_unit, width, ff2 = gu_weight.shape
    ff = ff2 // 2
    tokens = expert_input.shape[0]
    group = 2 * tokens
    groups = size // 2
    first_expert = me // split * per_unit
    greet([{"ctx": (me + k) % size} for k in range(1, size)])

    loads = [
        pltpu.make_async_copy(expert_input, tokens_all.at[0], own_sem.at[0]),
        pltpu.make_async_copy(combine_rows, combine_all.at[0], own_sem.at[1]),
        pltpu.make_async_copy(gu_hbm, gu_weight, own_sem.at[2]),
        pltpu.make_async_copy(down_hbm, down_weight, own_sem.at[3]),
    ]
    rings = [
        RingGather(size, combine_rows, combine_all, send_c, recv_c, True),
        RingGather(size, expert_input, tokens_all, send_b, recv_b, True),
    ]
    for ring in rings:
        ring.start(0)
    for load in loads:
        load.start()
    for load in loads:
        load.wait()
    lanes = lax.broadcasted_iota(jnp.int32, (group, 128), 1)

    def forward(turn, _):
        for step in range(1, groups):
            @pl.when(turn == step - 1)
            def _():
                for ring in rings:
                    ring.start(step)

        @pl.when(turn == groups - 1)
        def _():
            for ring in rings:
                ring.land()

        g = (turn + 1) % groups
        pair = pl.ds(2 * g, 2)
        rows = pl.ds(pl.multiple_of(g * group, group), group)
        token = tokens_all[pair].reshape(group, width)
        up_wide = upstream[pair].reshape(group, width).astype(WIDE)
        weights = jnp.concatenate([combine_all[2 * g].T, combine_all[2 * g + 1].T], axis=0)
        names = lax.broadcasted_iota(jnp.int32, weights.shape, 1)
        out_acc[...] = jnp.zeros_like(out_acc)

        def one(e, gates):
            weight = jnp.sum(jnp.where(names == first_expert + e, weights, 0.0), axis=1, keepdims=True)
            combine_cols[e, rows] = jnp.broadcast_to(weight, (group, 128))
            both = dot_nn(token, gu_weight[e])
            gate_up[e, rows] = both.astype(gate_up.dtype)
            gate, up = both[:, :ff], both[:, ff:]
            hid = (gate / (1.0 + jnp.exp(-gate)) * up).astype(LOW)
            hidden[e, rows] = hid
            produced = dot_nn(hid, down_weight[e])
            out_acc[...] += weight * produced
            dg = jnp.sum(up_wide * produced, axis=1, keepdims=True)
            return jnp.where(lanes == e, dg, gates)

        gates = lax.fori_loop(0, per_unit, one, jnp.zeros((group, 128), WIDE)).T
        gate_send[2 * g] = gates[:8, :tokens]
        gate_send[2 * g + 1] = gates[:8, tokens:]
        out_own[pair] = out_acc[...].astype(LOW).reshape(2, tokens, width)
        return 0

    lax.fori_loop(0, groups, forward, 0)

    def gate_copy(distance):
        there = ring_member(place + distance, size)
        k = distance % size
        return push(gate_send.at[slot_of(distance, size)], gate_home.at[me], send_g.at[k], recv_g.at[k], ctx=there)

    distances = [d for d in range(1 - groups, groups + 1) if d]
    for distance in distances:
        gate_copy(distance).start()
    gate_home[me] = gate_send[0]

    ring_out = RingReduce(size, held_out, send_y, recv_y)
    ring_back = RingReduce(size, held_back, send_d, recv_d)

    def backward(turn, _):
        for step in range(groups):
            @pl.when(turn == step)
            def _():
                ring_out.start(
                    step, [out_own.at[slot_of(groups - step, size)], out_own.at[slot_of(step - groups, size)]]
                )

        g = (groups - turn) % groups
        pair = pl.ds(2 * g, 2)
        rows = pl.ds(pl.multiple_of(g * group, group), group)
        up_wide = upstream[pair].reshape(group, width).astype(WIDE)
        out_acc[...] = jnp.zeros_like(out_acc)

        def one(e, _):
            weight = combine_cols[e, rows][:, 0:1]
            grad = (weight * up_wide).astype(LOW)
            hid_grad = dot_nt(grad, down_weight[e])
            gate = gate_up[e, rows, pl.ds(0, ff)].astype(WIDE)
            up = gate_up[e, rows, pl.ds(ff, ff)].astype(WIDE)
            sigmoid = 1.0 / (1.0 + jnp.exp(-gate))
            gate_part = (hid_grad * up * sigmoid * (1.0 + gate * (1.0 - sigmoid))).astype(LOW)
            up_part = (hid_grad * (gate * sigmoid)).astype(LOW)
            both_grad[e, rows, pl.ds(0, ff)] = gate_part
            both_grad[e, rows, pl.ds(ff, ff)] = up_part
            out_acc[...] += dot_nt(both_grad[e, rows], gu_weight[e])
            return 0

        lax.fori_loop(0, per_unit, one, 0)
        near = 2 * ((g + groups - 1) // groups)
        back_own[pl.ds(near, 2)] = out_acc[...].astype(LOW).reshape(2, tokens, width)
        for step in range(groups):
            @pl.when(turn == step)
            def _():
                ring_back.start(step, [back_own.at[1]] * 2 if step == 0 else [back_own.at[3], back_own.at[2]])
        return 0

    lax.fori_loop(0, groups, backward, 0)

    tile = 256
    length = size * tokens

    def gu_tile(j, _):
        turned = tokens_all[:, :, pl.ds(pl.multiple_of(j * tile, tile), tile)].reshape(length, tile)
        turned = turned.astype(WIDE).T.astype(LOW)
        depth = gu_grads.shape[2]
        count = tile // depth

        def one(e, _):
            part = dot_nn(turned, both_grad[e]).reshape(count, depth, ff2)
            gu_grads[e, pl.ds(j * count, count)] = part.astype(LOW)
            return 0

        return lax.fori_loop(0, per_unit, one, 0)

    lax.fori_loop(0, width // tile, gu_tile, 0)

    def down_tile(index, _):
        e, j = index // (ff // tile), index % (ff // tile)
        turned = hidden[e, :, pl.ds(pl.multiple_of(j * tile, tile), tile)].astype(WIDE).T.astype(LOW)
        depth = down_grads.shape[2]
        count = tile // depth
        for half in range(2):
            cols = pl.ds(half * (width // 2), width // 2)
            grad = upstream[:, :, cols].reshape(length, width // 2).astype(WIDE) * combine_cols[e][:, 0:1]
            part = dot_nn(turned, grad.astype(LOW)).reshape(count, depth, width // 2)
            down_grads[e, pl.ds(j * count, count), :, cols] = part.astype(LOW)
        return 0

    lax.fori_loop(0, per_unit * (ff // tile), down_tile, 0)

    ring_back.finish(back_sum, back_own.at[0], back_own.at[1])
    ring_out.finish(mix, out_own.at[0], out_own.at[1])
    for ring in rings:
        ring.drain()
    for distance in distances:
        here = ring_member(place - distance, size)
        k = distance % size
        push(gate_send.at[0], gate_home.at[here], send_g.at[k], recv_g.at[k], ctx=here).wait_recv()
        gate_copy(distance).wait_send()


def run_experts(expert_input, combine_rows, upstream, gu_full, down_full, size, split, owners, down_rows, collective):
    tokens, width = expert_input.shape
    per_unit, _, ff2 = gu_full.shape
    ff = ff2 // 2
    length = size * tokens
    dma = pltpu.SemaphoreType.DMA
    vmem = pl.BlockSpec(memory_space=pltpu.VMEM)
    anywhere = pl.BlockSpec(memory_space=pl.ANY)
    steps = (2, size // 2)
    return pl.pallas_call(
        functools.partial(expert_kernel, size, split),
        out_shape=[
            jax.ShapeDtypeStruct((tokens, width), WIDE),
            jax.ShapeDtypeStruct((tokens, width), WIDE),
            jax.ShapeDtypeStruct((size, 8, tokens), WIDE),
            jax.ShapeDtypeStruct((per_unit, owners, width // owners, ff2), LOW),
            jax.ShapeDtypeStruct((per_unit, ff // down_rows, down_rows, width), LOW),
        ],
        in_specs=[vmem, vmem, vmem, anywhere, anywhere],
        out_specs=[vmem] * 5,
        scratch_shapes=[
            pltpu.VMEM((size, tokens, width), LOW),
            pltpu.VMEM((size,) + combine_rows.shape, WIDE),
            pltpu.VMEM(gu_full.shape, LOW),
            pltpu.VMEM(down_full.shape, LOW),
            pltpu.VMEM((per_unit, length, 128), WIDE),
            pltpu.VMEM((per_unit, length, ff2), WIDE if length <= 2048 else LOW),
            pltpu.VMEM((per_unit, length, ff), LOW),
            pltpu.VMEM((per_unit, length, ff2), LOW),
            pltpu.VMEM((2 * tokens, width), WIDE),
            pltpu.VMEM((size, tokens, width), LOW),
            pltpu.VMEM((4, tokens, width), LOW),
            pltpu.VMEM((size, 8, tokens), WIDE),
            pltpu.VMEM((2, size // 2, tokens, width), LOW),
            pltpu.VMEM((2, size // 2, tokens, width), LOW),
            dma(steps), dma(steps), dma(steps), dma(steps), dma(steps), dma(steps), dma(steps), dma(steps),
            dma((size,)), dma((size,)), dma((4,)),
        ],
        compiler_params=pltpu.CompilerParams(
            collective_id=collective, has_side_effects=True, vmem_limit_bytes=63 << 20
        ),
        name="run_experts",
    )(expert_input, combine_rows, upstream, gu_full, down_full)


class Spread:
    def __init__(self, size, source, slab, sems, gathered=False):
        self.size, self.source, self.slab, self.gathered = size, source, slab, gathered
        self.send_a, self.recv_a, self.send_b, self.recv_b, self.own = sems
        self.me, self.seq = lax.axis_index("ctx"), lax.axis_index("seq")

    def _from(self, k):
        return (self.me + self.size - k) % self.size

    def local(self):
        return pltpu.make_async_copy(self.source(self.me), self.slab(self.seq * self.size + self.me), self.own)

    def outward(self, k):
        there = (self.me + k) % self.size
        slab = self.slab(self.seq * self.size + self.me)
        return push(self.source(there), slab, self.send_a.at[k], self.recv_a.at[k], ctx=there)

    def inward(self, k):
        here = self._from(k)
        slab = self.slab(self.seq * self.size + here)
        return push(self.source(here), slab, self.send_a.at[k], self.recv_a.at[k], ctx=here)

    def sideways(self, which, k):
        owner = row_mate(self.seq) if which == 2 else self.seq
        slab = self.slab(owner * self.size + self._from(k))
        mate = row_mate(self.seq) if which == 1 else core_mate(self.seq)
        return push(slab, slab, self.send_b.at[which, k], self.recv_b.at[which, k], seq=mate)

    def landing(self, which, k):
        owner = (core_mate(self.seq), row_mate(self.seq), core_mate(row_mate(self.seq)))[which]
        slab = self.slab(owner * self.size + self._from(k))
        return push(slab, slab, self.send_b.at[which, k], self.recv_b.at[which, k], seq=core_mate(self.seq))

    def start(self):
        for k in range(1, self.size):
            self.outward(k).start()

    def step(self, k):
        if k == 0:
            self.local().wait()
        elif not self.gathered:
            self.inward(k).wait_recv()
        self.sideways(1, k).start()
        self.sideways(0, k).start()
        if k and not self.gathered:
            self.pass_on(k - 1)

    def pass_on(self, k):
        self.landing(1, k).wait_recv()
        self.sideways(2, k).start()

    def land(self):
        for k in range(self.size):
            self.landing(0, k).wait_recv()
            self.landing(2, k).wait_recv()

    def drain(self):
        for k in range(self.size):
            for which in range(3):
                self.sideways(which, k).wait_send()
            if k and not self.gathered:
                self.outward(k).wait_send()

    @staticmethod
    def scratch(size):
        dma = pltpu.SemaphoreType.DMA
        return [dma((size,)), dma((size,)), dma((3, size)), dma((3, size)), dma]


def front_kernel(
    size, split, tile,
    tokens_in, upstream, docs_in, cos_turned, sin_turned, pack, gu_pack, down_pack, out_rows,
    inputs_all, upstream_all, mixed, query_pair, key_value, out_pair, log_total, docs_row, docs_col, places_row,
    cosine, sine, row_scale, head_weight, small, gu_full, down_full, out_full,
    docs_all, pack_all, key_pad, value_turned, head_out,
    send_t, recv_t, send_n, recv_n, send_x, recv_x, own, *scratch,
):
    me, seq = lax.axis_index("ctx"), lax.axis_index("seq")
    lane, row, number = me % split, me // split, size // split
    tokens, width = tokens_in.shape
    steps = size // 2
    place = ring_place(me, size)
    greet(
        [{"ctx": (me + k) % size} for k in range(1, size)]
        + [{"seq": core_mate(seq)}, {"seq": row_mate(seq)}]
    )
    heads = Spread(size, lambda c: pack.at[c], lambda owner: pack_all.at[owner], scratch[0:5])
    bulk = [
        Spread(size, lambda c: gu_pack.at[c], lambda owner: gu_full.at[:, owner], scratch[5:10]),
        Spread(size, lambda c: down_pack.at[c], lambda owner: down_full.at[:, owner], scratch[10:15]),
    ]
    out = Spread(size, lambda c: out_rows, lambda owner: out_full.at[owner], scratch[15:20], True)
    lines = LineGather(
        size, out_rows, lambda owner, viewer: out_full.at[seq * size + owner], scratch[20:24]
    )
    ring = RingGather(size, tokens_in, inputs_all, send_t, recv_t)
    lines_up = LineGather(
        size, upstream, lambda owner, viewer: upstream_all.at[slot_seen(owner, viewer, size)], scratch[24:28]
    )

    def note(k):
        return push(docs_in, docs_all.at[me], send_n.at[k], recv_n.at[k], ctx=(me + k) % size)

    def noted(k):
        here = (me + size - k) % size
        return push(docs_in, docs_all.at[here], send_n.at[k], recv_n.at[k], ctx=here)

    def send_bulk(turn):
        for k in range(2 * turn + 1, min(2 * turn + 3, size)):
            for part in bulk:
                part.outward(k).start()

    heads.start()
    for k in range(1, size):
        note(k).start()
    lines.start()
    ring.start(0)
    heads.local().start()
    local = [
        pltpu.make_async_copy(tokens_in, inputs_all.at[me], own.at[0]),
        pltpu.make_async_copy(upstream, upstream_all.at[0], own.at[1]),
    ]
    for copy in local:
        copy.start()
    for part in bulk + [out]:
        part.local().start()
    docs_all[me] = docs_in[...]

    def tables(i, _):
        rows = pl.ds(pl.multiple_of(i * tile, tile), tile)
        cos, sin = cos_turned[:, rows], sin_turned[:, rows]
        cosine[rows] = jnp.concatenate([cos] * 4, axis=0).T
        sine[rows] = jnp.concatenate([-sin, sin] * 2, axis=0).T
        return 0

    lax.fori_loop(0, size * tokens // tile, tables, 0)
    for k in range(size):
        heads.step(k)
    heads.pass_on(size - 1)
    for part in bulk + [out]:
        part.step(0)
    lines.turn(1)
    ring.start(1)
    send_bulk(0)
    for k in range(1, size):
        noted(k).wait_recv()
    log_total[...] = jnp.zeros_like(log_total)

    def documents(c, _):
        rows = pl.ds(pl.multiple_of(c * tokens, tokens), tokens)
        docs_col[rows] = docs_all[c].astype(WIDE).T[:, 0:1].astype(jnp.int32)
        return 0

    lax.fori_loop(0, size, documents, 0)

    def my_documents(b, _):
        rows = pl.ds(pl.multiple_of(b * tokens, tokens), tokens)
        docs_row[:, rows] = docs_all[b * split + lane]
        first = (b * split + lane) * tokens
        places_row[:, rows] = lax.broadcasted_iota(jnp.int32, (8, tokens), 1) + first
        return 0

    lax.fori_loop(0, number, my_documents, 0)
    heads.land()
    whole = pack_all[...].astype(WIDE).reshape(width, pack_all.shape[2])
    head_weight[...] = whole[:, :HEAD_COLS].astype(LOW)
    small[...] = whole[:, HEAD_COLS:].T[: small.shape[0]]
    gain_row = small.shape[0] - 8
    for copy in local:
        copy.wait()

    half = lax.broadcasted_iota(jnp.int32, (tokens, 2 * HEAD_DIM), 1) < HEAD_DIM

    def project(spot):
        owner = ring_member(spot, size)
        rows = pl.ds(pl.multiple_of(owner * tokens, tokens), tokens)
        values = inputs_all[owner].astype(WIDE)
        scale_one = lax.rsqrt(jnp.mean(values * values, axis=-1, keepdims=True) + NORM_EPS)
        row_scale[rows] = scale_one
        attend = (values * scale_one * small[gain_row : gain_row + 1]).astype(LOW)
        pre = dot_nn(attend, head_weight[...])
        cos, sin = cosine[rows], sine[rows]
        query, pair = pre[:, : 2 * HEAD_DIM], pre[:, 2 * HEAD_DIM :]
        query = query * cos + swap_halves(query) * sin
        pair = pair * jnp.where(half, cos, 1.0) + swap_halves(pair) * jnp.where(half, sin, 0.0)
        key_value[rows] = pair.astype(LOW)
        key_pad[0, rows] = jnp.where(half, pair, 0.0).astype(LOW)
        key_pad[1, rows] = jnp.where(half, 0.0, pltpu.roll(pair, HEAD_DIM, 1)).astype(LOW)
        value_turned[:, rows] = pair.T[HEAD_DIM:].astype(LOW)

        @pl.when(owner % split == lane)
        def _():
            query_pair[pl.ds(pl.multiple_of(owner // split * tokens, tokens), tokens)] = query.astype(LOW)

    project(place)

    def visit(turn, _):
        for step in range(1, steps):
            @pl.when(turn == step)
            def _():
                if step > 1:
                    ring.start(step)
                if step < steps - 1:
                    lines.turn(step + 1)
                else:
                    lines.finish()
                    for k in range(1, size):
                        out.step(k)
                send_bulk(step)
                if step == steps - 1:
                    lines_up.start()
                for k in range(2 * step - 3, 2 * step - 1):
                    for part in bulk if k > 0 else []:
                        part.step(k)

        def side(way, _):
            project(place + (2 * way - 1) * turn)
            return 0

        return lax.fori_loop(0, 2, side, 0)

    lax.fori_loop(1, steps, visit, 0)
    ring.land()
    project(place + steps)

    todo = [functools.partial(out.pass_on, k) for k in range(size)]
    todo.append(functools.partial(lines_up.turn, 1))
    for k in range(size - 3, size):
        todo += [functools.partial(part.step, k) for part in bulk]
        if k < size - 1:
            todo.append(functools.partial(lines_up.turn, k - size + 5))
    todo += [functools.partial(lines_up.turn, k) for k in range(4, steps)]

    def pump(count):
        for _ in range(min(count, len(todo))):
            todo.pop(0)()

    scale = HEAD_DIM**-0.5
    for i in range(number * tokens // tile):
        rows = pl.ds(i * tile, tile)
        query = query_pair[rows]
        query_doc, query_place = docs_row[0:1, rows], places_row[0:1, rows]

        def pairs(j, carry):
            keys = pl.ds(pl.multiple_of(j * tile, tile), tile)
            spot = lax.broadcasted_iota(jnp.int32, (tile, tile), 0) + j * tile
            allowed = (spot <= query_place) & (docs_col[keys] == query_doc)
            found = []
            for h in range(GROUP):
                peak, total, gathered = carry[3 * h : 3 * h + 3]
                score = jnp.where(allowed, dot_nt(key_pad[h, keys], query) * scale, NEG_BIG)
                higher = jnp.maximum(peak, jnp.max(score, axis=0, keepdims=True))
                keep = jnp.exp(peak - higher)
                prob = jnp.exp(score - higher)
                total = total * keep + jnp.sum(prob, axis=0, keepdims=True)
                gathered = gathered * keep + dot_nn(value_turned[:, keys], prob.astype(LOW))
                found += [higher, total, gathered]
            return tuple(found)

        empty = (
            jnp.full((1, tile), NEG_BIG, WIDE), jnp.zeros((1, tile), WIDE), jnp.zeros((HEAD_DIM, tile), WIDE)
        )
        found = lax.fori_loop(0, min(size * tokens // tile, (i + 1) * split), pairs, empty * GROUP)
        for h in range(GROUP):
            log_total[h : h + 1, rows] = found[3 * h] + jnp.log(found[3 * h + 1])
        result = jnp.concatenate([found[3 * h + 2] / found[3 * h + 1] for h in range(GROUP)], axis=0).T
        out_pair[rows] = result
        blocks = tile // tokens
        head_out[pl.ds(i * blocks, blocks)] = result.astype(LOW).reshape(blocks, tokens, 2 * HEAD_DIM)
        pump(4)

    def seat(index):
        return mixed.at[:, pl.ds(pl.multiple_of(index * 2 * HEAD_DIM, 2 * HEAD_DIM), 2 * HEAD_DIM)]

    swaps = []
    for k in range(1, number):
        there = (row + k) % number
        swaps.append(push(head_out.at[there], seat(row), send_x.at[k], recv_x.at[k], ctx=there * split + lane))
        swaps[-1].start()
    mine = pltpu.make_async_copy(head_out.at[row], seat(row), own.at[2])
    mine.start()
    pump(len(todo))
    for part in bulk:
        part.pass_on(size - 1)
    lines_up.finish()
    for k in range(1, number):
        here = (row + number - k) % number
        push(head_out.at[here], seat(here), send_x.at[k], recv_x.at[k], ctx=here * split + lane).wait_recv()
    mine.wait()
    for part in bulk + [out]:
        part.land()
    for copy in swaps:
        copy.wait_send()
    for k in range(1, size):
        note(k).wait_send()
    ring.drain()
    lines.drain()
    lines_up.drain()
    for part in [heads, out] + bulk:
        part.drain()


def run_front(tokens_in, upstream, docs, cos_turned, sin_turned, pack, gu_pack, down_pack, out_rows, split, owners, small_rows,
              collective):
    size = pack.shape[0]
    tokens, width = tokens_in.shape
    length, mine = size * tokens, size * tokens // split
    tile = 2 * tokens
    dma = pltpu.SemaphoreType.DMA
    vmem = pl.BlockSpec(memory_space=pltpu.VMEM)
    anywhere = pl.BlockSpec(memory_space=pl.ANY)
    pair = 2 * HEAD_DIM
    per_unit = gu_pack.shape[1]
    shape = jax.ShapeDtypeStruct
    return pl.pallas_call(
        functools.partial(front_kernel, size, split, tile),
        out_shape=[
            shape((size, tokens, width), LOW), shape((size, tokens, width), LOW),
            shape((tokens, HEADS * HEAD_DIM), LOW), shape((mine, pair), LOW), shape((length, pair), LOW),
            shape((mine, pair), WIDE), shape((8, mine), WIDE), shape((8, mine), jnp.int32),
            shape((length, 1), jnp.int32), shape((8, mine), jnp.int32),
            shape((length, pair), WIDE), shape((length, pair), WIDE), shape((length, 1), WIDE),
            shape((width, HEAD_COLS), LOW), shape((small_rows, width), WIDE),
            shape((per_unit, owners) + gu_pack.shape[2:], LOW),
            shape((per_unit, owners) + down_pack.shape[2:], LOW),
            shape((owners,) + out_rows.shape, LOW),
        ],
        in_specs=[vmem] * 9,
        out_specs=[vmem, anywhere] + [vmem] * 13 + [anywhere] * 3,
        scratch_shapes=[
            pltpu.VMEM((size, 8, tokens), jnp.int32),
            pltpu.VMEM((owners,) + pack.shape[1:], LOW),
            pltpu.VMEM((GROUP, length, pair), LOW),
            pltpu.VMEM((HEAD_DIM, length), LOW),
            pltpu.VMEM((size // split, tokens, pair), LOW),
            dma((2, size // 2)), dma((2, size // 2)),
            dma((size,)), dma((size,)), dma((size // split,)), dma((size // split,)), dma((3,)),
        ] + Spread.scratch(size) * 4 + LineGather.scratch(size) * 2,
        compiler_params=pltpu.CompilerParams(
            collective_id=collective, has_side_effects=True, vmem_limit_bytes=60 << 20
        ),
        name="run_front",
    )(tokens_in, upstream, docs, cos_turned, sin_turned, pack, gu_pack, down_pack, out_rows)


class Homing:
    def __init__(self, size, grads, out, bufs, sems):
        self.size, self.grads, self.out = size, grads, out
        self.near, self.from_core, self.from_row, self.to_row, self.to_home = bufs
        self.load, self.send_a, self.recv_a, self.send_b, self.recv_b, self.send_c, self.recv_c = sems
        self.me, self.seq = lax.axis_index("ctx"), lax.axis_index("seq")

    def _block(self, s0, k):
        index = s0 * self.size + (self.me + k) % self.size
        return self.grads.at[:, index] if self.grads.ndim == 4 else self.grads.at[index]

    def _row(self, which):
        return row_mate(self.seq) if which == 0 else self.seq

    def fetch(self, which, k):
        return pltpu.make_async_copy(self._block(self._row(which), k), self.near.at[which, k], self.load.at[which, k])

    def to_core(self, which, k):
        return push(
            self._block(core_mate(self._row(which)), k), self.from_core.at[which, k],
            self.send_a.at[which, k], self.recv_a.at[which, k], seq=core_mate(self.seq),
        )

    def across(self, k):
        return push(
            self.to_row.at[k], self.from_row.at[k], self.send_b.at[k], self.recv_b.at[k], seq=row_mate(self.seq)
        )

    def homeward(self, k):
        there = (self.me + k) % self.size
        return push(self.to_home.at[k], self.out.at[self.me], self.send_c.at[k], self.recv_c.at[k], ctx=there)

    def arriving(self, k):
        here = (self.me + self.size - k) % self.size
        return push(self.to_home.at[k], self.out.at[here], self.send_c.at[k], self.recv_c.at[k], ctx=here)

    def start(self):
        def body(k, _):
            for which in range(2):
                self.to_core(which, k).start()
                self.fetch(which, k).start()
            return 0

        lax.fori_loop(0, self.size, body, 0)

    def first(self, k):
        self.fetch(0, k).wait()
        self.to_core(0, k).wait_recv()
        sum_into(self.to_row.at[k], [self.near.at[0, k], self.from_core.at[0, k]])
        self.across(k).start()

    def second(self, k, home=False):
        self.fetch(1, k).wait()
        self.to_core(1, k).wait_recv()
        self.across(k).wait_recv()
        target = self.out.at[self.me] if home else self.to_home.at[k]
        sum_into(target, [self.near.at[1, k], self.from_core.at[1, k], self.from_row.at[k]])
        if not home:
            self.homeward(k).start()

    def close(self):
        def body(k, _):
            self.arriving(k).wait_recv()
            self.homeward(k).wait_send()
            return 0

        lax.fori_loop(1, self.size, body, 0)

        def drain(k, _):
            self.to_core(0, k).wait_send()
            self.to_core(1, k).wait_send()
            self.across(k).wait_send()
            return 0

        lax.fori_loop(0, self.size, drain, 0)

    @staticmethod
    def scratch(size, block):
        slab = (size,) + block
        dma = pltpu.SemaphoreType.DMA
        return [
            pltpu.VMEM((2,) + slab, LOW), pltpu.VMEM((2,) + slab, LOW), pltpu.VMEM(slab, LOW),
            pltpu.VMEM(slab, LOW), pltpu.VMEM(slab, LOW),
            dma((2, size)), dma((2, size)), dma((2, size)), dma((size,)), dma((size,)), dma((size,)), dma((size,)),
        ]


class SmallSum:
    def __init__(self, size, small, out, from_seq, total, from_ctx, sems):
        self.size, self.small, self.out = size, small, out
        self.from_seq, self.total, self.from_ctx = from_seq, total, from_ctx
        self.send_a, self.recv_a, self.send_b, self.recv_b = sems
        self.me, self.seq = lax.axis_index("ctx"), lax.axis_index("seq")

    def _swap(self, k):
        there = (self.seq + k) % 4
        return push(self.small.at[there], self.from_seq.at[k], self.send_a.at[k], self.recv_a.at[k], seq=there)

    def _tell(self, k):
        there = (self.me + k) % self.size
        return push(self.total, self.from_ctx.at[self.me], self.send_b.at[k], self.recv_b.at[k], ctx=there)

    def _hear(self, k):
        here = (self.me + self.size - k) % self.size
        return push(self.total, self.from_ctx.at[here], self.send_b.at[k], self.recv_b.at[k], ctx=here)

    def start(self):
        for k in range(1, 4):
            self._swap(k).start()

    def middle(self):
        for k in range(1, 4):
            self._swap(k).wait_recv()
        self.total[...] = self.small[self.seq] + self.from_seq[1] + self.from_seq[2] + self.from_seq[3]
        for k in range(1, self.size):
            self._tell(k).start()

    def finish(self):
        total = self.total[...]
        for k in range(1, self.size):
            self._hear(k).wait_recv()
            total = total + self.from_ctx[(self.me + self.size - k) % self.size]
        self.out[...] = total
        for k in range(1, 4):
            self._swap(k).wait_send()
        for k in range(1, self.size):
            self._tell(k).wait_send()

    @staticmethod
    def scratch(size, rows, lanes):
        dma = pltpu.SemaphoreType.DMA
        part = (rows, lanes // 4)
        return [
            pltpu.VMEM((4,) + part, WIDE), pltpu.VMEM(part, WIDE), pltpu.VMEM((size,) + part, WIDE),
            dma((4,)), dma((4,)), dma((size,)), dma((size,)),
        ]


def back_kernel(
    size, split, tile,
    mixed_grad, gu_grads, down_grads, out_grads, small, query_pair, key_value, out_pair, log_total,
    docs_row, docs_col, places_row, cosine, sine, gain, inputs_all, row_scale, head_weight,
    attend_sum, gu_home, down_home, out_home, head_home, small_home,
    head_grad, key_pad, value_pad, key_acc, value_acc, query_acc, heads_grad, heads_turned, head_part, small_full,
    attend_own, held, send_r, recv_r, send_x, recv_x, own_x, *scratch,
):
    me, seq = lax.axis_index("ctx"), lax.axis_index("seq")
    lane, row, number = me % split, me // split, size // split
    tokens = mixed_grad.shape[1]
    length, width = inputs_all.shape
    greet(
        [{"ctx": (me + k) % size} for k in range(1, size)]
        + [{"seq": (seq + k) % 4} for k in range(1, 4)]
    )

    def homing(i, grads, out):
        part = scratch[12 * i : 12 * i + 12]
        return Homing(size, grads, out, part[:5], part[5:])

    early = [homing(0, gu_grads, gu_home), homing(1, down_grads, down_home), homing(2, out_grads, out_home)]
    late = homing(3, head_part, head_home)
    tail = scratch[48:]
    total_small = SmallSum(size, small_full, small_home, tail[0], tail[1], tail[2], tail[3:])

    mine = pltpu.make_async_copy(mixed_grad.at[row], head_grad.at[row], own_x)
    mine.start()
    swaps = []
    for k in range(1, number):
        there = (row + k) % number
        swaps.append(
            push(mixed_grad.at[there], head_grad.at[row], send_x.at[k], recv_x.at[k], ctx=there * split + lane)
        )
        swaps[-1].start()
    for home in early:
        home.start()

    steps = []
    for k in range(size):
        steps += [functools.partial(home.first, k) for home in early]
    for k in range(1, size):
        steps += [functools.partial(home.second, k) for home in early]
    steps += [functools.partial(home.second, 0, True) for home in early]

    def pump(count):
        for _ in range(min(count, len(steps))):
            steps.pop(0)()

    half = lax.broadcasted_iota(jnp.int32, (tile, 2 * HEAD_DIM), 1) < HEAD_DIM
    zero = jnp.zeros((tile, 2 * HEAD_DIM), WIDE)

    def prepare(i, _):
        rows = pl.ds(pl.multiple_of(i * tile, tile), tile)
        pair = key_value[rows].astype(WIDE)
        turned = pltpu.roll(pair, HEAD_DIM, 1)
        key_pad[0, rows] = jnp.where(half, pair, zero).astype(LOW)
        key_pad[1, rows] = jnp.where(half, zero, turned).astype(LOW)
        value_pad[0, rows] = jnp.where(half, turned, zero).astype(LOW)
        value_pad[1, rows] = jnp.where(half, zero, pair).astype(LOW)
        key_acc[rows] = zero
        value_acc[rows] = zero
        heads_grad[rows, pl.ds(0, 2 * HEAD_DIM)] = zero.astype(LOW)
        return 0

    lax.fori_loop(0, length // tile, prepare, 0)
    for k in range(1, number):
        here = (row + number - k) % number
        push(mixed_grad.at[here], head_grad.at[here], send_x.at[k], recv_x.at[k], ctx=here * split + lane).wait_recv()
    mine.wait()

    scale = HEAD_DIM**-0.5
    blocks = tile // tokens
    for i in range(number * tokens // tile):
        rows = pl.ds(i * tile, tile)
        query = query_pair[rows]
        grad = head_grad[pl.ds(i * blocks, blocks)].reshape(tile, 2 * HEAD_DIM)
        product = (grad.astype(WIDE) * out_pair[rows].astype(WIDE)).T
        deltas = [
            jnp.sum(product[h * HEAD_DIM : (h + 1) * HEAD_DIM], axis=0, keepdims=True) for h in range(GROUP)
        ]
        query_doc, query_place = docs_row[0:1, rows], places_row[0:1, rows]
        totals = [log_total[h : h + 1, rows] for h in range(GROUP)]
        query_acc[...] = zero

        def pairs(j, _):
            keys = pl.ds(pl.multiple_of(j * tile, tile), tile)
            place = lax.broadcasted_iota(jnp.int32, (tile, tile), 0) + j * tile
            allowed = (place <= query_place) & (docs_col[keys] == query_doc)
            key_part, value_part, query_part = zero, zero, zero
            for h in range(GROUP):
                mine_half = half if h == 0 else jnp.logical_not(half)
                score = dot_nt(key_pad[h, keys], query)
                prob = jnp.where(allowed, jnp.exp(score * scale - totals[h]), 0.0)
                slope = dot_nt(value_pad[h, keys], grad)
                ds = (prob * (slope - deltas[h])).astype(LOW)
                value_part = jnp.where(mine_half, dot_nn(prob.astype(LOW), grad), value_part)
                key_part = jnp.where(mine_half, dot_nn(ds, query), key_part)
                query_part = query_part + dot_tn(ds, key_pad[h, keys])
            key_acc[keys] += key_part
            value_acc[keys] += value_part
            query_acc[...] += query_part
            return 0

        lax.fori_loop(0, min(length // tile, (i + 1) * split), pairs, 0)
        turn = query_acc[...] * scale
        for b in range(blocks):
            at = pl.ds(pl.multiple_of(((i * blocks + b) * split + lane) * tokens, tokens), tokens)
            piece = turn[b * tokens : (b + 1) * tokens]
            heads_grad[at, pl.ds(0, 2 * HEAD_DIM)] = unturn(piece, cosine, sine, at, 0).astype(LOW)
        pump(6)

    def fold(i, _):
        rows = pl.ds(pl.multiple_of(i * tile, tile), tile)
        key_part, value_part = key_acc[rows], value_acc[rows]
        key_part = (key_part + pltpu.roll(key_part, HEAD_DIM, 1)) * scale
        value_part = value_part + pltpu.roll(value_part, HEAD_DIM, 1)
        both = jnp.where(half, key_part, value_part)
        heads_grad[rows, pl.ds(2 * HEAD_DIM, 2 * HEAD_DIM)] = unturn(both, cosine, sine, rows, 1).astype(LOW)
        return 0

    lax.fori_loop(0, length // tile, fold, 0)

    def transpose(i, _):
        rows = pl.ds(pl.multiple_of(i * tile, tile), tile)
        heads_turned[:, rows] = heads_grad[rows].astype(WIDE).T.astype(LOW)
        return 0

    lax.fori_loop(0, length // tile, transpose, 0)

    reduce = RingReduce(size, held, send_r, recv_r)
    small_full[...] = small[...]
    gain_row = small.shape[1] - 8

    def attend(place, slot):
        owner = ring_member(place, size)
        rows = pl.ds(pl.multiple_of(owner * tokens, tokens), tokens)
        part = dot_nt(heads_grad[rows], head_weight[...])
        attend_own[slot] = part.astype(LOW)
        normed = inputs_all[rows].astype(WIDE) * row_scale[rows]
        share = jnp.sum(part * normed, axis=0, keepdims=True)
        lanes = width // 4
        for s0 in range(4):
            small_full[s0, gain_row : gain_row + 1] += share[:, s0 * lanes : (s0 + 1) * lanes]

    place = ring_place(me, size)
    half_ring = size // 2
    attend(place + half_ring, 0)
    reduce.start(0, [attend_own.at[0]] * 2)
    for step in range(1, half_ring):
        attend(place + half_ring - step, 1)
        attend(place - half_ring + step, 2)
        if step == 1:
            def columns(j, _):
                cols = pl.ds(pl.multiple_of(j * tile, tile), tile)
                normed = inputs_all[:, cols].astype(WIDE) * row_scale[...]
                part = dot_nn(heads_turned[...], (normed * gain[gain.shape[0] - 8 : gain.shape[0] - 7, cols]).astype(LOW)).T.astype(LOW)
                depth = head_part.shape[1]
                head_part[pl.ds(j * (tile // depth), tile // depth)] = part.reshape(tile // depth, depth, HEAD_COLS)
                return 0

            lax.fori_loop(0, width // tile, columns, 0)
            late.start()
        reduce.start(step, [attend_own.at[1], attend_own.at[2]])
        pump(3)
    attend(place, 1)
    total_small.start()
    pump(len(steps))
    for k in range(size):
        late.first(k)
    total_small.middle()
    for k in range(1, size):
        late.second(k)
    late.second(0, True)
    reduce.finish(attend_sum, attend_own.at[1], attend_own.at[0])
    for home in early:
        home.close()
    late.close()
    total_small.finish()
    for copy in swaps:
        copy.wait_send()


def swap_halves(values):
    lane = lax.broadcasted_iota(jnp.int32, values.shape, 1) % HEAD_DIM
    return jnp.where(
        lane < HEAD_DIM // 2,
        pltpu.roll(values, values.shape[1] - HEAD_DIM // 2, 1),
        pltpu.roll(values, HEAD_DIM // 2, 1),
    )


def unturn(values, cosine, sine, rows, which):
    cos, sin = cosine[rows], sine[rows]
    if which:
        half = lax.broadcasted_iota(jnp.int32, values.shape, 1) < HEAD_DIM
        cos, sin = jnp.where(half, cos, 1.0), jnp.where(half, sin, 0.0)
    return values * cos - swap_halves(values) * sin


def attention_back(arrays, size, split, collective):
    (mixed_grad, gu_grads, down_grads, out_grads, small, query_pair, key_value, out_pair, log_total,
     docs_row, docs_col, places_row, cosine, sine, gain, inputs_all, row_scale, head_weight) = arrays
    tokens = mixed_grad.shape[1]
    length, width = inputs_all.shape
    tile = 2 * tokens
    blocks = [
        (gu_grads.shape[0],) + gu_grads.shape[2:], (down_grads.shape[0],) + down_grads.shape[2:],
        out_grads.shape[1:], (out_grads.shape[1], HEAD_COLS),
    ]
    small_rows = small.shape[1]
    dma = pltpu.SemaphoreType.DMA
    vmem = pl.BlockSpec(memory_space=pltpu.VMEM)
    anywhere = pl.BlockSpec(memory_space=pl.ANY)
    pair = (length, 2 * HEAD_DIM)
    scratch = [
        pltpu.VMEM(mixed_grad.shape, LOW),
        pltpu.VMEM((GROUP,) + pair, LOW), pltpu.VMEM((GROUP,) + pair, LOW),
        pltpu.VMEM(pair, WIDE), pltpu.VMEM(pair, WIDE), pltpu.VMEM((tile, 2 * HEAD_DIM), WIDE),
        pltpu.VMEM((length, HEAD_COLS), LOW), pltpu.VMEM((HEAD_COLS, length), LOW),
        pltpu.VMEM((4 * size, out_grads.shape[1], HEAD_COLS), LOW),
        pltpu.VMEM(small.shape, WIDE),
        pltpu.VMEM((3, tokens, width), LOW), pltpu.VMEM((2, size // 2, tokens, width), LOW),
        dma((2, size // 2)), dma((2, size // 2)), dma((size // split,)), dma((size // split,)), dma,
    ]
    for block in blocks:
        scratch += Homing.scratch(size, block)
    scratch += SmallSum.scratch(size, small_rows, width)
    return pl.pallas_call(
        functools.partial(back_kernel, size, split, tile),
        out_shape=[jax.ShapeDtypeStruct((tokens, width), WIDE)]
        + [jax.ShapeDtypeStruct((size,) + block, LOW) for block in blocks]
        + [jax.ShapeDtypeStruct((small_rows, width // 4), WIDE)],
        in_specs=[vmem, anywhere, anywhere, anywhere] + [vmem] * 14,
        out_specs=[vmem] * 6,
        scratch_shapes=scratch,
        compiler_params=pltpu.CompilerParams(
            collective_id=collective, has_side_effects=True, vmem_limit_bytes=62 << 20
        ),
        name="attention_back",
    )(*arrays)


def rms_scale(values):
    return lax.rsqrt(jnp.mean(values * values, axis=-1, keepdims=True) + NORM_EPS)


def rope_tables(places, factor):
    freqs = 1.0 / ROPE_BASE ** (jnp.arange(0, HEAD_DIM, 2).astype(WIDE) / HEAD_DIM)
    angles = (places.astype(WIDE) / factor)[None, :] * freqs[:, None]
    return jnp.cos(angles), jnp.sin(angles)


def dot(equation, left, right):
    return jnp.einsum(equation, left, right, preferred_element_type=WIDE)


def on_device(
    layer_input, document_ids, expert_routes, rope_factor, attention_gain, feedforward_gain,
    query_weight, key_weight, value_weight, output_weight, router_weight, gate_up, down_weight, cotangent,
):
    nseq, nctx = lax.axis_size("seq"), lax.axis_size("ctx")
    tokens, width = layer_input.shape[1:]
    length = tokens * nctx
    rows, experts, ff2 = gate_up.shape
    ff = ff2 // 2
    down_rows = down_weight.shape[0]
    per_unit = max(1, experts // nctx)
    ff_split = max(1, nctx // experts)
    ff_part = ff // ff_split
    head_split = nctx // KV_HEADS
    unit = lax.axis_index("ctx")
    owners = nseq * nctx

    if ff_split == 1:
        gu_pack = gate_up.astype(LOW).transpose(1, 0, 2).reshape(nctx, per_unit, rows, ff2)
    else:
        gu_pack = (
            gate_up.astype(LOW).reshape(rows, experts, 2, ff_split, ff_part).transpose(1, 3, 0, 2, 4)
            .reshape(nctx, per_unit, rows, 2 * ff_part)
        )
    down_pack = jnp.repeat(
        down_weight.astype(LOW).transpose(1, 0, 2), ff_split, axis=0
    ).reshape(nctx, per_unit, down_rows, width)
    head_pack = jnp.concatenate(
        [
            query_weight.reshape(rows, KV_HEADS, GROUP * HEAD_DIM),
            key_weight.reshape(rows, KV_HEADS, HEAD_DIM),
            value_weight.reshape(rows, KV_HEADS, HEAD_DIM),
        ],
        axis=-1,
    ).astype(LOW).transpose(1, 0, 2)
    head_pack = jnp.repeat(head_pack, head_split, axis=0)
    small_rows = experts + 8
    small_pack = jnp.concatenate(
        [router_weight, attention_gain[:, None], feedforward_gain[:, None], jnp.zeros((rows, 110 + 16 - experts), WIDE)],
        axis=1,
    ).astype(LOW)
    small_pack = jnp.broadcast_to(small_pack[None], (nctx,) + small_pack.shape)
    pack = jnp.concatenate([head_pack, small_pack], axis=2)
    documents = jnp.broadcast_to(document_ids.reshape(1, tokens), (8, tokens))
    cos_turned, sin_turned = rope_tables(jnp.arange(length, dtype=jnp.int32), rope_factor[0])

    (inputs_all, upstream_all, mixed_low, query_pair, key_value, out_pair, log_total, docs_row, docs_col, places_row,
     cosine, sine, row_scale, head_full, small_full, gu_full, down_full, out_full) = run_front(
        layer_input[0], cotangent[0], documents, cos_turned, sin_turned, pack, gu_pack, down_pack,
        output_weight.astype(LOW), head_split, owners, small_rows, 1,
    )
    gu_full = gu_full.reshape(per_unit, width, 2 * ff_part)
    down_full = down_full.reshape(per_unit, ff, width)
    if ff_split > 1:
        down_full = lax.dynamic_slice_in_dim(down_full, (unit % ff_split) * ff_part, ff_part, 1)
    out_full = out_full.reshape(HEADS * HEAD_DIM, width)
    router_full = small_full[:experts].astype(LOW)
    gain_one, gain_two = small_full[experts], small_full[experts + 1]

    inputs = layer_input[0].astype(WIDE)
    middle = inputs + dot("tj,jd->td", mixed_low, out_full)
    scale_two = rms_scale(middle)
    normed_two = middle * scale_two
    expert_input = (normed_two * gain_two).astype(LOW)
    logits = dot("td,ed->te", expert_input, router_full)
    chosen = jnp.any(
        expert_routes[0][:, :, None] == jnp.arange(experts, dtype=jnp.int32)[None, None, :], axis=1
    )
    picked = jnp.where(chosen, logits, NEG_BIG)
    expo_gate = jnp.where(chosen, jnp.exp(picked - jnp.max(picked, axis=-1, keepdims=True)), 0.0)
    combine = expo_gate / jnp.sum(expo_gate, axis=-1, keepdims=True)

    mix, back_sum, gate_grad_all, gu_grads, down_grads = run_experts(
        expert_input, combine.T, upstream_all, gu_full, down_full, nctx, ff_split, owners, down_rows, 3
    )

    layer_output = (middle + mix).astype(LOW)[None]
    upstream = cotangent[0].astype(WIDE)
    gate_grad = gate_grad_all[:, :per_unit].reshape(experts, ff_split, tokens).sum(axis=1).T
    gate_grad = jnp.where(chosen, gate_grad, 0.0)
    select_grad = combine * (gate_grad - jnp.sum(combine * gate_grad, axis=-1, keepdims=True))
    logit_grad = select_grad.astype(LOW)
    back_two = back_sum + dot("te,ed->td", logit_grad, router_full)
    router_part = dot("te,td->ed", logit_grad, expert_input)
    gain_two_part = jnp.sum(back_two * normed_two, axis=0)
    normed_two_grad = back_two * gain_two
    middle_grad = upstream + scale_two * (
        normed_two_grad - normed_two * jnp.mean(normed_two_grad * normed_two, axis=-1, keepdims=True)
    )
    project_grad = middle_grad.astype(LOW)
    out_grad_part = dot("tj,td->jd", mixed_low, project_grad)
    mixed_grad = dot("td,jd->tj", project_grad, out_full).astype(LOW)
    mixed_grad = mixed_grad.reshape(tokens, KV_HEADS, GROUP * HEAD_DIM).transpose(1, 0, 2)

    small_grads = jnp.concatenate(
        [router_part, gain_two_part[None], jnp.zeros((31 - experts, width), WIDE)], axis=0
    ).reshape(32, nseq, width // nseq).transpose(1, 0, 2)
    if ff_split > 1:
        down_grads = lax.dynamic_update_slice_in_dim(
            jnp.zeros((per_unit, owners, down_rows, width), LOW), down_grads,
            (unit % ff_split) * (ff_part // down_rows), 1,
        )
    attend_sum, gu_home, down_home, out_home, head_home, small_home = attention_back(
        [
            mixed_grad,
            gu_grads,
            down_grads,
            out_grad_part.astype(LOW).reshape(owners, rows, width),
            small_grads,
            query_pair, key_value, out_pair, log_total, docs_row, docs_col, places_row,
            cosine, sine, small_full, inputs_all.reshape(length, width), row_scale, head_full,
        ],
        nctx, head_split, 7,
    )
    gu_home, down_home = gu_home.astype(WIDE), down_home.astype(WIDE)
    out_home, head_home = out_home.astype(WIDE), head_home.astype(WIDE)
    if ff_split == 1:
        gate_up_gradient = gu_home.reshape(experts, rows, ff2).transpose(1, 0, 2)
        down_gradient = down_home.reshape(experts, down_rows, width).transpose(1, 0, 2)
    else:
        gate_up_gradient = (
            gu_home.reshape(experts, ff_split, rows, 2, ff_part).transpose(2, 0, 3, 1, 4).reshape(rows, experts, ff2)
        )
        down_gradient = down_home.reshape(experts, ff_split, down_rows, width).sum(axis=1).transpose(1, 0, 2)
    output_gradient = out_home.sum(axis=0)
    head_home = head_home.reshape(KV_HEADS, head_split, rows, HEAD_COLS).sum(axis=1).transpose(1, 0, 2)
    query_gradient = head_home[..., : GROUP * HEAD_DIM].reshape(rows, HEADS * HEAD_DIM)
    key_gradient = head_home[..., GROUP * HEAD_DIM : -HEAD_DIM].reshape(rows, KV_HEADS * HEAD_DIM)
    value_gradient = head_home[..., -HEAD_DIM:].reshape(rows, KV_HEADS * HEAD_DIM)
    small_home = lax.dynamic_slice_in_dim(small_home, unit * rows, rows, axis=1)
    router_gradient = small_home[:experts].T

    scale_one = rms_scale(inputs)
    normed_one = inputs * scale_one
    normed_one_grad = attend_sum * gain_one
    input_gradient = (
        middle_grad
        + scale_one
        * (normed_one_grad - normed_one * jnp.mean(normed_one_grad * normed_one, axis=-1, keepdims=True))
    ).astype(LOW)[None]
    return (
        layer_output, input_gradient, small_home[24], small_home[experts],
        query_gradient, key_gradient, value_gradient, output_gradient, router_gradient,
        gate_up_gradient, down_gradient,
    )


def solution(mesh):
    both = ("seq", "ctx")
    return jax.shard_map(
        on_device,
        mesh=mesh,
        in_specs=(
            P("seq", "ctx", None), P("seq", "ctx"), P("seq", "ctx", None), P(), P(both), P(both),
            P(both, None), P(both, None), P(both, None), P(both, None), P(both, None),
            P(both, None, None), P(both, None, None), P("seq", "ctx", None),
        ),
        out_specs=(
            P("seq", "ctx", None), P("seq", "ctx", None), P(both), P(both),
            P(both, None), P(both, None), P(both, None), P(both, None), P(both, None),
            P(both, None, None), P(both, None, None),
        ),
        check_vma=False,
    )
```

```python
import functools
import math

import jax
import jax.numpy as jnp
from jax import lax
from jax.experimental import pallas as pl
from jax.experimental.pallas import tpu as pltpu
from jax.sharding import PartitionSpec as P

HEADS = 16
KV_HEADS = 8
HEAD_DIM = 64
GROUP = HEADS // KV_HEADS
HEAD_COLS = (GROUP + 2) * HEAD_DIM

NORM_EPS = 1e-06
ROPE_BASE = 10000.0
NEG_BIG = -1e30
LOW = jnp.bfloat16
WIDE = jnp.float32
MESH = pl.DeviceIdType.MESH


def ring_place(index, size):
    half = index // 2
    return half + (index % 2) * (size - 1 - 2 * half)


def ring_member(place, size):
    place = (place + 2 * size) % size
    far = place // (size // 2)
    return 2 * place + far * (2 * size - 1 - 4 * place)


def slot_of(distance, size):
    if distance == 0:
        return 0
    if abs(distance) == size // 2:
        return 1
    return 2 * abs(distance) + (distance > 0)


def slot_seen(owner, viewer, size):
    half = size // 2
    ahead = (ring_place(owner, size) - ring_place(viewer, size) + 2 * size) % size
    far = ahead // half
    plain = (2 * ahead + 1) * (1 - far) + 2 * (size - ahead) * far
    same = (size - ahead) // size
    opposite = (size - (ahead + half) % size) // size
    return plain - same - (size - 1) * opposite


def core_mate(index):
    return index + 1 - 2 * (index % 2)


def row_mate(index):
    return (index + 2) % 4


def push(src, dst, send, recv, **where):
    return pltpu.make_async_remote_copy(
        src_ref=src, dst_ref=dst, send_sem=send, recv_sem=recv, device_id=where, device_id_type=MESH
    )


def greet(peers):
    barrier = pltpu.get_barrier_semaphore()
    for where in peers:
        pl.semaphore_signal(barrier, inc=1, device_id=where, device_id_type=MESH)
    pl.semaphore_wait(barrier, len(peers))


def ring_peers(size):
    place = ring_place(lax.axis_index("ctx"), size)
    return ring_member(place + 1, size), ring_member(place - 1, size)


class RingGather:
    def __init__(self, size, source, target, send, recv, relative=False):
        self.size, self.source, self.target, self.send, self.recv = size, source, target, send, recv
        self.relative = relative
        self.place = ring_place(lax.axis_index("ctx"), size)
        self.right, self.left = ring_peers(size)
        self.steps = size // 2

    def _copy(self, way, step, piece, arriving):
        sign = 2 * way - 1
        rows = self.source.shape[0]
        part = pl.ds(piece * (rows // 2), rows // 2)
        if self.relative:
            here, there = slot_of(sign * step, self.size), slot_of(sign * (step + 1), self.size)
        else:
            here = there = ring_member(self.place + sign * (step + arriving), self.size)
        dst = self.target.at[there, part]
        src = self.target.at[here, part] if step else self.source.at[part]
        where = self.left if way else self.right
        send, recv = self.send.at[way, step, piece], self.recv.at[way, step, piece]
        return push(dst if arriving else src, dst, send, recv, ctx=where)

    def start(self, step):
        for piece in range(2):
            for way in range(2):
                if step:
                    self._copy(way, step - 1, piece, 1).wait_recv()
                if step < self.steps - 1 or piece == way:
                    self._copy(way, step, piece, 0).start()

    def land(self):
        for way in range(2):
            self._copy(way, self.steps - 1, way, 1).wait_recv()

    def drain(self):
        for way in range(2):
            for step in range(self.steps):
                for piece in range(2) if step < self.steps - 1 else [way]:
                    self._copy(way, step, piece, 0).wait_send()

    def finish(self):
        self.land()
        self.drain()


class LineGather:
    def __init__(self, size, source, slab, sems):
        self.source, self.slab, self.count = source, slab, size // 2
        self.send, self.recv, self.send_m, self.recv_m = sems
        self.me = lax.axis_index("ctx")
        self.spot, self.side = self.me // 2, self.me % 2
        self.mate = core_mate(self.me)

    def _line(self, way, step):
        owner = self.me - 2 * step if way == 0 else self.me + 2 * step
        there = self.me + 2 if way == 0 else self.me - 2
        source = self.slab(owner, self.me) if step else self.source
        return push(source, self.slab(owner, there), self.send.at[way, step], self.recv.at[way, step], ctx=there)

    def _arriving(self, way, step):
        owner = self.me - 2 * step - 2 if way == 0 else self.me + 2 * step + 2
        here = self.slab(owner, self.me)
        return push(here, here, self.send.at[way, step], self.recv.at[way, step], ctx=self.mate)

    def _across(self, spot, own=False):
        owner = 2 * spot + self.side
        source = self.source if own else self.slab(owner, self.me)
        return push(
            source, self.slab(owner, self.mate), self.send_m.at[spot], self.recv_m.at[spot], ctx=self.mate
        )

    def _sends(self, way, step):
        if way == 0:
            return (self.spot + 1 < self.count) & (self.spot >= step)
        return (self.spot >= 1) & (self.spot + step < self.count)

    def start(self):
        for way in range(2):
            pl.when(self._sends(way, 0))(self._line(way, 0).start)
        self._across(self.spot, True).start()

    def turn(self, step):
        for way in range(2):
            there = self.spot >= step if way == 0 else self.spot + step < self.count

            @pl.when(there)
            def _():
                self._arriving(way, step - 1).wait_recv()
                self._across(self.spot - step if way == 0 else self.spot + step).start()

            pl.when(self._sends(way, step))(self._line(way, step).start)

    def finish(self):
        for spot in range(self.count):
            owner = 2 * spot + 1 - self.side
            here = self.slab(owner, self.me)
            push(here, here, self.send_m.at[spot], self.recv_m.at[spot], ctx=self.mate).wait_recv()

    def drain(self):
        for spot in range(self.count):
            self._across(spot).wait_send()
        for way in range(2):
            for step in range(self.count - 1):
                pl.when(self._sends(way, step))(self._line(way, step).wait_send)

    @staticmethod
    def scratch(size):
        dma, count = pltpu.SemaphoreType.DMA, size // 2
        return [dma((2, count)), dma((2, count)), dma((count,)), dma((count,))]


def row_step(rows):
    return rows if rows < 16 else 16


def sum_into(target, parts):
    rows = target.shape[-2]
    step = row_step(rows)

    def add_at(lead):
        def body(r, _):
            at = lead + (pl.ds(pl.multiple_of(r * step, step), step),)
            total = parts[0][at].astype(WIDE)
            for part in parts[1:]:
                total = total + part[at].astype(WIDE)
            target[at] = total.astype(target.dtype)
            return 0

        lax.fori_loop(0, rows // step, body, 0)

    for lead in [()] if target.ndim == 2 else [(u,) for u in range(target.shape[0])]:
        add_at(lead)


def dot_nn(a, b):
    return lax.dot_general(a, b, (((1,), (0,)), ((), ())), preferred_element_type=WIDE)


def dot_nt(a, b):
    return lax.dot_general(a, b, (((1,), (1,)), ((), ())), preferred_element_type=WIDE)


def dot_tn(a, b):
    return lax.dot_general(a, b, (((0,), (0,)), ((), ())), preferred_element_type=WIDE)


class RingReduce:
    def __init__(self, size, held, send, recv):
        self.size, self.held, self.send, self.recv = size, held, send, recv
        self.place = ring_place(lax.axis_index("ctx"), size)
        self.right, self.left = ring_peers(size)
        self.steps = size // 2
        self.rows = held.shape[2]

    def owner(self, way, step):
        ahead = self.steps - step
        return ring_member(self.place + ahead if way == 0 else self.place - ahead, self.size)

    def _copy(self, way, step, source):
        half = self.rows // 2
        part = pl.ds(0, self.rows) if step else pl.ds(half * way, half)
        where = self.right if way == 0 else self.left
        return push(
            source, self.held.at[way, step, part], self.send.at[way, step], self.recv.at[way, step], ctx=where
        )

    def start(self, step, own):
        for way in range(2):
            half = self.rows // 2
            near = pl.ds(0, half) if way == 0 else pl.ds(half, half)
            far = pl.ds(half, half) if way == 0 else pl.ds(0, half)
            source = own[way].at[near]
            if step:
                self._copy(way, step - 1, source).wait_recv()
                source = self.held.at[way, step - 1]
                if step == 1:
                    sum_into(source.at[near], [own[way].at[near], source.at[near]])
                    sum_into(source.at[far], [own[way].at[far]])
                else:
                    sum_into(source, [own[way], source])
            self._copy(way, step, source).start()

    def finish(self, target, own, first):
        last, half = self.steps - 1, self.rows // 2
        for way in range(2):
            self._copy(way, last, self.held.at[way, last]).wait_recv()
        sum_into(target, [own, self.held.at[0, last], self.held.at[1, last]])
        for way in range(2):
            for step in range(self.steps):
                source = self.held.at[way, step - 1] if step else first.at[pl.ds(half * way, half)]
                self._copy(way, step, source).wait_send()


def expert_kernel(
    size, split,
    expert_input, combine_rows, upstream, gu_hbm, down_hbm,
    mix, back_sum, gate_home, gu_grads, down_grads,
    tokens_all, combine_all, gu_weight, down_weight, combine_cols, gate_up, hidden, both_grad, out_acc, out_own,
    back_own, gate_send, held_out, held_back,
    send_b, recv_b, send_c, recv_c, send_y, recv_y, send_d, recv_d, send_g, recv_g, own_sem,
):
    me = lax.axis_index("ctx")
    place = ring_place(me, size)
    per_unit, width, ff2 = gu_weight.shape
    ff = ff2 // 2
    tokens = expert_input.shape[0]
    group = 2 * tokens
    groups = size // 2
    first_expert = me // split * per_unit
    greet([{"ctx": (me + k) % size} for k in range(1, size)])

    loads = [
        pltpu.make_async_copy(expert_input, tokens_all.at[0], own_sem.at[0]),
        pltpu.make_async_copy(combine_rows, combine_all.at[0], own_sem.at[1]),
        pltpu.make_async_copy(gu_hbm, gu_weight, own_sem.at[2]),
        pltpu.make_async_copy(down_hbm, down_weight, own_sem.at[3]),
    ]
    rings = [
        RingGather(size, combine_rows, combine_all, send_c, recv_c, True),
        RingGather(size, expert_input, tokens_all, send_b, recv_b, True),
    ]
    for ring in rings:
        ring.start(0)
    for load in loads:
        load.start()
    for load in loads:
        load.wait()
    lanes = lax.broadcasted_iota(jnp.int32, (group, 128), 1)

    def forward(turn, _):
        for step in range(1, groups):
            @pl.when(turn == step - 1)
            def _():
                for ring in rings:
                    ring.start(step)

        @pl.when(turn == groups - 1)
        def _():
            for ring in rings:
                ring.land()

        g = (turn + 1) % groups
        pair = pl.ds(2 * g, 2)
        rows = pl.ds(pl.multiple_of(g * group, group), group)
        token = tokens_all[pair].reshape(group, width)
        up_wide = upstream[pair].reshape(group, width).astype(WIDE)
        weights = jnp.concatenate([combine_all[2 * g].T, combine_all[2 * g + 1].T], axis=0)
        names = lax.broadcasted_iota(jnp.int32, weights.shape, 1)
        out_acc[...] = jnp.zeros_like(out_acc)

        def one(e, gates):
            weight = jnp.sum(jnp.where(names == first_expert + e, weights, 0.0), axis=1, keepdims=True)
            combine_cols[e, rows] = jnp.broadcast_to(weight, (group, 128))
            both = dot_nn(token, gu_weight[e])
            gate_up[e, rows] = both.astype(gate_up.dtype)
            gate, up = both[:, :ff], both[:, ff:]
            hid = (gate / (1.0 + jnp.exp(-gate)) * up).astype(LOW)
            hidden[e, rows] = hid
            produced = dot_nn(hid, down_weight[e])
            out_acc[...] += weight * produced
            dg = jnp.sum(up_wide * produced, axis=1, keepdims=True)
            return jnp.where(lanes == e, dg, gates)

        gates = lax.fori_loop(0, per_unit, one, jnp.zeros((group, 128), WIDE)).T
        gate_send[2 * g] = gates[:8, :tokens]
        gate_send[2 * g + 1] = gates[:8, tokens:]
        out_own[pair] = out_acc[...].astype(LOW).reshape(2, tokens, width)
        return 0

    lax.fori_loop(0, groups, forward, 0)

    def gate_copy(distance):
        there = ring_member(place + distance, size)
        k = distance % size
        return push(gate_send.at[slot_of(distance, size)], gate_home.at[me], send_g.at[k], recv_g.at[k], ctx=there)

    distances = [d for d in range(1 - groups, groups + 1) if d]
    for distance in distances:
        gate_copy(distance).start()
    gate_home[me] = gate_send[0]

    ring_out = RingReduce(size, held_out, send_y, recv_y)
    ring_back = RingReduce(size, held_back, send_d, recv_d)

    def backward(turn, _):
        for step in range(groups):
            @pl.when(turn == step)
            def _():
                ring_out.start(
                    step, [out_own.at[slot_of(groups - step, size)], out_own.at[slot_of(step - groups, size)]]
                )

        g = (groups - turn) % groups
        pair = pl.ds(2 * g, 2)
        rows = pl.ds(pl.multiple_of(g * group, group), group)
        up_wide = upstream[pair].reshape(group, width).astype(WIDE)
        out_acc[...] = jnp.zeros_like(out_acc)

        def one(e, _):
            weight = combine_cols[e, rows][:, 0:1]
            grad = (weight * up_wide).astype(LOW)
            hid_grad = dot_nt(grad, down_weight[e])
            gate = gate_up[e, rows, pl.ds(0, ff)].astype(WIDE)
            up = gate_up[e, rows, pl.ds(ff, ff)].astype(WIDE)
            sigmoid = 1.0 / (1.0 + jnp.exp(-gate))
            gate_part = (hid_grad * up * sigmoid * (1.0 + gate * (1.0 - sigmoid))).astype(LOW)
            up_part = (hid_grad * (gate * sigmoid)).astype(LOW)
            both_grad[e, rows, pl.ds(0, ff)] = gate_part
            both_grad[e, rows, pl.ds(ff, ff)] = up_part
            out_acc[...] += dot_nt(both_grad[e, rows], gu_weight[e])
            return 0

        lax.fori_loop(0, per_unit, one, 0)
        near = 2 * ((g + groups - 1) // groups)
        back_own[pl.ds(near, 2)] = out_acc[...].astype(LOW).reshape(2, tokens, width)
        for step in range(groups):
            @pl.when(turn == step)
            def _():
                ring_back.start(step, [back_own.at[1]] * 2 if step == 0 else [back_own.at[3], back_own.at[2]])
        return 0

    lax.fori_loop(0, groups, backward, 0)

    tile = 256
    length = size * tokens

    def gu_tile(j, _):
        turned = tokens_all[:, :, pl.ds(pl.multiple_of(j * tile, tile), tile)].reshape(length, tile)
        turned = turned.astype(WIDE).T.astype(LOW)
        depth = gu_grads.shape[2]
        count = tile // depth

        def one(e, _):
            part = dot_nn(turned, both_grad[e]).reshape(count, depth, ff2)
            gu_grads[e, pl.ds(j * count, count)] = part.astype(LOW)
            return 0

        return lax.fori_loop(0, per_unit, one, 0)

    lax.fori_loop(0, width // tile, gu_tile, 0)

    def down_tile(index, _):
        e, j = index // (ff // tile), index % (ff // tile)
        turned = hidden[e, :, pl.ds(pl.multiple_of(j * tile, tile), tile)].astype(WIDE).T.astype(LOW)
        depth = down_grads.shape[2]
        count = tile // depth
        for half in range(2):
            cols = pl.ds(half * (width // 2), width // 2)
            grad = upstream[:, :, cols].reshape(length, width // 2).astype(WIDE) * combine_cols[e][:, 0:1]
            part = dot_nn(turned, grad.astype(LOW)).reshape(count, depth, width // 2)
            down_grads[e, pl.ds(j * count, count), :, cols] = part.astype(LOW)
        return 0

    lax.fori_loop(0, per_unit * (ff // tile), down_tile, 0)

    ring_back.finish(back_sum, back_own.at[0], back_own.at[1])
    ring_out.finish(mix, out_own.at[0], out_own.at[1])
    for ring in rings:
        ring.drain()
    for distance in distances:
        here = ring_member(place - distance, size)
        k = distance % size
        push(gate_send.at[0], gate_home.at[here], send_g.at[k], recv_g.at[k], ctx=here).wait_recv()
        gate_copy(distance).wait_send()


def run_experts(expert_input, combine_rows, upstream, gu_full, down_full, size, split, owners, down_rows, collective):
    tokens, width = expert_input.shape
    per_unit, _, ff2 = gu_full.shape
    ff = ff2 // 2
    length = size * tokens
    dma = pltpu.SemaphoreType.DMA
    vmem = pl.BlockSpec(memory_space=pltpu.VMEM)
    anywhere = pl.BlockSpec(memory_space=pl.ANY)
    steps = (2, size // 2)
    return pl.pallas_call(
        functools.partial(expert_kernel, size, split),
        out_shape=[
            jax.ShapeDtypeStruct((tokens, width), WIDE),
            jax.ShapeDtypeStruct((tokens, width), WIDE),
            jax.ShapeDtypeStruct((size, 8, tokens), WIDE),
            jax.ShapeDtypeStruct((per_unit, owners, width // owners, ff2), LOW),
            jax.ShapeDtypeStruct((per_unit, ff // down_rows, down_rows, width), LOW),
        ],
        in_specs=[vmem, vmem, vmem, anywhere, anywhere],
        out_specs=[vmem] * 5,
        scratch_shapes=[
            pltpu.VMEM((size, tokens, width), LOW),
            pltpu.VMEM((size,) + combine_rows.shape, WIDE),
            pltpu.VMEM(gu_full.shape, LOW),
            pltpu.VMEM(down_full.shape, LOW),
            pltpu.VMEM((per_unit, length, 128), WIDE),
            pltpu.VMEM((per_unit, length, ff2), WIDE if length <= 2048 else LOW),
            pltpu.VMEM((per_unit, length, ff), LOW),
            pltpu.VMEM((per_unit, length, ff2), LOW),
            pltpu.VMEM((2 * tokens, width), WIDE),
            pltpu.VMEM((size, tokens, width), LOW),
            pltpu.VMEM((4, tokens, width), LOW),
            pltpu.VMEM((size, 8, tokens), WIDE),
            pltpu.VMEM((2, size // 2, tokens, width), LOW),
            pltpu.VMEM((2, size // 2, tokens, width), LOW),
            dma(steps + (2,)), dma(steps + (2,)), dma(steps + (2,)), dma(steps + (2,)),
            dma(steps), dma(steps), dma(steps), dma(steps),
            dma((size,)), dma((size,)), dma((4,)),
        ],
        compiler_params=pltpu.CompilerParams(
            collective_id=collective, has_side_effects=True, vmem_limit_bytes=63 << 20
        ),
        name="run_experts",
    )(expert_input, combine_rows, upstream, gu_full, down_full)


class Spread:
    def __init__(self, size, source, slab, sems, gathered=False):
        self.size, self.source, self.slab, self.gathered = size, source, slab, gathered
        self.send_a, self.recv_a, self.send_b, self.recv_b, self.own = sems
        self.me, self.seq = lax.axis_index("ctx"), lax.axis_index("seq")

    def _from(self, k):
        return (self.me + self.size - k) % self.size

    def local(self):
        return pltpu.make_async_copy(self.source(self.me), self.slab(self.seq * self.size + self.me), self.own)

    def outward(self, k):
        there = (self.me + k) % self.size
        slab = self.slab(self.seq * self.size + self.me)
        return push(self.source(there), slab, self.send_a.at[k], self.recv_a.at[k], ctx=there)

    def inward(self, k):
        here = self._from(k)
        slab = self.slab(self.seq * self.size + here)
        return push(self.source(here), slab, self.send_a.at[k], self.recv_a.at[k], ctx=here)

    def sideways(self, which, k):
        owner = row_mate(self.seq) if which == 2 else self.seq
        slab = self.slab(owner * self.size + self._from(k))
        mate = row_mate(self.seq) if which == 1 else core_mate(self.seq)
        return push(slab, slab, self.send_b.at[which, k], self.recv_b.at[which, k], seq=mate)

    def landing(self, which, k):
        owner = (core_mate(self.seq), row_mate(self.seq), core_mate(row_mate(self.seq)))[which]
        slab = self.slab(owner * self.size + self._from(k))
        return push(slab, slab, self.send_b.at[which, k], self.recv_b.at[which, k], seq=core_mate(self.seq))

    def start(self):
        for k in range(1, self.size):
            self.outward(k).start()

    def step(self, k):
        if k == 0:
            self.local().wait()
        elif not self.gathered:
            self.inward(k).wait_recv()
        self.sideways(1, k).start()
        self.sideways(0, k).start()
        if k and not self.gathered:
            self.pass_on(k - 1)

    def pass_on(self, k):
        self.landing(1, k).wait_recv()
        self.sideways(2, k).start()

    def land(self):
        for k in range(self.size):
            self.landing(0, k).wait_recv()
            self.landing(2, k).wait_recv()

    def drain(self):
        for k in range(self.size):
            for which in range(3):
                self.sideways(which, k).wait_send()
            if k and not self.gathered:
                self.outward(k).wait_send()

    @staticmethod
    def scratch(size):
        dma = pltpu.SemaphoreType.DMA
        return [dma((size,)), dma((size,)), dma((3, size)), dma((3, size)), dma]


def front_kernel(
    size, split, tile,
    tokens_in, upstream, docs_in, cos_turned, sin_turned, pack, gu_pack, down_pack, out_rows,
    inputs_all, upstream_all, mixed, query_pair, key_value, out_pair, log_total, docs_row, docs_col, places_row,
    cosine, sine, row_scale, head_weight, small, gu_full, down_full, out_full,
    docs_all, pack_all, key_pad, value_turned, head_out,
    send_t, recv_t, send_n, recv_n, send_x, recv_x, own, *scratch,
):
    me, seq = lax.axis_index("ctx"), lax.axis_index("seq")
    lane, row, number = me % split, me // split, size // split
    tokens, width = tokens_in.shape
    steps = size // 2
    place = ring_place(me, size)
    greet(
        [{"ctx": (me + k) % size} for k in range(1, size)]
        + [{"seq": core_mate(seq)}, {"seq": row_mate(seq)}]
    )
    heads = Spread(size, lambda c: pack.at[c], lambda owner: pack_all.at[owner], scratch[0:5])
    bulk = [
        Spread(size, lambda c: gu_pack.at[c], lambda owner: gu_full.at[:, owner], scratch[5:10]),
        Spread(size, lambda c: down_pack.at[c], lambda owner: down_full.at[:, owner], scratch[10:15]),
    ]
    out = Spread(size, lambda c: out_rows, lambda owner: out_full.at[owner], scratch[15:20], True)
    lines = LineGather(
        size, out_rows, lambda owner, viewer: out_full.at[seq * size + owner], scratch[20:24]
    )
    ring = RingGather(size, tokens_in, inputs_all, send_t, recv_t)
    lines_up = LineGather(
        size, upstream, lambda owner, viewer: upstream_all.at[slot_seen(owner, viewer, size)], scratch[24:28]
    )

    def note(k):
        return push(docs_in, docs_all.at[me], send_n.at[k], recv_n.at[k], ctx=(me + k) % size)

    def noted(k):
        here = (me + size - k) % size
        return push(docs_in, docs_all.at[here], send_n.at[k], recv_n.at[k], ctx=here)

    def send_bulk(turn):
        for k in range(2 * turn + 1, min(2 * turn + 3, size)):
            for part in bulk:
                part.outward(k).start()

    heads.start()
    for k in range(1, size):
        note(k).start()
    lines.start()
    ring.start(0)
    heads.local().start()
    local = [
        pltpu.make_async_copy(tokens_in, inputs_all.at[me], own.at[0]),
        pltpu.make_async_copy(upstream, upstream_all.at[0], own.at[1]),
    ]
    for copy in local:
        copy.start()
    for part in bulk + [out]:
        part.local().start()
    docs_all[me] = docs_in[...]

    def tables(i, _):
        rows = pl.ds(pl.multiple_of(i * tile, tile), tile)
        cos, sin = cos_turned[:, rows], sin_turned[:, rows]
        cosine[rows] = jnp.concatenate([cos] * 4, axis=0).T
        sine[rows] = jnp.concatenate([-sin, sin] * 2, axis=0).T
        return 0

    lax.fori_loop(0, size * tokens // tile, tables, 0)
    for k in range(size):
        heads.step(k)
    heads.pass_on(size - 1)
    for part in bulk + [out]:
        part.step(0)
    lines.turn(1)
    ring.start(1)
    send_bulk(0)
    for k in range(1, size):
        noted(k).wait_recv()
    log_total[...] = jnp.zeros_like(log_total)

    def documents(c, _):
        rows = pl.ds(pl.multiple_of(c * tokens, tokens), tokens)
        docs_col[rows] = docs_all[c].astype(WIDE).T[:, 0:1].astype(jnp.int32)
        return 0

    lax.fori_loop(0, size, documents, 0)

    def my_documents(b, _):
        rows = pl.ds(pl.multiple_of(b * tokens, tokens), tokens)
        docs_row[:, rows] = docs_all[b * split + lane]
        first = (b * split + lane) * tokens
        places_row[:, rows] = lax.broadcasted_iota(jnp.int32, (8, tokens), 1) + first
        return 0

    lax.fori_loop(0, number, my_documents, 0)
    heads.land()
    whole = pack_all[...].astype(WIDE).reshape(width, pack_all.shape[2])
    head_weight[...] = whole[:, :HEAD_COLS].astype(LOW)
    small[...] = whole[:, HEAD_COLS:].T[: small.shape[0]]
    gain_row = small.shape[0] - 8
    for copy in local:
        copy.wait()

    half = lax.broadcasted_iota(jnp.int32, (tokens, 2 * HEAD_DIM), 1) < HEAD_DIM

    def project(spot):
        owner = ring_member(spot, size)
        rows = pl.ds(pl.multiple_of(owner * tokens, tokens), tokens)
        values = inputs_all[owner].astype(WIDE)
        scale_one = lax.rsqrt(jnp.mean(values * values, axis=-1, keepdims=True) + NORM_EPS)
        row_scale[rows] = scale_one
        attend = (values * scale_one * small[gain_row : gain_row + 1]).astype(LOW)
        pre = dot_nn(attend, head_weight[...])
        cos, sin = cosine[rows], sine[rows]
        query, pair = pre[:, : 2 * HEAD_DIM], pre[:, 2 * HEAD_DIM :]
        query = query * cos + swap_halves(query) * sin
        pair = pair * jnp.where(half, cos, 1.0) + swap_halves(pair) * jnp.where(half, sin, 0.0)
        key_value[rows] = pair.astype(LOW)
        key_pad[0, rows] = jnp.where(half, pair, 0.0).astype(LOW)
        key_pad[1, rows] = jnp.where(half, 0.0, pltpu.roll(pair, HEAD_DIM, 1)).astype(LOW)
        value_turned[:, rows] = pair.T[HEAD_DIM:].astype(LOW)

        @pl.when(owner % split == lane)
        def _():
            query_pair[pl.ds(pl.multiple_of(owner // split * tokens, tokens), tokens)] = query.astype(LOW)

    project(place)

    def visit(turn, _):
        for step in range(1, steps):
            @pl.when(turn == step)
            def _():
                if step > 1:
                    ring.start(step)
                if step < steps - 1:
                    lines.turn(step + 1)
                else:
                    lines.finish()
                    for k in range(1, size):
                        out.step(k)
                send_bulk(step)
                if step == steps - 1:
                    lines_up.start()
                for k in range(2 * step - 3, 2 * step - 1):
                    for part in bulk if k > 0 else []:
                        part.step(k)

        def side(way, _):
            project(place + (2 * way - 1) * turn)
            return 0

        return lax.fori_loop(0, 2, side, 0)

    lax.fori_loop(1, steps, visit, 0)
    ring.land()
    project(place + steps)

    todo = [functools.partial(out.pass_on, k) for k in range(size)]
    todo.append(functools.partial(lines_up.turn, 1))
    for k in range(size - 3, size):
        todo += [functools.partial(part.step, k) for part in bulk]
        if k < size - 1:
            todo.append(functools.partial(lines_up.turn, k - size + 5))
    todo += [functools.partial(lines_up.turn, k) for k in range(4, steps)]

    def pump(count):
        for _ in range(min(count, len(todo))):
            todo.pop(0)()

    scale = HEAD_DIM**-0.5
    for i in range(number * tokens // tile):
        rows = pl.ds(i * tile, tile)
        query = query_pair[rows]
        query_doc, query_place = docs_row[0:1, rows], places_row[0:1, rows]

        def pairs(j, carry):
            keys = pl.ds(pl.multiple_of(j * tile, tile), tile)
            spot = lax.broadcasted_iota(jnp.int32, (tile, tile), 0) + j * tile
            allowed = (spot <= query_place) & (docs_col[keys] == query_doc)
            found = []
            for h in range(GROUP):
                peak, total, gathered = carry[3 * h : 3 * h + 3]
                score = jnp.where(allowed, dot_nt(key_pad[h, keys], query) * scale, NEG_BIG)
                higher = jnp.maximum(peak, jnp.max(score, axis=0, keepdims=True))
                keep = jnp.exp(peak - higher)
                prob = jnp.exp(score - higher)
                total = total * keep + jnp.sum(prob, axis=0, keepdims=True)
                gathered = gathered * keep + dot_nn(value_turned[:, keys], prob.astype(LOW))
                found += [higher, total, gathered]
            return tuple(found)

        empty = (
            jnp.full((1, tile), NEG_BIG, WIDE), jnp.zeros((1, tile), WIDE), jnp.zeros((HEAD_DIM, tile), WIDE)
        )
        found = lax.fori_loop(0, min(size * tokens // tile, (i + 1) * split), pairs, empty * GROUP)
        for h in range(GROUP):
            log_total[h : h + 1, rows] = found[3 * h] + jnp.log(found[3 * h + 1])
        result = jnp.concatenate([found[3 * h + 2] / found[3 * h + 1] for h in range(GROUP)], axis=0).T
        out_pair[rows] = result
        blocks = tile // tokens
        head_out[pl.ds(i * blocks, blocks)] = result.astype(LOW).reshape(blocks, tokens, 2 * HEAD_DIM)
        pump(4)

    def seat(index):
        return mixed.at[:, pl.ds(pl.multiple_of(index * 2 * HEAD_DIM, 2 * HEAD_DIM), 2 * HEAD_DIM)]

    swaps = []
    for k in range(1, number):
        there = (row + k) % number
        swaps.append(push(head_out.at[there], seat(row), send_x.at[k], recv_x.at[k], ctx=there * split + lane))
        swaps[-1].start()
    mine = pltpu.make_async_copy(head_out.at[row], seat(row), own.at[2])
    mine.start()
    pump(len(todo))
    for part in bulk:
        part.pass_on(size - 1)
    lines_up.finish()
    for k in range(1, number):
        here = (row + number - k) % number
        push(head_out.at[here], seat(here), send_x.at[k], recv_x.at[k], ctx=here * split + lane).wait_recv()
    mine.wait()
    for part in bulk + [out]:
        part.land()
    for copy in swaps:
        copy.wait_send()
    for k in range(1, size):
        note(k).wait_send()
    ring.drain()
    lines.drain()
    lines_up.drain()
    for part in [heads, out] + bulk:
        part.drain()


def run_front(tokens_in, upstream, docs, cos_turned, sin_turned, pack, gu_pack, down_pack, out_rows, split, owners, small_rows,
              collective):
    size = pack.shape[0]
    tokens, width = tokens_in.shape
    length, mine = size * tokens, size * tokens // split
    tile = 2 * tokens
    dma = pltpu.SemaphoreType.DMA
    vmem = pl.BlockSpec(memory_space=pltpu.VMEM)
    anywhere = pl.BlockSpec(memory_space=pl.ANY)
    pair = 2 * HEAD_DIM
    per_unit = gu_pack.shape[1]
    shape = jax.ShapeDtypeStruct
    return pl.pallas_call(
        functools.partial(front_kernel, size, split, tile),
        out_shape=[
            shape((size, tokens, width), LOW), shape((size, tokens, width), LOW),
            shape((tokens, HEADS * HEAD_DIM), LOW), shape((mine, pair), LOW), shape((length, pair), LOW),
            shape((mine, pair), WIDE), shape((8, mine), WIDE), shape((8, mine), jnp.int32),
            shape((length, 1), jnp.int32), shape((8, mine), jnp.int32),
            shape((length, pair), WIDE), shape((length, pair), WIDE), shape((length, 1), WIDE),
            shape((width, HEAD_COLS), LOW), shape((small_rows, width), WIDE),
            shape((per_unit, owners) + gu_pack.shape[2:], LOW),
            shape((per_unit, owners) + down_pack.shape[2:], LOW),
            shape((owners,) + out_rows.shape, LOW),
        ],
        in_specs=[vmem] * 9,
        out_specs=[vmem, anywhere] + [vmem] * 13 + [anywhere] * 3,
        scratch_shapes=[
            pltpu.VMEM((size, 8, tokens), jnp.int32),
            pltpu.VMEM((owners,) + pack.shape[1:], LOW),
            pltpu.VMEM((GROUP, length, pair), LOW),
            pltpu.VMEM((HEAD_DIM, length), LOW),
            pltpu.VMEM((size // split, tokens, pair), LOW),
            dma((2, size // 2, 2)), dma((2, size // 2, 2)),
            dma((size,)), dma((size,)), dma((size // split,)), dma((size // split,)), dma((3,)),
        ] + Spread.scratch(size) * 4 + LineGather.scratch(size) * 2,
        compiler_params=pltpu.CompilerParams(
            collective_id=collective, has_side_effects=True, vmem_limit_bytes=60 << 20
        ),
        name="run_front",
    )(tokens_in, upstream, docs, cos_turned, sin_turned, pack, gu_pack, down_pack, out_rows)


class Homing:
    def __init__(self, size, grads, out, bufs, sems):
        self.size, self.grads, self.out = size, grads, out
        self.near, self.from_core, self.from_row, self.to_row, self.to_home = bufs
        self.load, self.send_a, self.recv_a, self.send_b, self.recv_b, self.send_c, self.recv_c = sems
        self.me, self.seq = lax.axis_index("ctx"), lax.axis_index("seq")

    def _block(self, s0, k):
        index = s0 * self.size + (self.me + k) % self.size
        return self.grads.at[:, index] if self.grads.ndim == 4 else self.grads.at[index]

    def _row(self, which):
        return row_mate(self.seq) if which == 0 else self.seq

    def fetch(self, which, k):
        return pltpu.make_async_copy(self._block(self._row(which), k), self.near.at[which, k], self.load.at[which, k])

    def to_core(self, which, k):
        return push(
            self._block(core_mate(self._row(which)), k), self.from_core.at[which, k],
            self.send_a.at[which, k], self.recv_a.at[which, k], seq=core_mate(self.seq),
        )

    def across(self, k):
        return push(
            self.to_row.at[k], self.from_row.at[k], self.send_b.at[k], self.recv_b.at[k], seq=row_mate(self.seq)
        )

    def homeward(self, k):
        there = (self.me + k) % self.size
        return push(self.to_home.at[k], self.out.at[self.me], self.send_c.at[k], self.recv_c.at[k], ctx=there)

    def arriving(self, k):
        here = (self.me + self.size - k) % self.size
        return push(self.to_home.at[k], self.out.at[here], self.send_c.at[k], self.recv_c.at[k], ctx=here)

    def start(self):
        def body(k, _):
            for which in range(2):
                self.to_core(which, k).start()
                self.fetch(which, k).start()
            return 0

        lax.fori_loop(0, self.size, body, 0)

    def first(self, k):
        self.fetch(0, k).wait()
        self.to_core(0, k).wait_recv()
        sum_into(self.to_row.at[k], [self.near.at[0, k], self.from_core.at[0, k]])
        self.across(k).start()

    def second(self, k, home=False):
        self.fetch(1, k).wait()
        self.to_core(1, k).wait_recv()
        self.across(k).wait_recv()
        target = self.out.at[self.me] if home else self.to_home.at[k]
        sum_into(target, [self.near.at[1, k], self.from_core.at[1, k], self.from_row.at[k]])
        if not home:
            self.homeward(k).start()

    def close(self):
        def body(k, _):
            self.arriving(k).wait_recv()
            self.homeward(k).wait_send()
            return 0

        lax.fori_loop(1, self.size, body, 0)

        def drain(k, _):
            self.to_core(0, k).wait_send()
            self.to_core(1, k).wait_send()
            self.across(k).wait_send()
            return 0

        lax.fori_loop(0, self.size, drain, 0)

    @staticmethod
    def scratch(size, block):
        slab = (size,) + block
        dma = pltpu.SemaphoreType.DMA
        return [
            pltpu.VMEM((2,) + slab, LOW), pltpu.VMEM((2,) + slab, LOW), pltpu.VMEM(slab, LOW),
            pltpu.VMEM(slab, LOW), pltpu.VMEM(slab, LOW),
            dma((2, size)), dma((2, size)), dma((2, size)), dma((size,)), dma((size,)), dma((size,)), dma((size,)),
        ]


class SmallSum:
    def __init__(self, size, small, out, from_seq, total, from_ctx, sems):
        self.size, self.small, self.out = size, small, out
        self.from_seq, self.total, self.from_ctx = from_seq, total, from_ctx
        self.send_a, self.recv_a, self.send_b, self.recv_b = sems
        self.me, self.seq = lax.axis_index("ctx"), lax.axis_index("seq")

    def _swap(self, k):
        there = (self.seq + k) % 4
        return push(self.small.at[there], self.from_seq.at[k], self.send_a.at[k], self.recv_a.at[k], seq=there)

    def _tell(self, k):
        there = (self.me + k) % self.size
        return push(self.total, self.from_ctx.at[self.me], self.send_b.at[k], self.recv_b.at[k], ctx=there)

    def _hear(self, k):
        here = (self.me + self.size - k) % self.size
        return push(self.total, self.from_ctx.at[here], self.send_b.at[k], self.recv_b.at[k], ctx=here)

    def start(self):
        for k in range(1, 4):
            self._swap(k).start()

    def middle(self):
        for k in range(1, 4):
            self._swap(k).wait_recv()
        self.total[...] = self.small[self.seq] + self.from_seq[1] + self.from_seq[2] + self.from_seq[3]
        for k in range(1, self.size):
            self._tell(k).start()

    def finish(self):
        total = self.total[...]
        for k in range(1, self.size):
            self._hear(k).wait_recv()
            total = total + self.from_ctx[(self.me + self.size - k) % self.size]
        self.out[...] = total
        for k in range(1, 4):
            self._swap(k).wait_send()
        for k in range(1, self.size):
            self._tell(k).wait_send()

    @staticmethod
    def scratch(size, rows, lanes):
        dma = pltpu.SemaphoreType.DMA
        part = (rows, lanes // 4)
        return [
            pltpu.VMEM((4,) + part, WIDE), pltpu.VMEM(part, WIDE), pltpu.VMEM((size,) + part, WIDE),
            dma((4,)), dma((4,)), dma((size,)), dma((size,)),
        ]


def back_kernel(
    size, split, tile,
    mixed_grad, gu_grads, down_grads, mixed_low, project_grad, small, query_pair, key_value, out_pair, log_total,
    docs_row, docs_col, places_row, cosine, sine, gain, inputs_all, row_scale, head_weight,
    attend_sum, gu_home, down_home, out_home, head_home, small_home,
    head_grad, key_pad, value_pad, key_acc, value_acc, query_acc, heads_grad, heads_turned, head_part, small_full,
    attend_own, held, out_grads, send_r, recv_r, send_x, recv_x, own_x, *scratch,
):
    me, seq = lax.axis_index("ctx"), lax.axis_index("seq")
    lane, row, number = me % split, me // split, size // split
    tokens = mixed_grad.shape[0]
    length, width = inputs_all.shape

    def heads_of(index):
        return mixed_grad.at[:, pl.ds(pl.multiple_of(index * 2 * HEAD_DIM, 2 * HEAD_DIM), 2 * HEAD_DIM)]

    greet(
        [{"ctx": (me + k) % size} for k in range(1, size)]
        + [{"seq": (seq + k) % 4} for k in range(1, 4)]
    )

    def homing(i, grads, out):
        part = scratch[12 * i : 12 * i + 12]
        return Homing(size, grads, out, part[:5], part[5:])

    early = [homing(0, gu_grads, gu_home), homing(1, down_grads, down_home), homing(2, out_grads, out_home)]
    late = homing(3, head_part, head_home)
    tail = scratch[48:]
    total_small = SmallSum(size, small_full, small_home, tail[0], tail[1], tail[2], tail[3:])

    mine = pltpu.make_async_copy(heads_of(row), head_grad.at[row], own_x)
    mine.start()
    swaps = []
    for k in range(1, number):
        there = (row + k) % number
        swaps.append(
            push(heads_of(there), head_grad.at[row], send_x.at[k], recv_x.at[k], ctx=there * split + lane)
        )
        swaps[-1].start()
    for home in early[:2]:
        home.start()

    def out_tile(j, _):
        cols = pl.ds(pl.multiple_of(j * tile, tile), tile)
        depth = out_grads.shape[1]
        part = dot_tn(mixed_low[:, cols], project_grad[...]).reshape(tile // depth, depth, width)
        out_grads[pl.ds(j * (tile // depth), tile // depth)] = part.astype(LOW)
        return 0

    lax.fori_loop(0, width // tile, out_tile, 0)
    early[2].start()

    steps = []
    for k in range(size):
        steps += [functools.partial(home.first, k) for home in early]
    for k in range(1, size):
        steps += [functools.partial(home.second, k) for home in early]
    steps += [functools.partial(home.second, 0, True) for home in early]

    def pump(count):
        for _ in range(min(count, len(steps))):
            steps.pop(0)()

    half = lax.broadcasted_iota(jnp.int32, (tile, 2 * HEAD_DIM), 1) < HEAD_DIM
    zero = jnp.zeros((tile, 2 * HEAD_DIM), WIDE)

    def prepare(i, _):
        rows = pl.ds(pl.multiple_of(i * tile, tile), tile)
        pair = key_value[rows].astype(WIDE)
        turned = pltpu.roll(pair, HEAD_DIM, 1)
        key_pad[0, rows] = jnp.where(half, pair, zero).astype(LOW)
        key_pad[1, rows] = jnp.where(half, zero, turned).astype(LOW)
        value_pad[0, rows] = jnp.where(half, turned, zero).astype(LOW)
        value_pad[1, rows] = jnp.where(half, zero, pair).astype(LOW)
        key_acc[rows] = zero
        value_acc[rows] = zero
        heads_grad[rows, pl.ds(0, 2 * HEAD_DIM)] = zero.astype(LOW)
        return 0

    lax.fori_loop(0, length // tile, prepare, 0)
    for k in range(1, number):
        here = (row + number - k) % number
        push(heads_of(here), head_grad.at[here], send_x.at[k], recv_x.at[k], ctx=here * split + lane).wait_recv()
    mine.wait()

    scale = HEAD_DIM**-0.5
    blocks = tile // tokens
    for i in range(number * tokens // tile):
        rows = pl.ds(i * tile, tile)
        query = query_pair[rows]
        grad = head_grad[pl.ds(i * blocks, blocks)].reshape(tile, 2 * HEAD_DIM)
        product = (grad.astype(WIDE) * out_pair[rows].astype(WIDE)).T
        deltas = [
            jnp.sum(product[h * HEAD_DIM : (h + 1) * HEAD_DIM], axis=0, keepdims=True) for h in range(GROUP)
        ]
        query_doc, query_place = docs_row[0:1, rows], places_row[0:1, rows]
        totals = [log_total[h : h + 1, rows] for h in range(GROUP)]
        query_acc[...] = zero

        def pairs(j, _):
            keys = pl.ds(pl.multiple_of(j * tile, tile), tile)
            place = lax.broadcasted_iota(jnp.int32, (tile, tile), 0) + j * tile
            allowed = (place <= query_place) & (docs_col[keys] == query_doc)
            key_part, value_part, query_part = zero, zero, zero
            for h in range(GROUP):
                mine_half = half if h == 0 else jnp.logical_not(half)
                score = dot_nt(key_pad[h, keys], query)
                prob = jnp.where(allowed, jnp.exp(score * scale - totals[h]), 0.0)
                slope = dot_nt(value_pad[h, keys], grad)
                ds = (prob * (slope - deltas[h])).astype(LOW)
                value_part = jnp.where(mine_half, dot_nn(prob.astype(LOW), grad), value_part)
                key_part = jnp.where(mine_half, dot_nn(ds, query), key_part)
                query_part = query_part + dot_tn(ds, key_pad[h, keys])
            key_acc[keys] += key_part
            value_acc[keys] += value_part
            query_acc[...] += query_part
            return 0

        lax.fori_loop(0, min(length // tile, (i + 1) * split), pairs, 0)
        turn = query_acc[...] * scale
        for b in range(blocks):
            at = pl.ds(pl.multiple_of(((i * blocks + b) * split + lane) * tokens, tokens), tokens)
            piece = turn[b * tokens : (b + 1) * tokens]
            heads_grad[at, pl.ds(0, 2 * HEAD_DIM)] = unturn(piece, cosine, sine, at, 0).astype(LOW)
        pump(6)

    def fold(i, _):
        rows = pl.ds(pl.multiple_of(i * tile, tile), tile)
        key_part, value_part = key_acc[rows], value_acc[rows]
        key_part = (key_part + pltpu.roll(key_part, HEAD_DIM, 1)) * scale
        value_part = value_part + pltpu.roll(value_part, HEAD_DIM, 1)
        both = jnp.where(half, key_part, value_part)
        heads_grad[rows, pl.ds(2 * HEAD_DIM, 2 * HEAD_DIM)] = unturn(both, cosine, sine, rows, 1).astype(LOW)
        return 0

    lax.fori_loop(0, length // tile, fold, 0)

    def transpose(i, _):
        rows = pl.ds(pl.multiple_of(i * tile, tile), tile)
        heads_turned[:, rows] = heads_grad[rows].astype(WIDE).T.astype(LOW)
        return 0

    lax.fori_loop(0, length // tile, transpose, 0)

    reduce = RingReduce(size, held, send_r, recv_r)
    small_full[...] = small[...]
    gain_row = small.shape[1] - 8

    def attend(place, slot):
        owner = ring_member(place, size)
        rows = pl.ds(pl.multiple_of(owner * tokens, tokens), tokens)
        part = dot_nt(heads_grad[rows], head_weight[...])
        attend_own[slot] = part.astype(LOW)
        normed = inputs_all[rows].astype(WIDE) * row_scale[rows]
        share = jnp.sum(part * normed, axis=0, keepdims=True)
        lanes = width // 4
        for s0 in range(4):
            small_full[s0, gain_row : gain_row + 1] += share[:, s0 * lanes : (s0 + 1) * lanes]

    place = ring_place(me, size)
    half_ring = size // 2
    attend(place + half_ring, 0)
    reduce.start(0, [attend_own.at[0]] * 2)
    for step in range(1, half_ring):
        attend(place + half_ring - step, 1)
        attend(place - half_ring + step, 2)
        if step == 1:
            def columns(j, _):
                cols = pl.ds(pl.multiple_of(j * tile, tile), tile)
                normed = inputs_all[:, cols].astype(WIDE) * row_scale[...]
                part = dot_nn(heads_turned[...], (normed * gain[gain.shape[0] - 8 : gain.shape[0] - 7, cols]).astype(LOW)).T.astype(LOW)
                depth = head_part.shape[1]
                head_part[pl.ds(j * (tile // depth), tile // depth)] = part.reshape(tile // depth, depth, HEAD_COLS)
                return 0

            lax.fori_loop(0, width // tile, columns, 0)
            late.start()
        reduce.start(step, [attend_own.at[1], attend_own.at[2]])
        pump(3)
    attend(place, 1)
    total_small.start()
    for k in range(size):
        late.first(k)
    pump(len(steps))
    total_small.middle()
    for k in range(1, size):
        late.second(k)
    late.second(0, True)
    reduce.finish(attend_sum, attend_own.at[1], attend_own.at[0])
    for home in early:
        home.close()
    late.close()
    total_small.finish()
    for copy in swaps:
        copy.wait_send()


def swap_halves(values):
    lane = lax.broadcasted_iota(jnp.int32, values.shape, 1) % HEAD_DIM
    return jnp.where(
        lane < HEAD_DIM // 2,
        pltpu.roll(values, values.shape[1] - HEAD_DIM // 2, 1),
        pltpu.roll(values, HEAD_DIM // 2, 1),
    )


def unturn(values, cosine, sine, rows, which):
    cos, sin = cosine[rows], sine[rows]
    if which:
        half = lax.broadcasted_iota(jnp.int32, values.shape, 1) < HEAD_DIM
        cos, sin = jnp.where(half, cos, 1.0), jnp.where(half, sin, 0.0)
    return values * cos - swap_halves(values) * sin


def attention_back(arrays, size, split, collective):
    (mixed_grad, gu_grads, down_grads, mixed_low, project_grad, small, query_pair, key_value, out_pair, log_total,
     docs_row, docs_col, places_row, cosine, sine, gain, inputs_all, row_scale, head_weight) = arrays
    tokens = mixed_grad.shape[0]
    length, width = inputs_all.shape
    tile = 2 * tokens
    out_shape = (4 * size, gu_grads.shape[2], width)
    blocks = [
        (gu_grads.shape[0],) + gu_grads.shape[2:], (down_grads.shape[0],) + down_grads.shape[2:],
        out_shape[1:], (out_shape[1], HEAD_COLS),
    ]
    small_rows = small.shape[1]
    dma = pltpu.SemaphoreType.DMA
    vmem = pl.BlockSpec(memory_space=pltpu.VMEM)
    anywhere = pl.BlockSpec(memory_space=pl.ANY)
    pair = (length, 2 * HEAD_DIM)
    scratch = [
        pltpu.VMEM((size // split, tokens, 2 * HEAD_DIM), LOW),
        pltpu.VMEM((GROUP,) + pair, LOW), pltpu.VMEM((GROUP,) + pair, LOW),
        pltpu.VMEM(pair, WIDE), pltpu.VMEM(pair, WIDE), pltpu.VMEM((tile, 2 * HEAD_DIM), WIDE),
        pltpu.VMEM((length, HEAD_COLS), LOW), pltpu.VMEM((HEAD_COLS, length), LOW),
        pltpu.VMEM(out_shape[:2] + (HEAD_COLS,), LOW),
        pltpu.VMEM(small.shape, WIDE),
        pltpu.VMEM((3, tokens, width), LOW), pltpu.VMEM((2, size // 2, tokens, width), LOW),
        pltpu.VMEM(out_shape, LOW),
        dma((2, size // 2)), dma((2, size // 2)), dma((size // split,)), dma((size // split,)), dma,
    ]
    for block in blocks:
        scratch += Homing.scratch(size, block)
    scratch += SmallSum.scratch(size, small_rows, width)
    return pl.pallas_call(
        functools.partial(back_kernel, size, split, tile),
        out_shape=[jax.ShapeDtypeStruct((tokens, width), WIDE)]
        + [jax.ShapeDtypeStruct((size,) + block, LOW) for block in blocks]
        + [jax.ShapeDtypeStruct((small_rows, width // 4), WIDE)],
        in_specs=[vmem, anywhere, anywhere] + [vmem] * 16,
        out_specs=[vmem] * 6,
        scratch_shapes=scratch,
        compiler_params=pltpu.CompilerParams(
            collective_id=collective, has_side_effects=True, vmem_limit_bytes=62 << 20
        ),
        name="attention_back",
    )(*arrays)


def rms_scale(values):
    return lax.rsqrt(jnp.mean(values * values, axis=-1, keepdims=True) + NORM_EPS)


def rope_tables(places, factor):
    freqs = 1.0 / ROPE_BASE ** (jnp.arange(0, HEAD_DIM, 2).astype(WIDE) / HEAD_DIM)
    angles = (places.astype(WIDE) / factor)[None, :] * freqs[:, None]
    return jnp.cos(angles), jnp.sin(angles)


def dot(equation, left, right):
    return jnp.einsum(equation, left, right, preferred_element_type=WIDE)


def on_device(
    layer_input, document_ids, expert_routes, rope_factor, attention_gain, feedforward_gain,
    query_weight, key_weight, value_weight, output_weight, router_weight, gate_up, down_weight, cotangent,
):
    nseq, nctx = lax.axis_size("seq"), lax.axis_size("ctx")
    tokens, width = layer_input.shape[1:]
    length = tokens * nctx
    rows, experts, ff2 = gate_up.shape
    ff = ff2 // 2
    down_rows = down_weight.shape[0]
    per_unit = max(1, experts // nctx)
    ff_split = max(1, nctx // experts)
    ff_part = ff // ff_split
    head_split = nctx // KV_HEADS
    unit = lax.axis_index("ctx")
    owners = nseq * nctx

    if ff_split == 1:
        gu_pack = gate_up.astype(LOW).transpose(1, 0, 2).reshape(nctx, per_unit, rows, ff2)
    else:
        gu_pack = (
            gate_up.astype(LOW).reshape(rows, experts, 2, ff_split, ff_part).transpose(1, 3, 0, 2, 4)
            .reshape(nctx, per_unit, rows, 2 * ff_part)
        )
    down_pack = jnp.repeat(
        down_weight.astype(LOW).transpose(1, 0, 2), ff_split, axis=0
    ).reshape(nctx, per_unit, down_rows, width)
    head_pack = jnp.concatenate(
        [
            query_weight.reshape(rows, KV_HEADS, GROUP * HEAD_DIM),
            key_weight.reshape(rows, KV_HEADS, HEAD_DIM),
            value_weight.reshape(rows, KV_HEADS, HEAD_DIM),
        ],
        axis=-1,
    ).astype(LOW).transpose(1, 0, 2)
    head_pack = jnp.repeat(head_pack, head_split, axis=0)
    small_rows = experts + 8
    small_pack = jnp.concatenate(
        [router_weight, attention_gain[:, None], feedforward_gain[:, None], jnp.zeros((rows, 110 + 16 - experts), WIDE)],
        axis=1,
    ).astype(LOW)
    small_pack = jnp.broadcast_to(small_pack[None], (nctx,) + small_pack.shape)
    pack = jnp.concatenate([head_pack, small_pack], axis=2)
    documents = jnp.broadcast_to(document_ids.reshape(1, tokens), (8, tokens))
    cos_turned, sin_turned = rope_tables(jnp.arange(length, dtype=jnp.int32), rope_factor[0])

    (inputs_all, upstream_all, mixed_low, query_pair, key_value, out_pair, log_total, docs_row, docs_col, places_row,
     cosine, sine, row_scale, head_full, small_full, gu_full, down_full, out_full) = run_front(
        layer_input[0], cotangent[0], documents, cos_turned, sin_turned, pack, gu_pack, down_pack,
        output_weight.astype(LOW), head_split, owners, small_rows, 1,
    )
    gu_full = gu_full.reshape(per_unit, width, 2 * ff_part)
    down_full = down_full.reshape(per_unit, ff, width)
    if ff_split > 1:
        down_full = lax.dynamic_slice_in_dim(down_full, (unit % ff_split) * ff_part, ff_part, 1)
    out_full = out_full.reshape(HEADS * HEAD_DIM, width)
    router_full = small_full[:experts].astype(LOW)
    gain_one, gain_two = small_full[experts], small_full[experts + 1]

    inputs = layer_input[0].astype(WIDE)
    middle = inputs + dot("tj,jd->td", mixed_low, out_full)
    scale_two = rms_scale(middle)
    normed_two = middle * scale_two
    expert_input = (normed_two * gain_two).astype(LOW)
    logits = dot("td,ed->te", expert_input, router_full)
    chosen = jnp.any(
        expert_routes[0][:, :, None] == jnp.arange(experts, dtype=jnp.int32)[None, None, :], axis=1
    )
    picked = jnp.where(chosen, logits, NEG_BIG)
    expo_gate = jnp.where(chosen, jnp.exp(picked - jnp.max(picked, axis=-1, keepdims=True)), 0.0)
    combine = expo_gate / jnp.sum(expo_gate, axis=-1, keepdims=True)

    mix, back_sum, gate_grad_all, gu_grads, down_grads = run_experts(
        expert_input, combine.T, upstream_all, gu_full, down_full, nctx, ff_split, owners, down_rows, 3
    )

    layer_output = (middle + mix).astype(LOW)[None]
    upstream = cotangent[0].astype(WIDE)
    gate_grad = gate_grad_all[:, :per_unit].reshape(experts, ff_split, tokens).sum(axis=1).T
    gate_grad = jnp.where(chosen, gate_grad, 0.0)
    select_grad = combine * (gate_grad - jnp.sum(combine * gate_grad, axis=-1, keepdims=True))
    logit_grad = select_grad.astype(LOW)
    back_two = back_sum + dot("te,ed->td", logit_grad, router_full)
    router_part = dot("te,td->ed", logit_grad, expert_input)
    gain_two_part = jnp.sum(back_two * normed_two, axis=0)
    normed_two_grad = back_two * gain_two
    middle_grad = upstream + scale_two * (
        normed_two_grad - normed_two * jnp.mean(normed_two_grad * normed_two, axis=-1, keepdims=True)
    )
    project_grad = middle_grad.astype(LOW)
    mixed_grad = dot("td,jd->tj", project_grad, out_full).astype(LOW)

    small_grads = jnp.concatenate(
        [router_part, gain_two_part[None], jnp.zeros((31 - experts, width), WIDE)], axis=0
    ).reshape(32, nseq, width // nseq).transpose(1, 0, 2)
    if ff_split > 1:
        down_grads = lax.dynamic_update_slice_in_dim(
            jnp.zeros((per_unit, owners, down_rows, width), LOW), down_grads,
            (unit % ff_split) * (ff_part // down_rows), 1,
        )
    attend_sum, gu_home, down_home, out_home, head_home, small_home = attention_back(
        [
            mixed_grad,
            gu_grads,
            down_grads,
            mixed_low, project_grad,
            small_grads,
            query_pair, key_value, out_pair, log_total, docs_row, docs_col, places_row,
            cosine, sine, small_full, inputs_all.reshape(length, width), row_scale, head_full,
        ],
        nctx, head_split, 7,
    )
    out_home, head_home = out_home.astype(WIDE), head_home.astype(WIDE)
    if ff_split == 1:
        gate_up_gradient = lax.optimization_barrier(gu_home.reshape(experts, rows, ff2).transpose(1, 0, 2)).astype(WIDE)
        down_gradient = lax.optimization_barrier(
            down_home.reshape(experts, down_rows, width).transpose(1, 0, 2)
        ).astype(WIDE)
    else:
        gate_up_gradient = (
            gu_home.astype(WIDE).reshape(experts, ff_split, rows, 2, ff_part).transpose(2, 0, 3, 1, 4)
            .reshape(rows, experts, ff2)
        )
        down_gradient = down_home.astype(WIDE).reshape(experts, ff_split, down_rows, width).sum(axis=1).transpose(1, 0, 2)
    output_gradient = out_home.sum(axis=0)
    head_home = head_home.reshape(KV_HEADS, head_split, rows, HEAD_COLS).sum(axis=1).transpose(1, 0, 2)
    query_gradient = head_home[..., : GROUP * HEAD_DIM].reshape(rows, HEADS * HEAD_DIM)
    key_gradient = head_home[..., GROUP * HEAD_DIM : -HEAD_DIM].reshape(rows, KV_HEADS * HEAD_DIM)
    value_gradient = head_home[..., -HEAD_DIM:].reshape(rows, KV_HEADS * HEAD_DIM)
    small_home = lax.dynamic_slice_in_dim(small_home, unit * rows, rows, axis=1)
    router_gradient = small_home[:experts].T

    scale_one = rms_scale(inputs)
    normed_one = inputs * scale_one
    normed_one_grad = attend_sum * gain_one
    input_gradient = (
        middle_grad
        + scale_one
        * (normed_one_grad - normed_one * jnp.mean(normed_one_grad * normed_one, axis=-1, keepdims=True))
    ).astype(LOW)[None]
    return (
        layer_output, input_gradient, small_home[24], small_home[experts],
        query_gradient, key_gradient, value_gradient, output_gradient, router_gradient,
        gate_up_gradient, down_gradient,
    )


def solution(mesh):
    both = ("seq", "ctx")
    return jax.shard_map(
        on_device,
        mesh=mesh,
        in_specs=(
            P("seq", "ctx", None), P("seq", "ctx"), P("seq", "ctx", None), P(), P(both), P(both),
            P(both, None), P(both, None), P(both, None), P(both, None), P(both, None),
            P(both, None, None), P(both, None, None), P("seq", "ctx", None),
        ),
        out_specs=(
            P("seq", "ctx", None), P("seq", "ctx", None), P(both), P(both),
            P(both, None), P(both, None), P(both, None), P(both, None), P(both, None),
            P(both, None, None), P(both, None, None),
        ),
        check_vma=False,
    )
```

```python
import functools
import math

import jax
import jax.numpy as jnp
from jax import lax
from jax.experimental import pallas as pl
from jax.experimental.pallas import tpu as pltpu
from jax.sharding import PartitionSpec as P

HEADS = 16
KV_HEADS = 8
HEAD_DIM = 64
GROUP = HEADS // KV_HEADS
HEAD_COLS = (GROUP + 2) * HEAD_DIM

NORM_EPS = 1e-06
ROPE_BASE = 10000.0
NEG_BIG = -1e30
LOW = jnp.bfloat16
WIDE = jnp.float32
MESH = pl.DeviceIdType.MESH


def ring_place(index, size):
    half = index // 2
    return half + (index % 2) * (size - 1 - 2 * half)


def ring_member(place, size):
    place = (place + 2 * size) % size
    far = place // (size // 2)
    return 2 * place + far * (2 * size - 1 - 4 * place)


def slot_of(distance, size):
    if distance == 0:
        return 0
    if abs(distance) == size // 2:
        return 1
    return 2 * abs(distance) + (distance > 0)


def slot_seen(owner, viewer, size):
    half = size // 2
    ahead = (ring_place(owner, size) - ring_place(viewer, size) + 2 * size) % size
    far = ahead // half
    plain = (2 * ahead + 1) * (1 - far) + 2 * (size - ahead) * far
    same = (size - ahead) // size
    opposite = (size - (ahead + half) % size) // size
    return plain - same - (size - 1) * opposite


def core_mate(index):
    return index + 1 - 2 * (index % 2)


def row_mate(index):
    return (index + 2) % 4


def push(src, dst, send, recv, **where):
    return pltpu.make_async_remote_copy(
        src_ref=src, dst_ref=dst, send_sem=send, recv_sem=recv, device_id=where, device_id_type=MESH
    )


def greet(peers):
    barrier = pltpu.get_barrier_semaphore()
    for where in peers:
        pl.semaphore_signal(barrier, inc=1, device_id=where, device_id_type=MESH)
    pl.semaphore_wait(barrier, len(peers))


def ring_peers(size):
    place = ring_place(lax.axis_index("ctx"), size)
    return ring_member(place + 1, size), ring_member(place - 1, size)


class RingGather:
    def __init__(self, size, source, target, send, recv, relative=False):
        self.size, self.source, self.target, self.send, self.recv = size, source, target, send, recv
        self.relative = relative
        self.place = ring_place(lax.axis_index("ctx"), size)
        self.right, self.left = ring_peers(size)
        self.steps = size // 2

    def _copy(self, way, step, piece, arriving):
        sign = 2 * way - 1
        rows = self.source.shape[0]
        part = pl.ds(piece * (rows // 2), rows // 2)
        if self.relative:
            here, there = slot_of(sign * step, self.size), slot_of(sign * (step + 1), self.size)
        else:
            here = there = ring_member(self.place + sign * (step + arriving), self.size)
        dst = self.target.at[there, part]
        src = self.target.at[here, part] if step else self.source.at[part]
        where = self.left if way else self.right
        send, recv = self.send.at[way, step, piece], self.recv.at[way, step, piece]
        return push(dst if arriving else src, dst, send, recv, ctx=where)

    def start(self, step):
        for piece in range(2):
            for way in range(2):
                if step:
                    self._copy(way, step - 1, piece, 1).wait_recv()
                if step < self.steps - 1 or piece == way:
                    self._copy(way, step, piece, 0).start()

    def land(self):
        for way in range(2):
            self._copy(way, self.steps - 1, way, 1).wait_recv()

    def drain(self):
        for way in range(2):
            for step in range(self.steps):
                for piece in range(2) if step < self.steps - 1 else [way]:
                    self._copy(way, step, piece, 0).wait_send()

    def finish(self):
        self.land()
        self.drain()


class LineGather:
    def __init__(self, size, source, slab, sems):
        self.source, self.slab, self.count = source, slab, size // 2
        self.send, self.recv, self.send_m, self.recv_m = sems
        self.me = lax.axis_index("ctx")
        self.spot, self.side = self.me // 2, self.me % 2
        self.mate = core_mate(self.me)

    def _line(self, way, step):
        owner = self.me - 2 * step if way == 0 else self.me + 2 * step
        there = self.me + 2 if way == 0 else self.me - 2
        source = self.slab(owner, self.me) if step else self.source
        return push(source, self.slab(owner, there), self.send.at[way, step], self.recv.at[way, step], ctx=there)

    def _arriving(self, way, step):
        owner = self.me - 2 * step - 2 if way == 0 else self.me + 2 * step + 2
        here = self.slab(owner, self.me)
        return push(here, here, self.send.at[way, step], self.recv.at[way, step], ctx=self.mate)

    def _across(self, spot, own=False):
        owner = 2 * spot + self.side
        source = self.source if own else self.slab(owner, self.me)
        return push(
            source, self.slab(owner, self.mate), self.send_m.at[spot], self.recv_m.at[spot], ctx=self.mate
        )

    def _sends(self, way, step):
        if way == 0:
            return (self.spot + 1 < self.count) & (self.spot >= step)
        return (self.spot >= 1) & (self.spot + step < self.count)

    def start(self):
        for way in range(2):
            pl.when(self._sends(way, 0))(self._line(way, 0).start)
        self._across(self.spot, True).start()

    def turn(self, step):
        for way in range(2):
            there = self.spot >= step if way == 0 else self.spot + step < self.count

            @pl.when(there)
            def _():
                self._arriving(way, step - 1).wait_recv()
                self._across(self.spot - step if way == 0 else self.spot + step).start()

            pl.when(self._sends(way, step))(self._line(way, step).start)

    def finish(self):
        for spot in range(self.count):
            owner = 2 * spot + 1 - self.side
            here = self.slab(owner, self.me)
            push(here, here, self.send_m.at[spot], self.recv_m.at[spot], ctx=self.mate).wait_recv()

    def drain(self):
        for spot in range(self.count):
            self._across(spot).wait_send()
        for way in range(2):
            for step in range(self.count - 1):
                pl.when(self._sends(way, step))(self._line(way, step).wait_send)

    @staticmethod
    def scratch(size):
        dma, count = pltpu.SemaphoreType.DMA, size // 2
        return [dma((2, count)), dma((2, count)), dma((count,)), dma((count,))]


def row_step(rows):
    return rows if rows < 16 else 16


def sum_into(target, parts):
    rows = target.shape[-2]
    step = row_step(rows)

    def add_at(lead):
        def body(r, _):
            at = lead + (pl.ds(pl.multiple_of(r * step, step), step),)
            total = parts[0][at].astype(WIDE)
            for part in parts[1:]:
                total = total + part[at].astype(WIDE)
            target[at] = total.astype(target.dtype)
            return 0

        lax.fori_loop(0, rows // step, body, 0)

    for lead in [()] if target.ndim == 2 else [(u,) for u in range(target.shape[0])]:
        add_at(lead)


def dot_nn(a, b):
    return lax.dot_general(a, b, (((1,), (0,)), ((), ())), preferred_element_type=WIDE)


def dot_nt(a, b):
    return lax.dot_general(a, b, (((1,), (1,)), ((), ())), preferred_element_type=WIDE)


def dot_tn(a, b):
    return lax.dot_general(a, b, (((0,), (0,)), ((), ())), preferred_element_type=WIDE)


class RingReduce:
    def __init__(self, size, held, send, recv):
        self.size, self.held, self.send, self.recv = size, held, send, recv
        self.place = ring_place(lax.axis_index("ctx"), size)
        self.right, self.left = ring_peers(size)
        self.steps = size // 2
        self.rows = held.shape[2]

    def owner(self, way, step):
        ahead = self.steps - step
        return ring_member(self.place + ahead if way == 0 else self.place - ahead, self.size)

    def _copy(self, way, step, source):
        half = self.rows // 2
        part = pl.ds(0, self.rows) if step else pl.ds(half * way, half)
        where = self.right if way == 0 else self.left
        return push(
            source, self.held.at[way, step, part], self.send.at[way, step], self.recv.at[way, step], ctx=where
        )

    def start(self, step, own):
        for way in range(2):
            half = self.rows // 2
            near = pl.ds(0, half) if way == 0 else pl.ds(half, half)
            far = pl.ds(half, half) if way == 0 else pl.ds(0, half)
            source = own[way].at[near]
            if step:
                self._copy(way, step - 1, source).wait_recv()
                source = self.held.at[way, step - 1]
                if step == 1:
                    sum_into(source.at[near], [own[way].at[near], source.at[near]])
                    sum_into(source.at[far], [own[way].at[far]])
                else:
                    sum_into(source, [own[way], source])
            self._copy(way, step, source).start()

    def finish(self, target, own, first):
        last, half = self.steps - 1, self.rows // 2
        for way in range(2):
            self._copy(way, last, self.held.at[way, last]).wait_recv()
        sum_into(target, [own, self.held.at[0, last], self.held.at[1, last]])
        for way in range(2):
            for step in range(self.steps):
                source = self.held.at[way, step - 1] if step else first.at[pl.ds(half * way, half)]
                self._copy(way, step, source).wait_send()


def expert_kernel(
    size, split,
    expert_input, combine_rows, upstream, gu_hbm, down_hbm,
    mix, back_sum, gate_home, gu_grads, down_grads,
    tokens_all, combine_all, gu_weight, down_weight, combine_cols, gate_up, hidden, both_grad, out_acc, out_own,
    back_own, gate_send, held_out, held_back,
    send_b, recv_b, send_c, recv_c, send_y, recv_y, send_d, recv_d, send_g, recv_g, own_sem,
):
    me = lax.axis_index("ctx")
    place = ring_place(me, size)
    per_unit, width, ff2 = gu_weight.shape
    ff = ff2 // 2
    tokens = expert_input.shape[0]
    group = 2 * tokens
    groups = size // 2
    first_expert = me // split * per_unit
    greet([{"ctx": (me + k) % size} for k in range(1, size)])

    loads = [
        pltpu.make_async_copy(expert_input, tokens_all.at[0], own_sem.at[0]),
        pltpu.make_async_copy(combine_rows, combine_all.at[0], own_sem.at[1]),
        pltpu.make_async_copy(gu_hbm, gu_weight, own_sem.at[2]),
        pltpu.make_async_copy(down_hbm, down_weight, own_sem.at[3]),
    ]
    rings = [
        RingGather(size, combine_rows, combine_all, send_c, recv_c, True),
        RingGather(size, expert_input, tokens_all, send_b, recv_b, True),
    ]
    for ring in rings:
        ring.start(0)
    for load in loads:
        load.start()
    for load in loads:
        load.wait()
    lanes = lax.broadcasted_iota(jnp.int32, (group, 128), 1)

    def forward(turn, _):
        for step in range(1, groups):
            @pl.when(turn == step - 1)
            def _():
                for ring in rings:
                    ring.start(step)

        @pl.when(turn == groups - 1)
        def _():
            for ring in rings:
                ring.land()

        g = (turn + 1) % groups
        pair = pl.ds(2 * g, 2)
        rows = pl.ds(pl.multiple_of(g * group, group), group)
        token = tokens_all[pair].reshape(group, width)
        up_wide = upstream[pair].reshape(group, width).astype(WIDE)
        weights = jnp.concatenate([combine_all[2 * g].T, combine_all[2 * g + 1].T], axis=0)
        names = lax.broadcasted_iota(jnp.int32, weights.shape, 1)
        out_acc[...] = jnp.zeros_like(out_acc)

        def one(e, gates):
            weight = jnp.sum(jnp.where(names == first_expert + e, weights, 0.0), axis=1, keepdims=True)
            combine_cols[e, rows] = jnp.broadcast_to(weight, (group, 128))
            both = dot_nn(token, gu_weight[e])
            gate_up[e, rows] = both.astype(gate_up.dtype)
            gate, up = both[:, :ff], both[:, ff:]
            hid = (gate / (1.0 + jnp.exp(-gate)) * up).astype(LOW)
            hidden[e, rows] = hid
            produced = dot_nn(hid, down_weight[e])
            out_acc[...] += weight * produced
            dg = jnp.sum(up_wide * produced, axis=1, keepdims=True)
            return jnp.where(lanes == e, dg, gates)

        gates = lax.fori_loop(0, per_unit, one, jnp.zeros((group, 128), WIDE)).T
        gate_send[2 * g] = gates[:8, :tokens]
        gate_send[2 * g + 1] = gates[:8, tokens:]
        out_own[pair] = out_acc[...].astype(LOW).reshape(2, tokens, width)
        return 0

    lax.fori_loop(0, groups, forward, 0)

    def gate_copy(distance):
        there = ring_member(place + distance, size)
        k = distance % size
        return push(gate_send.at[slot_of(distance, size)], gate_home.at[me], send_g.at[k], recv_g.at[k], ctx=there)

    distances = [d for d in range(1 - groups, groups + 1) if d]
    for distance in distances:
        gate_copy(distance).start()
    gate_home[me] = gate_send[0]

    ring_out = RingReduce(size, held_out, send_y, recv_y)
    ring_back = RingReduce(size, held_back, send_d, recv_d)

    def backward(turn, _):
        for step in range(groups):
            @pl.when(turn == step)
            def _():
                ring_out.start(
                    step, [out_own.at[slot_of(groups - step, size)], out_own.at[slot_of(step - groups, size)]]
                )

        g = (groups - turn) % groups
        pair = pl.ds(2 * g, 2)
        rows = pl.ds(pl.multiple_of(g * group, group), group)
        up_wide = upstream[pair].reshape(group, width).astype(WIDE)
        out_acc[...] = jnp.zeros_like(out_acc)

        def one(e, _):
            weight = combine_cols[e, rows][:, 0:1]
            grad = (weight * up_wide).astype(LOW)
            hid_grad = dot_nt(grad, down_weight[e])
            gate = gate_up[e, rows, pl.ds(0, ff)].astype(WIDE)
            up = gate_up[e, rows, pl.ds(ff, ff)].astype(WIDE)
            sigmoid = 1.0 / (1.0 + jnp.exp(-gate))
            gate_part = (hid_grad * up * sigmoid * (1.0 + gate * (1.0 - sigmoid))).astype(LOW)
            up_part = (hid_grad * (gate * sigmoid)).astype(LOW)
            both_grad[e, rows, pl.ds(0, ff)] = gate_part
            both_grad[e, rows, pl.ds(ff, ff)] = up_part
            out_acc[...] += dot_nt(both_grad[e, rows], gu_weight[e])
            return 0

        lax.fori_loop(0, per_unit, one, 0)
        near = 2 * ((g + groups - 1) // groups)
        back_own[pl.ds(near, 2)] = out_acc[...].astype(LOW).reshape(2, tokens, width)
        for step in range(groups):
            @pl.when(turn == step)
            def _():
                ring_back.start(step, [back_own.at[1]] * 2 if step == 0 else [back_own.at[3], back_own.at[2]])
        return 0

    lax.fori_loop(0, groups, backward, 0)

    tile = 256
    length = size * tokens

    def gu_tile(j, _):
        turned = tokens_all[:, :, pl.ds(pl.multiple_of(j * tile, tile), tile)].reshape(length, tile)
        turned = turned.astype(WIDE).T.astype(LOW)
        depth = gu_grads.shape[2]
        count = tile // depth

        def one(e, _):
            part = dot_nn(turned, both_grad[e]).reshape(count, depth, ff2)
            gu_grads[e, pl.ds(j * count, count)] = part.astype(LOW)
            return 0

        return lax.fori_loop(0, per_unit, one, 0)

    lax.fori_loop(0, width // tile, gu_tile, 0)

    def down_tile(index, _):
        e, j = index // (ff // tile), index % (ff // tile)
        turned = hidden[e, :, pl.ds(pl.multiple_of(j * tile, tile), tile)].astype(WIDE).T.astype(LOW)
        depth = down_grads.shape[2]
        count = tile // depth
        for half in range(2):
            cols = pl.ds(half * (width // 2), width // 2)
            grad = upstream[:, :, cols].reshape(length, width // 2).astype(WIDE) * combine_cols[e][:, 0:1]
            part = dot_nn(turned, grad.astype(LOW)).reshape(count, depth, width // 2)
            down_grads[e, pl.ds(j * count, count), :, cols] = part.astype(LOW)
        return 0

    lax.fori_loop(0, per_unit * (ff // tile), down_tile, 0)

    ring_back.finish(back_sum, back_own.at[0], back_own.at[1])
    ring_out.finish(mix, out_own.at[0], out_own.at[1])
    for ring in rings:
        ring.drain()
    for distance in distances:
        here = ring_member(place - distance, size)
        k = distance % size
        push(gate_send.at[0], gate_home.at[here], send_g.at[k], recv_g.at[k], ctx=here).wait_recv()
        gate_copy(distance).wait_send()


def run_experts(expert_input, combine_rows, upstream, gu_full, down_full, size, split, owners, down_rows, collective):
    tokens, width = expert_input.shape
    per_unit, _, ff2 = gu_full.shape
    ff = ff2 // 2
    length = size * tokens
    dma = pltpu.SemaphoreType.DMA
    vmem = pl.BlockSpec(memory_space=pltpu.VMEM)
    anywhere = pl.BlockSpec(memory_space=pl.ANY)
    steps = (2, size // 2)
    return pl.pallas_call(
        functools.partial(expert_kernel, size, split),
        out_shape=[
            jax.ShapeDtypeStruct((tokens, width), WIDE),
            jax.ShapeDtypeStruct((tokens, width), WIDE),
            jax.ShapeDtypeStruct((size, 8, tokens), WIDE),
            jax.ShapeDtypeStruct((per_unit, owners, width // owners, ff2), LOW),
            jax.ShapeDtypeStruct((per_unit, ff // down_rows, down_rows, width), LOW),
        ],
        in_specs=[vmem, vmem, vmem, anywhere, anywhere],
        out_specs=[vmem] * 5,
        scratch_shapes=[
            pltpu.VMEM((size, tokens, width), LOW),
            pltpu.VMEM((size,) + combine_rows.shape, WIDE),
            pltpu.VMEM(gu_full.shape, LOW),
            pltpu.VMEM(down_full.shape, LOW),
            pltpu.VMEM((per_unit, length, 128), WIDE),
            pltpu.VMEM((per_unit, length, ff2), WIDE if length <= 2048 else LOW),
            pltpu.VMEM((per_unit, length, ff), LOW),
            pltpu.VMEM((per_unit, length, ff2), LOW),
            pltpu.VMEM((2 * tokens, width), WIDE),
            pltpu.VMEM((size, tokens, width), LOW),
            pltpu.VMEM((4, tokens, width), LOW),
            pltpu.VMEM((size, 8, tokens), WIDE),
            pltpu.VMEM((2, size // 2, tokens, width), LOW),
            pltpu.VMEM((2, size // 2, tokens, width), LOW),
            dma(steps + (2,)), dma(steps + (2,)), dma(steps + (2,)), dma(steps + (2,)),
            dma(steps), dma(steps), dma(steps), dma(steps),
            dma((size,)), dma((size,)), dma((4,)),
        ],
        compiler_params=pltpu.CompilerParams(
            collective_id=collective, has_side_effects=True, vmem_limit_bytes=63 << 20
        ),
        name="run_experts",
    )(expert_input, combine_rows, upstream, gu_full, down_full)


class Spread:
    def __init__(self, size, source, slab, sems, gathered=False):
        self.size, self.source, self.slab, self.gathered = size, source, slab, gathered
        self.send_a, self.recv_a, self.send_b, self.recv_b, self.own = sems
        self.me, self.seq = lax.axis_index("ctx"), lax.axis_index("seq")

    def _from(self, k):
        return (self.me + self.size - k) % self.size

    def local(self):
        return pltpu.make_async_copy(self.source(self.me), self.slab(self.seq * self.size + self.me), self.own)

    def outward(self, k):
        there = (self.me + k) % self.size
        slab = self.slab(self.seq * self.size + self.me)
        return push(self.source(there), slab, self.send_a.at[k], self.recv_a.at[k], ctx=there)

    def inward(self, k):
        here = self._from(k)
        slab = self.slab(self.seq * self.size + here)
        return push(self.source(here), slab, self.send_a.at[k], self.recv_a.at[k], ctx=here)

    def sideways(self, which, k):
        owner = row_mate(self.seq) if which == 2 else self.seq
        slab = self.slab(owner * self.size + self._from(k))
        mate = row_mate(self.seq) if which == 1 else core_mate(self.seq)
        return push(slab, slab, self.send_b.at[which, k], self.recv_b.at[which, k], seq=mate)

    def landing(self, which, k):
        owner = (core_mate(self.seq), row_mate(self.seq), core_mate(row_mate(self.seq)))[which]
        slab = self.slab(owner * self.size + self._from(k))
        return push(slab, slab, self.send_b.at[which, k], self.recv_b.at[which, k], seq=core_mate(self.seq))

    def start(self):
        for k in range(1, self.size):
            self.outward(k).start()

    def step(self, k):
        if k == 0:
            self.local().wait()
        elif not self.gathered:
            self.inward(k).wait_recv()
        self.sideways(1, k).start()
        self.sideways(0, k).start()
        if k and not self.gathered:
            self.pass_on(k - 1)

    def pass_on(self, k):
        self.landing(1, k).wait_recv()
        self.sideways(2, k).start()

    def land(self):
        for k in range(self.size):
            self.landing(0, k).wait_recv()
            self.landing(2, k).wait_recv()

    def drain(self):
        for k in range(self.size):
            for which in range(3):
                self.sideways(which, k).wait_send()
            if k and not self.gathered:
                self.outward(k).wait_send()

    @staticmethod
    def scratch(size):
        dma = pltpu.SemaphoreType.DMA
        return [dma((size,)), dma((size,)), dma((3, size)), dma((3, size)), dma]


def front_kernel(
    size, split, tile,
    tokens_in, upstream, docs_in, cos_turned, sin_turned, pack, gu_pack, down_pack, out_rows,
    inputs_all, upstream_all, mixed, query_pair, key_value, out_pair, log_total, docs_row, docs_col, places_row,
    cosine, sine, row_scale, head_weight, small, gu_full, down_full, out_full,
    docs_all, pack_all, key_pad, value_turned, head_out,
    send_t, recv_t, send_n, recv_n, send_x, recv_x, own, *scratch,
):
    me, seq = lax.axis_index("ctx"), lax.axis_index("seq")
    lane, row, number = me % split, me // split, size // split
    tokens, width = tokens_in.shape
    steps = size // 2
    place = ring_place(me, size)
    greet(
        [{"ctx": (me + k) % size} for k in range(1, size)]
        + [{"seq": core_mate(seq)}, {"seq": row_mate(seq)}]
    )
    heads = Spread(size, lambda c: pack.at[c], lambda owner: pack_all.at[owner], scratch[0:5])
    bulk = [
        Spread(size, lambda c: gu_pack.at[c], lambda owner: gu_full.at[:, owner], scratch[5:10]),
        Spread(size, lambda c: down_pack.at[c], lambda owner: down_full.at[:, owner], scratch[10:15]),
    ]
    out = Spread(size, lambda c: out_rows, lambda owner: out_full.at[owner], scratch[15:20], True)
    lines = LineGather(
        size, out_rows, lambda owner, viewer: out_full.at[seq * size + owner], scratch[20:24]
    )
    ring = RingGather(size, tokens_in, inputs_all, send_t, recv_t)
    lines_up = LineGather(
        size, upstream, lambda owner, viewer: upstream_all.at[slot_seen(owner, viewer, size)], scratch[24:28]
    )

    def note(k):
        return push(docs_in, docs_all.at[me], send_n.at[k], recv_n.at[k], ctx=(me + k) % size)

    def noted(k):
        here = (me + size - k) % size
        return push(docs_in, docs_all.at[here], send_n.at[k], recv_n.at[k], ctx=here)

    def send_bulk(turn):
        for k in range(2 * turn + 1, min(2 * turn + 3, size)):
            for part in bulk:
                part.outward(k).start()

    heads.start()
    for k in range(1, size):
        note(k).start()
    lines.start()
    ring.start(0)
    heads.local().start()
    local = [
        pltpu.make_async_copy(tokens_in, inputs_all.at[me], own.at[0]),
        pltpu.make_async_copy(upstream, upstream_all.at[0], own.at[1]),
    ]
    for copy in local:
        copy.start()
    for part in bulk + [out]:
        part.local().start()
    docs_all[me] = docs_in[...]

    def tables(i, _):
        rows = pl.ds(pl.multiple_of(i * tile, tile), tile)
        cos, sin = cos_turned[:, rows], sin_turned[:, rows]
        cosine[rows] = jnp.concatenate([cos] * 4, axis=0).T
        sine[rows] = jnp.concatenate([-sin, sin] * 2, axis=0).T
        return 0

    lax.fori_loop(0, size * tokens // tile, tables, 0)
    for k in range(size):
        heads.step(k)
    heads.pass_on(size - 1)
    for part in bulk + [out]:
        part.step(0)
    lines.turn(1)
    ring.start(1)
    send_bulk(0)
    for k in range(1, size):
        noted(k).wait_recv()
    log_total[...] = jnp.zeros_like(log_total)

    def documents(c, _):
        rows = pl.ds(pl.multiple_of(c * tokens, tokens), tokens)
        docs_col[rows] = docs_all[c].astype(WIDE).T[:, 0:1].astype(jnp.int32)
        return 0

    lax.fori_loop(0, size, documents, 0)

    def my_documents(b, _):
        rows = pl.ds(pl.multiple_of(b * tokens, tokens), tokens)
        docs_row[:, rows] = docs_all[b * split + lane]
        first = (b * split + lane) * tokens
        places_row[:, rows] = lax.broadcasted_iota(jnp.int32, (8, tokens), 1) + first
        return 0

    lax.fori_loop(0, number, my_documents, 0)
    heads.land()
    whole = pack_all[...].astype(WIDE).reshape(width, pack_all.shape[2])
    head_weight[...] = whole[:, :HEAD_COLS].astype(LOW)
    small[...] = whole[:, HEAD_COLS:].T[: small.shape[0]]
    gain_row = small.shape[0] - 8
    for copy in local:
        copy.wait()

    half = lax.broadcasted_iota(jnp.int32, (tokens, 2 * HEAD_DIM), 1) < HEAD_DIM

    def project(spot):
        owner = ring_member(spot, size)
        rows = pl.ds(pl.multiple_of(owner * tokens, tokens), tokens)
        values = inputs_all[owner].astype(WIDE)
        scale_one = lax.rsqrt(jnp.mean(values * values, axis=-1, keepdims=True) + NORM_EPS)
        row_scale[rows] = scale_one
        attend = (values * scale_one * small[gain_row : gain_row + 1]).astype(LOW)
        pre = dot_nn(attend, head_weight[...])
        cos, sin = cosine[rows], sine[rows]
        query, pair = pre[:, : 2 * HEAD_DIM], pre[:, 2 * HEAD_DIM :]
        query = query * cos + swap_halves(query) * sin
        pair = pair * jnp.where(half, cos, 1.0) + swap_halves(pair) * jnp.where(half, sin, 0.0)
        key_value[rows] = pair.astype(LOW)
        key_pad[0, rows] = jnp.where(half, pair, 0.0).astype(LOW)
        key_pad[1, rows] = jnp.where(half, 0.0, pltpu.roll(pair, HEAD_DIM, 1)).astype(LOW)
        value_turned[:, rows] = pair.T[HEAD_DIM:].astype(LOW)

        @pl.when(owner % split == lane)
        def _():
            query_pair[pl.ds(pl.multiple_of(owner // split * tokens, tokens), tokens)] = query.astype(LOW)

    project(place)

    def visit(turn, _):
        for step in range(1, steps):
            @pl.when(turn == step)
            def _():
                if step > 1:
                    ring.start(step)
                if step < steps - 1:
                    lines.turn(step + 1)
                else:
                    lines.finish()
                    for k in range(1, size):
                        out.step(k)
                send_bulk(step)
                if step == steps - 1:
                    lines_up.start()
                for k in range(2 * step - 3, 2 * step - 1):
                    for part in bulk if k > 0 else []:
                        part.step(k)

        def side(way, _):
            project(place + (2 * way - 1) * turn)
            return 0

        return lax.fori_loop(0, 2, side, 0)

    lax.fori_loop(1, steps, visit, 0)
    ring.land()
    project(place + steps)

    todo = [functools.partial(out.pass_on, k) for k in range(size)]
    todo.append(functools.partial(lines_up.turn, 1))
    for k in range(size - 3, size):
        todo += [functools.partial(part.step, k) for part in bulk]
        if k < size - 1:
            todo.append(functools.partial(lines_up.turn, k - size + 5))
    todo += [functools.partial(lines_up.turn, k) for k in range(4, steps)]

    def pump(count):
        for _ in range(min(count, len(todo))):
            todo.pop(0)()

    scale = HEAD_DIM**-0.5
    for i in range(number * tokens // tile):
        rows = pl.ds(i * tile, tile)
        query = query_pair[rows]
        query_doc, query_place = docs_row[0:1, rows], places_row[0:1, rows]

        def pairs(j, carry):
            keys = pl.ds(pl.multiple_of(j * tile, tile), tile)
            spot = lax.broadcasted_iota(jnp.int32, (tile, tile), 0) + j * tile
            allowed = (spot <= query_place) & (docs_col[keys] == query_doc)
            found = []
            for h in range(GROUP):
                peak, total, gathered = carry[3 * h : 3 * h + 3]
                score = jnp.where(allowed, dot_nt(key_pad[h, keys], query) * scale, NEG_BIG)
                higher = jnp.maximum(peak, jnp.max(score, axis=0, keepdims=True))
                keep = jnp.exp(peak - higher)
                prob = jnp.exp(score - higher)
                total = total * keep + jnp.sum(prob, axis=0, keepdims=True)
                gathered = gathered * keep + dot_nn(value_turned[:, keys], prob.astype(LOW))
                found += [higher, total, gathered]
            return tuple(found)

        empty = (
            jnp.full((1, tile), NEG_BIG, WIDE), jnp.zeros((1, tile), WIDE), jnp.zeros((HEAD_DIM, tile), WIDE)
        )
        found = lax.fori_loop(0, min(size * tokens // tile, (i + 1) * split), pairs, empty * GROUP)
        for h in range(GROUP):
            log_total[h : h + 1, rows] = found[3 * h] + jnp.log(found[3 * h + 1])
        result = jnp.concatenate([found[3 * h + 2] / found[3 * h + 1] for h in range(GROUP)], axis=0).T
        out_pair[rows] = result
        blocks = tile // tokens
        head_out[pl.ds(i * blocks, blocks)] = result.astype(LOW).reshape(blocks, tokens, 2 * HEAD_DIM)
        pump(7)

    def seat(index):
        return mixed.at[:, pl.ds(pl.multiple_of(index * 2 * HEAD_DIM, 2 * HEAD_DIM), 2 * HEAD_DIM)]

    swaps = []
    for k in range(1, number):
        there = (row + k) % number
        swaps.append(push(head_out.at[there], seat(row), send_x.at[k], recv_x.at[k], ctx=there * split + lane))
        swaps[-1].start()
    mine = pltpu.make_async_copy(head_out.at[row], seat(row), own.at[2])
    mine.start()
    pump(len(todo))
    for part in bulk:
        part.pass_on(size - 1)
    lines_up.finish()
    for k in range(1, number):
        here = (row + number - k) % number
        push(head_out.at[here], seat(here), send_x.at[k], recv_x.at[k], ctx=here * split + lane).wait_recv()
    mine.wait()
    for part in bulk + [out]:
        part.land()
    for copy in swaps:
        copy.wait_send()
    for k in range(1, size):
        note(k).wait_send()
    ring.drain()
    lines.drain()
    lines_up.drain()
    for part in [heads, out] + bulk:
        part.drain()


def run_front(tokens_in, upstream, docs, cos_turned, sin_turned, pack, gu_pack, down_pack, out_rows, split, owners, small_rows,
              collective):
    size = pack.shape[0]
    tokens, width = tokens_in.shape
    length, mine = size * tokens, size * tokens // split
    tile = 2 * tokens
    dma = pltpu.SemaphoreType.DMA
    vmem = pl.BlockSpec(memory_space=pltpu.VMEM)
    anywhere = pl.BlockSpec(memory_space=pl.ANY)
    pair = 2 * HEAD_DIM
    per_unit = gu_pack.shape[1]
    shape = jax.ShapeDtypeStruct
    return pl.pallas_call(
        functools.partial(front_kernel, size, split, tile),
        out_shape=[
            shape((size, tokens, width), LOW), shape((size, tokens, width), LOW),
            shape((tokens, HEADS * HEAD_DIM), LOW), shape((mine, pair), LOW), shape((length, pair), LOW),
            shape((mine, pair), WIDE), shape((8, mine), WIDE), shape((8, mine), jnp.int32),
            shape((length, 1), jnp.int32), shape((8, mine), jnp.int32),
            shape((length, pair), WIDE), shape((length, pair), WIDE), shape((length, 1), WIDE),
            shape((width, HEAD_COLS), LOW), shape((small_rows, width), WIDE),
            shape((per_unit, owners) + gu_pack.shape[2:], LOW),
            shape((per_unit, owners) + down_pack.shape[2:], LOW),
            shape((owners,) + out_rows.shape, LOW),
        ],
        in_specs=[vmem] * 9,
        out_specs=[vmem, anywhere] + [vmem] * 13 + [anywhere] * 3,
        scratch_shapes=[
            pltpu.VMEM((size, 8, tokens), jnp.int32),
            pltpu.VMEM((owners,) + pack.shape[1:], LOW),
            pltpu.VMEM((GROUP, length, pair), LOW),
            pltpu.VMEM((HEAD_DIM, length), LOW),
            pltpu.VMEM((size // split, tokens, pair), LOW),
            dma((2, size // 2, 2)), dma((2, size // 2, 2)),
            dma((size,)), dma((size,)), dma((size // split,)), dma((size // split,)), dma((3,)),
        ] + Spread.scratch(size) * 4 + LineGather.scratch(size) * 2,
        compiler_params=pltpu.CompilerParams(
            collective_id=collective, has_side_effects=True, vmem_limit_bytes=60 << 20
        ),
        name="run_front",
    )(tokens_in, upstream, docs, cos_turned, sin_turned, pack, gu_pack, down_pack, out_rows)


class Homing:
    def __init__(self, size, grads, out, bufs, sems):
        self.size, self.grads, self.out = size, grads, out
        self.near, self.from_core, self.from_row, self.to_row, self.to_home = bufs
        self.load, self.send_a, self.recv_a, self.send_b, self.recv_b, self.send_c, self.recv_c = sems
        self.me, self.seq = lax.axis_index("ctx"), lax.axis_index("seq")

    def _block(self, s0, k):
        index = s0 * self.size + (self.me + k) % self.size
        return self.grads.at[:, index] if self.grads.ndim == 4 else self.grads.at[index]

    def _row(self, which):
        return row_mate(self.seq) if which == 0 else self.seq

    def fetch(self, which, k):
        return pltpu.make_async_copy(self._block(self._row(which), k), self.near.at[which, k], self.load.at[which, k])

    def to_core(self, which, k):
        return push(
            self._block(core_mate(self._row(which)), k), self.from_core.at[which, k],
            self.send_a.at[which, k], self.recv_a.at[which, k], seq=core_mate(self.seq),
        )

    def across(self, k):
        return push(
            self.to_row.at[k], self.from_row.at[k], self.send_b.at[k], self.recv_b.at[k], seq=row_mate(self.seq)
        )

    def homeward(self, k):
        there = (self.me + k) % self.size
        return push(self.to_home.at[k], self.out.at[self.me], self.send_c.at[k], self.recv_c.at[k], ctx=there)

    def arriving(self, k):
        here = (self.me + self.size - k) % self.size
        return push(self.to_home.at[k], self.out.at[here], self.send_c.at[k], self.recv_c.at[k], ctx=here)

    def start(self):
        def body(k, _):
            for which in range(2):
                self.to_core(which, k).start()
                self.fetch(which, k).start()
            return 0

        lax.fori_loop(0, self.size, body, 0)

    def first(self, k):
        self.fetch(0, k).wait()
        self.to_core(0, k).wait_recv()
        sum_into(self.to_row.at[k], [self.near.at[0, k], self.from_core.at[0, k]])
        self.across(k).start()

    def second(self, k, home=False):
        self.fetch(1, k).wait()
        self.to_core(1, k).wait_recv()
        self.across(k).wait_recv()
        target = self.out.at[self.me] if home else self.to_home.at[k]
        sum_into(target, [self.near.at[1, k], self.from_core.at[1, k], self.from_row.at[k]])
        if not home:
            self.homeward(k).start()

    def close(self):
        def body(k, _):
            self.arriving(k).wait_recv()
            self.homeward(k).wait_send()
            return 0

        lax.fori_loop(1, self.size, body, 0)

        def drain(k, _):
            self.to_core(0, k).wait_send()
            self.to_core(1, k).wait_send()
            self.across(k).wait_send()
            return 0

        lax.fori_loop(0, self.size, drain, 0)

    @staticmethod
    def scratch(size, block):
        slab = (size,) + block
        dma = pltpu.SemaphoreType.DMA
        return [
            pltpu.VMEM((2,) + slab, LOW), pltpu.VMEM((2,) + slab, LOW), pltpu.VMEM(slab, LOW),
            pltpu.VMEM(slab, LOW), pltpu.VMEM(slab, LOW),
            dma((2, size)), dma((2, size)), dma((2, size)), dma((size,)), dma((size,)), dma((size,)), dma((size,)),
        ]


class SmallSum:
    def __init__(self, size, small, out, from_seq, total, from_ctx, sems):
        self.size, self.small, self.out = size, small, out
        self.from_seq, self.total, self.from_ctx = from_seq, total, from_ctx
        self.send_a, self.recv_a, self.send_b, self.recv_b = sems
        self.me, self.seq = lax.axis_index("ctx"), lax.axis_index("seq")

    def _swap(self, k):
        there = (self.seq + k) % 4
        return push(self.small.at[there], self.from_seq.at[k], self.send_a.at[k], self.recv_a.at[k], seq=there)

    def _tell(self, k):
        there = (self.me + k) % self.size
        return push(self.total, self.from_ctx.at[self.me], self.send_b.at[k], self.recv_b.at[k], ctx=there)

    def _hear(self, k):
        here = (self.me + self.size - k) % self.size
        return push(self.total, self.from_ctx.at[here], self.send_b.at[k], self.recv_b.at[k], ctx=here)

    def start(self):
        for k in range(1, 4):
            self._swap(k).start()

    def middle(self):
        for k in range(1, 4):
            self._swap(k).wait_recv()
        self.total[...] = self.small[self.seq] + self.from_seq[1] + self.from_seq[2] + self.from_seq[3]
        for k in range(1, self.size):
            self._tell(k).start()

    def finish(self):
        total = self.total[...]
        for k in range(1, self.size):
            self._hear(k).wait_recv()
            total = total + self.from_ctx[(self.me + self.size - k) % self.size]
        self.out[...] = total
        for k in range(1, 4):
            self._swap(k).wait_send()
        for k in range(1, self.size):
            self._tell(k).wait_send()

    @staticmethod
    def scratch(size, rows, lanes):
        dma = pltpu.SemaphoreType.DMA
        part = (rows, lanes // 4)
        return [
            pltpu.VMEM((4,) + part, WIDE), pltpu.VMEM(part, WIDE), pltpu.VMEM((size,) + part, WIDE),
            dma((4,)), dma((4,)), dma((size,)), dma((size,)),
        ]


def back_kernel(
    size, split, tile,
    mixed_grad, gu_grads, down_grads, mixed_low, project_grad, small, query_pair, key_value, out_pair, log_total,
    docs_row, docs_col, places_row, cosine, sine, gain, inputs_all, row_scale, head_weight,
    attend_sum, gu_home, down_home, out_home, head_home, small_home,
    head_grad, key_pad, value_pad, key_acc, value_acc, query_acc, heads_grad, heads_turned, head_part, small_full,
    attend_own, held, out_grads, send_r, recv_r, send_x, recv_x, own_x, *scratch,
):
    me, seq = lax.axis_index("ctx"), lax.axis_index("seq")
    lane, row, number = me % split, me // split, size // split
    tokens = mixed_grad.shape[0]
    length, width = inputs_all.shape

    def heads_of(index):
        return mixed_grad.at[:, pl.ds(pl.multiple_of(index * 2 * HEAD_DIM, 2 * HEAD_DIM), 2 * HEAD_DIM)]

    greet(
        [{"ctx": (me + k) % size} for k in range(1, size)]
        + [{"seq": (seq + k) % 4} for k in range(1, 4)]
    )

    def homing(i, grads, out):
        part = scratch[12 * i : 12 * i + 12]
        return Homing(size, grads, out, part[:5], part[5:])

    early = [homing(0, gu_grads, gu_home), homing(1, down_grads, down_home), homing(2, out_grads, out_home)]
    late = homing(3, head_part, head_home)
    tail = scratch[48:]
    total_small = SmallSum(size, small_full, small_home, tail[0], tail[1], tail[2], tail[3:])

    mine = pltpu.make_async_copy(heads_of(row), head_grad.at[row], own_x)
    mine.start()
    swaps = []
    for k in range(1, number):
        there = (row + k) % number
        swaps.append(
            push(heads_of(there), head_grad.at[row], send_x.at[k], recv_x.at[k], ctx=there * split + lane)
        )
        swaps[-1].start()
    for home in early[:2]:
        home.start()

    def out_tile(j, _):
        cols = pl.ds(pl.multiple_of(j * tile, tile), tile)
        depth = out_grads.shape[1]
        part = dot_tn(mixed_low[:, cols], project_grad[...]).reshape(tile // depth, depth, width)
        out_grads[pl.ds(j * (tile // depth), tile // depth)] = part.astype(LOW)
        return 0

    lax.fori_loop(0, width // tile, out_tile, 0)
    early[2].start()

    steps = []
    for k in range(size):
        steps += [functools.partial(home.first, k) for home in early]
    for k in range(1, size):
        steps += [functools.partial(home.second, k) for home in early]
    steps += [functools.partial(home.second, 0, True) for home in early]

    def pump(count):
        for _ in range(min(count, len(steps))):
            steps.pop(0)()

    half = lax.broadcasted_iota(jnp.int32, (tile, 2 * HEAD_DIM), 1) < HEAD_DIM
    zero = jnp.zeros((tile, 2 * HEAD_DIM), WIDE)

    def prepare(i, _):
        rows = pl.ds(pl.multiple_of(i * tile, tile), tile)
        pair = key_value[rows].astype(WIDE)
        turned = pltpu.roll(pair, HEAD_DIM, 1)
        key_pad[0, rows] = jnp.where(half, pair, zero).astype(LOW)
        key_pad[1, rows] = jnp.where(half, zero, turned).astype(LOW)
        value_pad[0, rows] = jnp.where(half, turned, zero).astype(LOW)
        value_pad[1, rows] = jnp.where(half, zero, pair).astype(LOW)
        key_acc[rows] = zero
        value_acc[rows] = zero
        heads_grad[rows, pl.ds(0, 2 * HEAD_DIM)] = zero.astype(LOW)
        return 0

    lax.fori_loop(0, length // tile, prepare, 0)
    for k in range(1, number):
        here = (row + number - k) % number
        push(heads_of(here), head_grad.at[here], send_x.at[k], recv_x.at[k], ctx=here * split + lane).wait_recv()
    mine.wait()

    scale = HEAD_DIM**-0.5
    blocks = tile // tokens
    for i in range(number * tokens // tile):
        rows = pl.ds(i * tile, tile)
        query = query_pair[rows]
        grad = head_grad[pl.ds(i * blocks, blocks)].reshape(tile, 2 * HEAD_DIM)
        product = (grad.astype(WIDE) * out_pair[rows].astype(WIDE)).T
        deltas = [
            jnp.sum(product[h * HEAD_DIM : (h + 1) * HEAD_DIM], axis=0, keepdims=True) for h in range(GROUP)
        ]
        query_doc, query_place = docs_row[0:1, rows], places_row[0:1, rows]
        totals = [log_total[h : h + 1, rows] for h in range(GROUP)]
        query_acc[...] = zero

        def pairs(j, _):
            keys = pl.ds(pl.multiple_of(j * tile, tile), tile)
            place = lax.broadcasted_iota(jnp.int32, (tile, tile), 0) + j * tile
            allowed = (place <= query_place) & (docs_col[keys] == query_doc)
            key_part, value_part, query_part = zero, zero, zero
            for h in range(GROUP):
                mine_half = half if h == 0 else jnp.logical_not(half)
                score = dot_nt(key_pad[h, keys], query)
                prob = jnp.where(allowed, jnp.exp(score * scale - totals[h]), 0.0)
                slope = dot_nt(value_pad[h, keys], grad)
                ds = (prob * (slope - deltas[h])).astype(LOW)
                value_part = jnp.where(mine_half, dot_nn(prob.astype(LOW), grad), value_part)
                key_part = jnp.where(mine_half, dot_nn(ds, query), key_part)
                query_part = query_part + dot_tn(ds, key_pad[h, keys])
            key_acc[keys] += key_part
            value_acc[keys] += value_part
            query_acc[...] += query_part
            return 0

        lax.fori_loop(0, min(length // tile, (i + 1) * split), pairs, 0)
        turn = query_acc[...] * scale
        for b in range(blocks):
            at = pl.ds(pl.multiple_of(((i * blocks + b) * split + lane) * tokens, tokens), tokens)
            piece = turn[b * tokens : (b + 1) * tokens]
            heads_grad[at, pl.ds(0, 2 * HEAD_DIM)] = unturn(piece, cosine, sine, at, 0).astype(LOW)
        pump(6)

    def fold(i, _):
        rows = pl.ds(pl.multiple_of(i * tile, tile), tile)
        key_part, value_part = key_acc[rows], value_acc[rows]
        key_part = (key_part + pltpu.roll(key_part, HEAD_DIM, 1)) * scale
        value_part = value_part + pltpu.roll(value_part, HEAD_DIM, 1)
        both = jnp.where(half, key_part, value_part)
        heads_grad[rows, pl.ds(2 * HEAD_DIM, 2 * HEAD_DIM)] = unturn(both, cosine, sine, rows, 1).astype(LOW)
        return 0

    lax.fori_loop(0, length // tile, fold, 0)

    def transpose(i, _):
        rows = pl.ds(pl.multiple_of(i * tile, tile), tile)
        heads_turned[:, rows] = heads_grad[rows].astype(WIDE).T.astype(LOW)
        return 0

    lax.fori_loop(0, length // tile, transpose, 0)

    reduce = RingReduce(size, held, send_r, recv_r)
    small_full[...] = small[...]
    gain_row = small.shape[1] - 8

    def attend(place, slot):
        owner = ring_member(place, size)
        rows = pl.ds(pl.multiple_of(owner * tokens, tokens), tokens)
        part = dot_nt(heads_grad[rows], head_weight[...])
        attend_own[slot] = part.astype(LOW)
        normed = inputs_all[rows].astype(WIDE) * row_scale[rows]
        share = jnp.sum(part * normed, axis=0, keepdims=True)
        lanes = width // 4
        for s0 in range(4):
            small_full[s0, gain_row : gain_row + 1] += share[:, s0 * lanes : (s0 + 1) * lanes]

    place = ring_place(me, size)
    half_ring = size // 2
    attend(place + half_ring, 0)
    reduce.start(0, [attend_own.at[0]] * 2)
    for step in range(1, half_ring):
        attend(place + half_ring - step, 1)
        attend(place - half_ring + step, 2)
        if step == 1:
            def columns(j, _):
                cols = pl.ds(pl.multiple_of(j * tile, tile), tile)
                normed = inputs_all[:, cols].astype(WIDE) * row_scale[...]
                part = dot_nn(heads_turned[...], (normed * gain[gain.shape[0] - 8 : gain.shape[0] - 7, cols]).astype(LOW)).T.astype(LOW)
                depth = head_part.shape[1]
                head_part[pl.ds(j * (tile // depth), tile // depth)] = part.reshape(tile // depth, depth, HEAD_COLS)
                return 0

            lax.fori_loop(0, width // tile, columns, 0)
            late.start()
        reduce.start(step, [attend_own.at[1], attend_own.at[2]])
        pump(3)
    attend(place, 1)
    total_small.start()
    for k in range(size):
        late.first(k)
    pump(len(steps))
    total_small.middle()
    for k in range(1, size):
        late.second(k)
    late.second(0, True)
    reduce.finish(attend_sum, attend_own.at[1], attend_own.at[0])
    for home in early:
        home.close()
    late.close()
    total_small.finish()
    for copy in swaps:
        copy.wait_send()


def swap_halves(values):
    lane = lax.broadcasted_iota(jnp.int32, values.shape, 1) % HEAD_DIM
    return jnp.where(
        lane < HEAD_DIM // 2,
        pltpu.roll(values, values.shape[1] - HEAD_DIM // 2, 1),
        pltpu.roll(values, HEAD_DIM // 2, 1),
    )


def unturn(values, cosine, sine, rows, which):
    cos, sin = cosine[rows], sine[rows]
    if which:
        half = lax.broadcasted_iota(jnp.int32, values.shape, 1) < HEAD_DIM
        cos, sin = jnp.where(half, cos, 1.0), jnp.where(half, sin, 0.0)
    return values * cos - swap_halves(values) * sin


def attention_back(arrays, size, split, collective):
    (mixed_grad, gu_grads, down_grads, mixed_low, project_grad, small, query_pair, key_value, out_pair, log_total,
     docs_row, docs_col, places_row, cosine, sine, gain, inputs_all, row_scale, head_weight) = arrays
    tokens = mixed_grad.shape[0]
    length, width = inputs_all.shape
    tile = 2 * tokens
    out_shape = (4 * size, gu_grads.shape[2], width)
    blocks = [
        (gu_grads.shape[0],) + gu_grads.shape[2:], (down_grads.shape[0],) + down_grads.shape[2:],
        out_shape[1:], (out_shape[1], HEAD_COLS),
    ]
    small_rows = small.shape[1]
    dma = pltpu.SemaphoreType.DMA
    vmem = pl.BlockSpec(memory_space=pltpu.VMEM)
    anywhere = pl.BlockSpec(memory_space=pl.ANY)
    pair = (length, 2 * HEAD_DIM)
    scratch = [
        pltpu.VMEM((size // split, tokens, 2 * HEAD_DIM), LOW),
        pltpu.VMEM((GROUP,) + pair, LOW), pltpu.VMEM((GROUP,) + pair, LOW),
        pltpu.VMEM(pair, WIDE), pltpu.VMEM(pair, WIDE), pltpu.VMEM((tile, 2 * HEAD_DIM), WIDE),
        pltpu.VMEM((length, HEAD_COLS), LOW), pltpu.VMEM((HEAD_COLS, length), LOW),
        pltpu.VMEM(out_shape[:2] + (HEAD_COLS,), LOW),
        pltpu.VMEM(small.shape, WIDE),
        pltpu.VMEM((3, tokens, width), LOW), pltpu.VMEM((2, size // 2, tokens, width), LOW),
        pltpu.VMEM(out_shape, LOW),
        dma((2, size // 2)), dma((2, size // 2)), dma((size // split,)), dma((size // split,)), dma,
    ]
    for block in blocks:
        scratch += Homing.scratch(size, block)
    scratch += SmallSum.scratch(size, small_rows, width)
    return pl.pallas_call(
        functools.partial(back_kernel, size, split, tile),
        out_shape=[jax.ShapeDtypeStruct((tokens, width), WIDE)]
        + [jax.ShapeDtypeStruct((size,) + block, LOW) for block in blocks]
        + [jax.ShapeDtypeStruct((small_rows, width // 4), WIDE)],
        in_specs=[vmem, anywhere, anywhere] + [vmem] * 16,
        out_specs=[vmem] * 6,
        scratch_shapes=scratch,
        compiler_params=pltpu.CompilerParams(
            collective_id=collective, has_side_effects=True, vmem_limit_bytes=62 << 20
        ),
        name="attention_back",
    )(*arrays)


def rms_scale(values):
    return lax.rsqrt(jnp.mean(values * values, axis=-1, keepdims=True) + NORM_EPS)


def rope_tables(places, factor):
    freqs = 1.0 / ROPE_BASE ** (jnp.arange(0, HEAD_DIM, 2).astype(WIDE) / HEAD_DIM)
    angles = (places.astype(WIDE) / factor)[None, :] * freqs[:, None]
    return jnp.cos(angles), jnp.sin(angles)


def dot(equation, left, right):
    return jnp.einsum(equation, left, right, preferred_element_type=WIDE)


def on_device(
    layer_input, document_ids, expert_routes, rope_factor, attention_gain, feedforward_gain,
    query_weight, key_weight, value_weight, output_weight, router_weight, gate_up, down_weight, cotangent,
):
    nseq, nctx = lax.axis_size("seq"), lax.axis_size("ctx")
    tokens, width = layer_input.shape[1:]
    length = tokens * nctx
    rows, experts, ff2 = gate_up.shape
    ff = ff2 // 2
    down_rows = down_weight.shape[0]
    per_unit = max(1, experts // nctx)
    ff_split = max(1, nctx // experts)
    ff_part = ff // ff_split
    head_split = nctx // KV_HEADS
    unit = lax.axis_index("ctx")
    owners = nseq * nctx

    if ff_split == 1:
        gu_pack = gate_up.astype(LOW).transpose(1, 0, 2).reshape(nctx, per_unit, rows, ff2)
    else:
        gu_pack = (
            gate_up.astype(LOW).reshape(rows, experts, 2, ff_split, ff_part).transpose(1, 3, 0, 2, 4)
            .reshape(nctx, per_unit, rows, 2 * ff_part)
        )
    down_pack = jnp.repeat(
        down_weight.astype(LOW).transpose(1, 0, 2), ff_split, axis=0
    ).reshape(nctx, per_unit, down_rows, width)
    head_pack = jnp.concatenate(
        [
            query_weight.reshape(rows, KV_HEADS, GROUP * HEAD_DIM),
            key_weight.reshape(rows, KV_HEADS, HEAD_DIM),
            value_weight.reshape(rows, KV_HEADS, HEAD_DIM),
        ],
        axis=-1,
    ).astype(LOW).transpose(1, 0, 2)
    head_pack = jnp.repeat(head_pack, head_split, axis=0)
    small_rows = experts + 8
    small_pack = jnp.concatenate(
        [router_weight, attention_gain[:, None], feedforward_gain[:, None], jnp.zeros((rows, 110 + 16 - experts), WIDE)],
        axis=1,
    ).astype(LOW)
    small_pack = jnp.broadcast_to(small_pack[None], (nctx,) + small_pack.shape)
    pack = jnp.concatenate([head_pack, small_pack], axis=2)
    documents = jnp.broadcast_to(document_ids.reshape(1, tokens), (8, tokens))
    cos_turned, sin_turned = rope_tables(jnp.arange(length, dtype=jnp.int32), rope_factor[0])

    (inputs_all, upstream_all, mixed_low, query_pair, key_value, out_pair, log_total, docs_row, docs_col, places_row,
     cosine, sine, row_scale, head_full, small_full, gu_full, down_full, out_full) = run_front(
        layer_input[0], cotangent[0], documents, cos_turned, sin_turned, pack, gu_pack, down_pack,
        output_weight.astype(LOW), head_split, owners, small_rows, 1,
    )
    gu_full = gu_full.reshape(per_unit, width, 2 * ff_part)
    down_full = down_full.reshape(per_unit, ff, width)
    if ff_split > 1:
        down_full = lax.dynamic_slice_in_dim(down_full, (unit % ff_split) * ff_part, ff_part, 1)
    out_full = out_full.reshape(HEADS * HEAD_DIM, width)
    router_full = small_full[:experts].astype(LOW)
    gain_one, gain_two = small_full[experts], small_full[experts + 1]

    inputs = layer_input[0].astype(WIDE)
    middle = inputs + dot("tj,jd->td", mixed_low, out_full)
    scale_two = rms_scale(middle)
    normed_two = middle * scale_two
    expert_input = (normed_two * gain_two).astype(LOW)
    logits = dot("td,ed->te", expert_input, router_full)
    chosen = jnp.any(
        expert_routes[0][:, :, None] == jnp.arange(experts, dtype=jnp.int32)[None, None, :], axis=1
    )
    picked = jnp.where(chosen, logits, NEG_BIG)
    expo_gate = jnp.where(chosen, jnp.exp(picked - jnp.max(picked, axis=-1, keepdims=True)), 0.0)
    combine = expo_gate / jnp.sum(expo_gate, axis=-1, keepdims=True)

    mix, back_sum, gate_grad_all, gu_grads, down_grads = run_experts(
        expert_input, combine.T, upstream_all, gu_full, down_full, nctx, ff_split, owners, down_rows, 3
    )

    layer_output = (middle + mix).astype(LOW)[None]
    upstream = cotangent[0].astype(WIDE)
    gate_grad = gate_grad_all[:, :per_unit].reshape(experts, ff_split, tokens).sum(axis=1).T
    gate_grad = jnp.where(chosen, gate_grad, 0.0)
    select_grad = combine * (gate_grad - jnp.sum(combine * gate_grad, axis=-1, keepdims=True))
    logit_grad = select_grad.astype(LOW)
    back_two = back_sum + dot("te,ed->td", logit_grad, router_full)
    router_part = dot("te,td->ed", logit_grad, expert_input)
    gain_two_part = jnp.sum(back_two * normed_two, axis=0)
    normed_two_grad = back_two * gain_two
    middle_grad = upstream + scale_two * (
        normed_two_grad - normed_two * jnp.mean(normed_two_grad * normed_two, axis=-1, keepdims=True)
    )
    project_grad = middle_grad.astype(LOW)
    mixed_grad = dot("td,jd->tj", project_grad, out_full).astype(LOW)

    small_grads = jnp.concatenate(
        [router_part, gain_two_part[None], jnp.zeros((31 - experts, width), WIDE)], axis=0
    ).reshape(32, nseq, width // nseq).transpose(1, 0, 2)
    if ff_split > 1:
        down_grads = lax.dynamic_update_slice_in_dim(
            jnp.zeros((per_unit, owners, down_rows, width), LOW), down_grads,
            (unit % ff_split) * (ff_part // down_rows), 1,
        )
    attend_sum, gu_home, down_home, out_home, head_home, small_home = attention_back(
        [
            mixed_grad,
            gu_grads,
            down_grads,
            mixed_low, project_grad,
            small_grads,
            query_pair, key_value, out_pair, log_total, docs_row, docs_col, places_row,
            cosine, sine, small_full, inputs_all.reshape(length, width), row_scale, head_full,
        ],
        nctx, head_split, 7,
    )
    out_home, head_home = out_home.astype(WIDE), head_home.astype(WIDE)
    if ff_split == 1:
        gate_up_gradient = lax.optimization_barrier(gu_home.reshape(experts, rows, ff2).transpose(1, 0, 2)).astype(WIDE)
        down_gradient = lax.optimization_barrier(
            down_home.reshape(experts, down_rows, width).transpose(1, 0, 2)
        ).astype(WIDE)
    else:
        gate_up_gradient = (
            gu_home.astype(WIDE).reshape(experts, ff_split, rows, 2, ff_part).transpose(2, 0, 3, 1, 4)
            .reshape(rows, experts, ff2)
        )
        down_gradient = down_home.astype(WIDE).reshape(experts, ff_split, down_rows, width).sum(axis=1).transpose(1, 0, 2)
    output_gradient = out_home.sum(axis=0)
    head_home = head_home.reshape(KV_HEADS, head_split, rows, HEAD_COLS).sum(axis=1).transpose(1, 0, 2)
    query_gradient = head_home[..., : GROUP * HEAD_DIM].reshape(rows, HEADS * HEAD_DIM)
    key_gradient = head_home[..., GROUP * HEAD_DIM : -HEAD_DIM].reshape(rows, KV_HEADS * HEAD_DIM)
    value_gradient = head_home[..., -HEAD_DIM:].reshape(rows, KV_HEADS * HEAD_DIM)
    small_home = lax.dynamic_slice_in_dim(small_home, unit * rows, rows, axis=1)
    router_gradient = small_home[:experts].T

    scale_one = rms_scale(inputs)
    normed_one = inputs * scale_one
    normed_one_grad = attend_sum * gain_one
    input_gradient = (
        middle_grad
        + scale_one
        * (normed_one_grad - normed_one * jnp.mean(normed_one_grad * normed_one, axis=-1, keepdims=True))
    ).astype(LOW)[None]
    return (
        layer_output, input_gradient, small_home[24], small_home[experts],
        query_gradient, key_gradient, value_gradient, output_gradient, router_gradient,
        gate_up_gradient, down_gradient,
    )


def solution(mesh):
    both = ("seq", "ctx")
    return jax.shard_map(
        on_device,
        mesh=mesh,
        in_specs=(
            P("seq", "ctx", None), P("seq", "ctx"), P("seq", "ctx", None), P(), P(both), P(both),
            P(both, None), P(both, None), P(both, None), P(both, None), P(both, None),
            P(both, None, None), P(both, None, None), P("seq", "ctx", None),
        ),
        out_specs=(
            P("seq", "ctx", None), P("seq", "ctx", None), P(both), P(both),
            P(both, None), P(both, None), P(both, None), P(both, None), P(both, None),
            P(both, None, None), P(both, None, None),
        ),
        check_vma=False,
    )
```
